32 devices in a mesh: groups: 2 (over x), gx: 4 (over y, core), gy: 4 (over z).
Axes of the slice: x: 2, y: 2, z: 4, core: 2. Of those that a mesh axis runs over, the one named last changes fastest.
Arguments:
- stay_feats: bfloat16 [16, 4, 4, 12288], P(None, 'gx', 'gy', 'groups'), parts along dimension 3, may hold values from -6 to 6
- stay_slots: int32 [4, 4, 12288], P('gx', 'gy', 'groups'), parts along dimension 2, may hold values from 0 to 32767, as said below
- move_feats: bfloat16 [16, 4, 4, 8, 1024], P(None, 'gx', 'gy', None, 'groups'), parts along dimension 4, may hold values from -6 to 6
- move_slots: int32 [4, 4, 8, 1024], P('gx', 'gy', None, 'groups'), parts along dimension 3, may hold values from 0 to 32767, as said below
- move_counts: int32 [4, 4, 16], P('gx', 'gy', 'groups'), parts along dimension 2, may hold values from 85 to 512
- encoder: bfloat16 [32, 16], replicated, may hold values from -1.5 to 1.5
- conv_weights: bfloat16 [3, 32, 864], replicated, may hold values from -0.21875 to 0.21875
- conv_biases: float32 [3, 32], replicated, may hold values from -3 to 3
- decoder: bfloat16 [3, 32], replicated, may hold values from -1 to 1
- self_weight: bfloat16 [3, 16], replicated, may hold values from -1.5 to 1.5
Outputs:
- velocity: float32 [3, 4, 4, 20480], P(None, 'gx', 'gy', 'groups'), parts along dimension 3
The draws below stay inside these ranges and needn't reach their ends.
There are 2 independent parts, one for each index of `groups`. The reference program is written for one: setup_inputs(seed, part) draws one part's arguments, and reference() takes and returns one part's arrays. A program takes and returns all parts, laid end to end along the dimension named above; an argument that names none is the same for every part. Nothing has to cross between parts.
Inputs may be any that keep to these rules, and one draw needn't show every extreme that they name: `stay_slots`: A slot s of a device belongs to its local cell s mod 8192. On each device the slots of its staying rows and of all rows sent to it by its eight neighbours are distinct. `move_slots`: slots at the destination device, distinct there together with its staying rows.
All inputs are finite; a program needn't handle non-finite values.
Results may differ from the reference program's by a relative error of at most 0.0055.
Values may be sent and summed in bfloat16 or wider, within the bound.
No kernel may reach another device: no remote copies, remote signals or barrier semaphores. Data moves between devices by JAX's collectives and lax.ppermute only.
A program may use at most 64 MiB of HBM per device.

```python
import jax
import jax.numpy as jnp
from jax import lax

C = 32
F = 16
Z = 8
SLOT_CELL = 4
CX = 8
CY = 128
DEVX = 4
DEVY = 4
NX = 32
NY = 512
SLOTS = 32768
STAY = 6144
CAP = 512


OFFSETS = ((-1, -1), (-1, 0), (-1, 1), (0, -1), (0, 1), (1, -1), (1, 0), (1, 1))


def slot_tables(key):
    base_key = jax.random.fold_in(key, 5)
    device_keys = jax.random.split(base_key, DEVX * DEVY)
    taken = STAY + 8 * CAP

    def one_device(device_key, device_number):
        order = jax.random.permutation(device_key, SLOTS)[:taken].astype(jnp.int32)
        anchor = jnp.where(device_number % 2 == 0, order[0], order[STAY])
        return (order + (SLOTS - 1) - anchor) % SLOTS
    tables = jax.vmap(one_device)(device_keys, jnp.arange(DEVX * DEVY, dtype=jnp.int32))
    tables = tables.reshape(DEVX, DEVY, taken)
    staying = tables[:, :, :STAY]
    incoming = tables[:, :, STAY:].reshape(DEVX, DEVY, 8, CAP)
    outgoing = []
    for bucket, (shift_x, shift_y) in enumerate(OFFSETS):
        outgoing.append(jnp.roll(incoming[:, :, bucket], (-shift_x, -shift_y), axis=(0, 1)))
    return (staying.astype(jnp.int32), jnp.stack(outgoing, 2).astype(jnp.int32))


def draw_stay_slots(key, part):
    return slot_tables(key)[0]


def draw_move_slots(key, part):
    return slot_tables(key)[1]


def draw_move_counts(key, part):
    load_key, base_key, pick_key = jax.random.split(jax.random.fold_in(key, 11), 3)
    load = jax.random.randint(load_key, (DEVX, DEVY, 1), 2, 6)
    base = jax.random.randint(base_key, (DEVX, DEVY, 8), CAP // 4, CAP // 2 + 1)
    counts = jnp.minimum(CAP, base * load // 3).reshape(-1)
    total = DEVX * DEVY * 8
    chosen = jax.random.randint(pick_key, (), 0, total)
    counts = counts.at[chosen].set(CAP)
    counts = counts.at[(chosen + 1) % total].set(CAP // 4 * 2 // 3)
    return counts.reshape(DEVX, DEVY, 8).astype(jnp.int32)


def levels(rng, extent, cuts, low, top_value):
    level, own = 1.0, jax.random.fold_in(rng, 6)
    for position, parts in cuts:
        heights = jnp.exp(jax.random.uniform(jax.random.fold_in(own, position), (parts,), jnp.float32, low / len(cuts), top_value / len(cuts)))
        level = level * jnp.repeat(heights, extent[position] // parts).reshape([-1 if axis == position else 1 for axis in range(len(extent))])
    return level


def noise(rng, dims, deviation, bound, shards=(), kind=jnp.bfloat16):
    factor_of = levels(rng, dims, shards, -0.22, 0.18) if shards else 1.0
    values = jax.random.normal(rng, dims, jnp.float32) * deviation * factor_of
    return jnp.minimum(jnp.maximum(values, -bound), bound).astype(kind)


def setup_inputs(seed: int = 0, part: int = 0) -> dict:
    key_list = jax.random.split(jax.random.key(seed), 11)
    part_keys = jax.random.split(jax.random.fold_in(key_list[10], part), 11)
    stay_feats = noise(part_keys[0], (F, DEVX, DEVY, STAY), 1.0, 6.0, ((1, 4), (2, 4)))
    stay_slots = draw_stay_slots(jax.random.fold_in(jax.random.fold_in(key_list[10], part), 71), part)
    move_feats = noise(part_keys[2], (F, DEVX, DEVY, 8, CAP), 1.0, 6.0, ((1, 4), (2, 4)))
    move_slots = draw_move_slots(jax.random.fold_in(jax.random.fold_in(key_list[10], part), 71), part)
    move_counts = draw_move_counts(jax.random.fold_in(jax.random.fold_in(key_list[10], part), 71), part)
    encoder = noise(key_list[5], (C, F), F ** -0.5, 1.5)
    conv_weights = noise(key_list[6], (3, C, 27 * C), (27 * C) ** -0.5, 0.21875)
    conv_biases = noise(key_list[7], (3, C), 0.5, 3.0, (), jnp.float32)
    decoder = noise(key_list[8], (3, C), C ** -0.5, 1.0)
    self_weight = noise(key_list[9], (3, F), F ** -0.5, 1.5)
    return {"stay_feats": stay_feats, "stay_slots": stay_slots, "move_feats": move_feats, "move_slots": move_slots, "move_counts": move_counts, "encoder": encoder, "conv_weights": conv_weights, "conv_biases": conv_biases, "decoder": decoder, "self_weight": self_weight}


OFFSETS = ((-1, -1), (-1, 0), (-1, 1), (0, -1), (0, 1), (1, -1), (1, 0), (1, 1))


def local_means(feature_rows, slot_rows):
    cell_total = Z * CX * CY
    slot_total = SLOT_CELL * cell_total
    feat_dim = feature_rows.shape[0]
    placed = jnp.zeros((feat_dim, slot_total), feature_rows.dtype).at[:, slot_rows].set(feature_rows, mode="drop")
    filled = jnp.zeros((slot_total,), jnp.float32).at[slot_rows].set(1.0, mode="drop")
    summed = jnp.sum(placed.reshape(feat_dim, SLOT_CELL, cell_total).astype(jnp.float32), axis=1)
    occupied = jnp.sum(filled.reshape(SLOT_CELL, cell_total), axis=0)
    return (summed / jnp.maximum(occupied, 1.0)).astype(jnp.bfloat16)


def convolve(volume, weight):
    channels = volume.shape[0]
    padded = jnp.pad(volume, ((0, 0), (1, 1), (0, 0), (0, 0)))
    padded = jnp.pad(padded, ((0, 0), (0, 0), (1, 1), (1, 1)), mode="wrap")
    summed = jnp.zeros(volume.shape, jnp.float32)
    for depth_off in range(3):
        for x_off in range(3):
            for y_off in range(3):
                tap_index = (depth_off * 3 + x_off) * 3 + y_off
                tap_weight = weight[:, tap_index * channels:(tap_index + 1) * channels].astype(jnp.float32)
                shifted = padded[:, depth_off:depth_off + Z, x_off:x_off + NX, y_off:y_off + NY].astype(jnp.float32)
                summed = summed + jnp.einsum("oc,czxy->ozxy", tap_weight, shifted, precision=lax.Precision.HIGHEST)
    return summed


def reference(stay_feats, stay_slots, move_feats, move_slots, move_counts, encoder, conv_weights, conv_biases, decoder, self_weight):
    cell_total = Z * CX * CY
    slot_total = SLOT_CELL * cell_total
    live_rows = jnp.arange(CAP, dtype=jnp.int32)[None, None, None, :] < move_counts[..., None]
    sent_slots = jnp.where(live_rows, move_slots, jnp.int32(slot_total)).astype(jnp.int32)
    feat_parts = [stay_feats]
    slot_parts = [stay_slots]
    for bucket, (shift_x, shift_y) in enumerate(OFFSETS):
        feat_parts.append(jnp.roll(move_feats[:, :, :, bucket], (shift_x, shift_y), axis=(1, 2)))
        slot_parts.append(jnp.roll(sent_slots[:, :, bucket], (shift_x, shift_y), axis=(0, 1)))
    held_feats = jnp.concatenate(feat_parts, 3)
    held_slots = jnp.concatenate(slot_parts, 2).astype(jnp.int32)
    device_feats = held_feats.transpose(1, 2, 0, 3)
    cell_mean = jax.vmap(jax.vmap(local_means))(device_feats, held_slots)
    cell_mean = cell_mean.reshape(DEVX, DEVY, F, Z, CX, CY).transpose(2, 3, 0, 4, 1, 5).reshape(F, Z, NX, NY)
    grid_in = jnp.einsum("cf,fzxy->czxy", encoder.astype(jnp.float32), cell_mean.astype(jnp.float32), precision=lax.Precision.HIGHEST).astype(jnp.bfloat16)
    hidden_one = jax.nn.gelu(convolve(grid_in, conv_weights[0]) + conv_biases[0][:, None, None, None]).astype(jnp.bfloat16)
    hidden_two = jax.nn.gelu(convolve(hidden_one, conv_weights[1]) + conv_biases[1][:, None, None, None]).astype(jnp.bfloat16)
    grid_out = (convolve(hidden_two, conv_weights[2]) + conv_biases[2][:, None, None, None] + grid_in.astype(jnp.float32)).astype(jnp.bfloat16)
    blocks = grid_out.reshape(C, Z, DEVX, CX, DEVY, CY).transpose(2, 4, 0, 1, 3, 5).reshape(DEVX, DEVY, C, cell_total)

    def decode(block, feature_rows, slot_rows):
        picked = jnp.take(block, slot_rows % cell_total, axis=1)
        moving = jnp.dot(decoder, picked, preferred_element_type=jnp.float32)
        moving = moving + jnp.dot(self_weight, feature_rows, preferred_element_type=jnp.float32)
        return jnp.where(slot_rows[None, :] < slot_total, moving, jnp.zeros_like(moving))

    result = jax.vmap(jax.vmap(decode))(blocks, device_feats, held_slots)
    return result.transpose(2, 0, 1, 3)
```

```python
import functools

import jax
import jax.numpy as jnp
from jax import lax
from jax.experimental import pallas as pl
from jax.experimental.pallas import tpu as pltpu
from jax.sharding import PartitionSpec as P

Z = 8
CX = 8
CY = 128
CELLS = Z * CX * CY
LO = 2 * CY
HI = CELLS // LO
DEAD = 2 * HI
HALO = 3
SIDE = 8
PITCH = CY + 2 * SIDE
BF = jnp.bfloat16
F32 = jnp.float32
NT = (((1,), (1,)), ((), ()))
NN = (((1,), (0,)), ((), ()))


def cell_codes(slots):
    cell = slots & (CELLS - 1)
    low = cell & (LO - 1)
    zx = cell // LO
    return (zx & (CX // 2 - 1)) * Z + zx // (CX // 2), low


def passed_along(x, axis, by):
    length = lax.axis_size(axis)
    return lax.ppermute(x, axis, [(i, (i + by) % length) for i in range(length)])


def dot(a, b, dims=NN):
    return lax.dot_general(a, b, dims, preferred_element_type=F32)


def vmem():
    return pl.BlockSpec(memory_space=pltpu.VMEM)


def call(kernel, name, outs, scratch, cost, count):
    single = not isinstance(outs, (list, tuple))
    return pl.pallas_call(
        kernel,
        name=name,
        out_shape=outs,
        in_specs=[vmem()] * count,
        out_specs=vmem() if single else [vmem()] * len(outs),
        scratch_shapes=scratch,
        cost_estimate=pl.CostEstimate(flops=cost, bytes_accessed=4 << 20, transcendentals=0),
        compiler_params=pltpu.CompilerParams(vmem_limit_bytes=48 << 20),
    )


def onehot(code, count):
    rows = lax.broadcasted_iota(jnp.int32, (count, code.shape[1]), 0).astype(F32).astype(BF)
    same = rows == jnp.broadcast_to(code, rows.shape)
    return jnp.where(same, jnp.ones_like(rows), jnp.zeros_like(rows))


def scatter_part(feats, high, low):
    spread = jnp.broadcast_to(high, feats.shape)
    zero = jnp.zeros_like(feats)
    parts = [jnp.where(spread == jnp.asarray(h, BF), feats, zero) for h in range(HI)]
    parts.append(onehot(high, HI))
    return dot(jnp.concatenate(parts, 0), onehot(low, LO), NT)


def stay_kernel(feat_ref, slot_ref, sum_ref):
    chunk = 1024
    sum_ref[...] = jnp.zeros_like(sum_ref)

    def body(step, carry):
        at = pl.ds(pl.multiple_of(step * chunk, chunk), chunk)
        high, low = cell_codes(slot_ref[:, at])
        sum_ref[...] += scatter_part(
            feat_ref[:, at], high.astype(F32).astype(BF), low.astype(F32).astype(BF)
        )
        return carry

    lax.fori_loop(0, feat_ref.shape[1] // chunk, body, 0)


def band_kernel(weight_ref, encoder_ref, band_ref, spread_ref, padded):
    layers, chans, width = weight_ref.shape
    taps = 9
    lane = lax.broadcasted_iota(jnp.int32, (chans, 128), 1) // chans
    per = 128 // chans
    padded[:, :, width:] = jnp.zeros((layers, chans, padded.shape[2] - width), F32)
    padded[:, :, :width] = weight_ref[...].astype(F32)

    def one(layer, carry):
        turned = []
        for block in range(padded.shape[2] // 128):
            source = padded[layer, :, block * 128 : (block + 1) * 128]
            turned.append(
                [source if k == 0 else pltpu.roll(source, k * chans, 1) for k in range(per)]
            )
        for out_z in range(Z):
            for tap in range(taps):
                for part in range(Z // per):
                    tile = jnp.zeros((chans, 128), F32)
                    for depth in range(3):
                        in_z = out_z + depth - 1
                        if in_z < 0 or in_z >= Z or in_z // per != part:
                            continue
                        index = depth * taps + tap
                        moved = turned[index // per][(in_z - index) % per]
                        tile = jnp.where(lane == in_z % per, moved, tile)
                    lanes = tap * Z * chans + part * 128
                    band_ref[
                        layer, out_z * chans : (out_z + 1) * chans, lanes : lanes + 128
                    ] = tile.astype(BF)
        return carry

    lax.fori_loop(0, layers, one, 0)
    feat_dim = encoder_ref.shape[1]
    wide = Z * feat_dim
    pick = lax.broadcasted_iota(jnp.int32, (feat_dim, wide), 0)
    column = lax.broadcasted_iota(jnp.int32, (feat_dim, wide), 1) % feat_dim
    tiled = dot(encoder_ref[...], jnp.where(pick == column, 1.0, 0.0).astype(BF))
    group = lax.broadcasted_iota(jnp.int32, (chans, wide), 1) // feat_dim
    for layer in range(Z):
        spread_ref[layer * chans : (layer + 1) * chans, :] = jnp.where(
            group == layer, tiled, 0.0
        ).astype(BF)


def mean_kernel(
    west_ref, east_ref, down_ref, up_ref, part_ref, mean_ref, first_ref, last_ref, held_ref, total
):
    cap = west_ref.shape[1] // 3
    order = [
        (down_ref, 0),
        (west_ref, 1),
        (up_ref, 0),
        (down_ref, 1),
        (up_ref, 1),
        (down_ref, 2),
        (east_ref, 1),
        (up_ref, 2),
    ]
    for place, (ref, which) in enumerate(order):
        held_ref[:, place * cap : (place + 1) * cap] = ref[:, which * cap : (which + 1) * cap]
    total[...] = part_ref[...]
    chunk = 1024
    feat_dim = held_ref.shape[0] - 2

    def body(step, carry):
        at = pl.ds(pl.multiple_of(step * chunk, chunk), chunk)
        rows = held_ref[:, at]
        total[...] += scatter_part(
            rows[:feat_dim], rows[feat_dim : feat_dim + 1], rows[feat_dim + 1 : feat_dim + 2]
        )
        return carry

    lax.fori_loop(0, held_ref.shape[1] // chunk, body, 0)
    inverse = 1.0 / jnp.maximum(total[HI * feat_dim :, :], 1.0)
    for pair in range(CX // 2):
        blocks = []
        for layer in range(Z):
            code = pair * Z + layer
            blocks.append(
                total[code * feat_dim : (code + 1) * feat_dim, :] * inverse[code : code + 1, :]
            )
        block = jnp.concatenate(blocks, 0)
        for odd in range(2):
            x = pair * 2 + odd
            turned = jnp.transpose(block[:, odd * CY : (odd + 1) * CY]).astype(BF)
            mean_ref[x * CY : (x + 1) * CY, :] = turned
            if x < HALO:
                first_ref[x * CY : (x + 1) * CY, :] = turned
            if x >= CX - HALO:
                at = x - (CX - HALO)
                last_ref[at * CY : (at + 1) * CY, :] = turned


def gelu(v):
    inner = 0.7978845608028654 * (v + 0.044715 * (v * v * v))
    return 0.5 * v * (1.0 + jnp.tanh(inner))


def grid_kernel(
    mean_ref,
    before_ref,
    after_ref,
    below_ref,
    above_ref,
    band_ref,
    spread_ref,
    bias_ref,
    decoder_ref,
    grid_ref,
    left,
    right,
    input_one,
    input_two,
    input_three,
    own,
):
    spread = spread_ref[...]
    left[...] = dot(below_ref[...], spread, NT).astype(BF).astype(F32)
    right[...] = dot(above_ref[...], spread, NT).astype(BF).astype(F32)

    def store_shifted(target, x, block, lead, length):
        rows = pl.ds(pl.multiple_of(x * length, length), length)
        for s, by in enumerate((1, 0, block.shape[0] - 1)):
            moved = pltpu.roll(block, by, 0) if by else block
            target[s, rows, :] = moved[lead : lead + length].astype(BF)

    def encode(ref, count, base, keep):
        def body(x, carry):
            rows = pl.ds(pl.multiple_of(x * CY, CY), CY)
            inside = dot(ref[rows, :], spread, NT).astype(BF)
            if keep:
                own[rows, :] = inside
            at = x + base
            side = pl.ds(pl.multiple_of(at * SIDE, SIDE), SIDE)
            block = jnp.concatenate([left[side, :], inside.astype(F32), right[side, :]], 0)
            store_shifted(input_one, at, block, 0, PITCH)
            return carry

        lax.fori_loop(0, count, body, 0)

    encode(before_ref, HALO, 0, False)
    encode(mean_ref, CX, HALO, True)
    encode(after_ref, HALO, HALO + CX, False)

    def conv(source, layer, x, count, length):
        pieces = []
        for q in range(3):
            rows = pl.ds(pl.multiple_of((x + q) * length, length), count * length)
            for s in range(3):
                pieces.append(source[s, rows, :])
        return dot(jnp.concatenate(pieces, 1), band_ref[layer], NT) + bias_ref[layer : layer + 1, :]

    def hidden(source, layer, target, outs, count, lead, length):
        def body(step, carry):
            x = step * count
            value = gelu(conv(source, layer, x, count, PITCH)).astype(BF).astype(F32)
            for k in range(count):
                store_shifted(
                    target, x + k, value[k * PITCH : (k + 1) * PITCH], lead, length
                )
            return carry

        lax.fori_loop(0, outs // count, body, 0)

    hidden(input_one, 0, input_two, CX + 4, 2, 0, PITCH)
    hidden(input_two, 1, input_three, CX + 2, 2, SIDE, CY)

    chans = decoder_ref.shape[1]
    wide = Z * chans
    pick = lax.broadcasted_iota(jnp.int32, (chans, wide), 0)
    column = lax.broadcasted_iota(jnp.int32, (chans, wide), 1) % chans
    tiled = dot(decoder_ref[...], jnp.where(pick == column, 1.0, 0.0).astype(BF))
    group = lax.broadcasted_iota(jnp.int32, (Z, wide), 1) // chans
    level = lax.broadcasted_iota(jnp.int32, (Z, wide), 0)
    decode = jnp.concatenate(
        [jnp.where(group == level, tiled[k : k + 1, :], 0.0) for k in range(3)], 0
    ).astype(BF)

    def last(step, carry):
        rows = pl.ds(pl.multiple_of(step * LO, LO), LO)
        value = conv(input_three, 2, step * 2, 2, CY) + own[rows, :].astype(F32)
        flow = dot(decode, value.astype(BF), NT)
        top = flow.astype(BF)
        grid_ref[0, step] = top
        grid_ref[1, step] = (flow - top.astype(F32)).astype(BF)
        return carry

    lax.fori_loop(0, CX // 2, last, 0)


def pick_rows(table, feats, high, low, self_weight):
    count = feats.shape[1]
    both = dot(table, onehot(low, LO))
    half = both.shape[0] // 2
    values = both[:half] + both[half:]
    level = lax.broadcasted_iota(jnp.int32, (Z, count), 0).astype(F32)
    spread = jnp.broadcast_to(high, (Z, count))
    masks = [spread == (level + float(pair * Z)) for pair in range(CX // 2)]
    live = high < float(DEAD)
    wide = feats.astype(F32)
    rows = []
    for k in range(3):
        total = jnp.zeros((Z, count), F32)
        for pair in range(CX // 2):
            at = (pair * 3 + k) * Z
            total = total + jnp.where(masks[pair], values[at : at + Z], 0.0)
        for part in range(feats.shape[0] // Z):
            part_rows = slice(part * Z, (part + 1) * Z)
            total = total + wide[part_rows] * self_weight[part_rows, k : k + 1]
        rows.append(jnp.where(live, jnp.sum(total, 0, keepdims=True), 0.0))
    return rows


def pick_kernel(grid_ref, feat_ref, slot_ref, held_ref, self_ref, out_ref, table):
    table[...] = grid_ref[...].reshape(table.shape)
    chunk = 1024
    feat_dim, stay = feat_ref.shape
    eye = jnp.where(
        lax.broadcasted_iota(jnp.int32, (feat_dim, feat_dim), 0)
        == lax.broadcasted_iota(jnp.int32, (feat_dim, feat_dim), 1),
        1.0,
        0.0,
    ).astype(BF)
    weight = dot(eye, self_ref[...], NT)

    def staying(step, carry):
        at = pl.ds(pl.multiple_of(step * chunk, chunk), chunk)
        high, low = cell_codes(slot_ref[:, at])
        rows = pick_rows(
            table[...], feat_ref[:, at], high.astype(F32), low.astype(F32).astype(BF), weight
        )
        for k in range(3):
            out_ref[k : k + 1, at] = rows[k]
        return carry

    lax.fori_loop(0, stay // chunk, staying, 0)

    def arrived(step, carry):
        at = pl.ds(pl.multiple_of(step * chunk, chunk), chunk)
        block = held_ref[:, at]
        rows = pick_rows(
            table[...],
            block[:feat_dim],
            block[feat_dim : feat_dim + 1].astype(F32),
            block[feat_dim + 1 : feat_dim + 2],
            weight,
        )
        to = pl.ds(pl.multiple_of(stay + step * chunk, chunk), chunk)
        for k in range(3):
            out_ref[k : k + 1, to] = rows[k]
        return carry

    lax.fori_loop(0, held_ref.shape[1] // chunk, arrived, 0)


def on_device(
    stay_feats,
    stay_slots,
    move_feats,
    move_slots,
    move_counts,
    encoder,
    conv_weights,
    conv_biases,
    decoder,
    self_weight,
):
    feat_dim = stay_feats.shape[0]
    stay = stay_feats.shape[3]
    cap = move_feats.shape[4]
    chans = encoder.shape[0]
    own_feats = stay_feats.reshape(feat_dim, stay)
    own_slots = stay_slots.reshape(1, stay)

    live = jnp.arange(cap, dtype=jnp.int32)[None, :] < move_counts.reshape(8)[:, None]
    high, low = cell_codes(move_slots.reshape(8, cap))
    high = jnp.where(live, high, DEAD)
    codes = jnp.stack([high, low], 0).astype(BF)
    sent = jnp.concatenate([move_feats.reshape(feat_dim, 8, cap), codes], 0)
    sent = sent.reshape(feat_dim + 2, 8 * cap)
    width = feat_dim + 2
    west = passed_along(sent[:, : 3 * cap], "gx", -1)
    east = passed_along(sent[:, 5 * cap :], "gx", 1)
    down = passed_along(
        jnp.concatenate([west[:, :cap], sent[:, 3 * cap : 4 * cap], east[:, :cap]], 1), "gy", -1
    )
    up = passed_along(
        jnp.concatenate(
            [west[:, 2 * cap :], sent[:, 4 * cap : 5 * cap], east[:, 2 * cap :]], 1
        ),
        "gy",
        1,
    )
    sums = jax.ShapeDtypeStruct((HI * (feat_dim + 1), LO), F32)
    part = call(stay_kernel, "stay", sums, [], 5 << 30, 2)(own_feats, own_slots)
    band, spread = call(
        band_kernel,
        "band",
        [
            jax.ShapeDtypeStruct((3, Z * chans, 9 * Z * chans), BF),
            jax.ShapeDtypeStruct((Z * chans, Z * feat_dim), BF),
        ],
        [pltpu.VMEM((3, chans, 7 * 128), F32)],
        2 << 30,
        2,
    )(conv_weights, encoder)
    lanes = Z * feat_dim
    mean, first, last, held = call(
        mean_kernel,
        "mean",
        [
            jax.ShapeDtypeStruct((CX * CY, lanes), BF),
            jax.ShapeDtypeStruct((HALO * CY, lanes), BF),
            jax.ShapeDtypeStruct((HALO * CY, lanes), BF),
            jax.ShapeDtypeStruct((width, 8 * cap), BF),
        ],
        [pltpu.VMEM(sums.shape, F32)],
        3 << 30,
        5,
    )(west, east, down, up, part)
    after = passed_along(first, "gx", -1)
    before = passed_along(last, "gx", 1)

    def edge(start):
        blocks = [
            value.reshape(-1, CY, lanes)[:, start : start + SIDE] for value in (before, mean, after)
        ]
        return jnp.concatenate(blocks, 0).reshape((CX + 2 * HALO) * SIDE, lanes)

    above = passed_along(edge(0), "gy", -1)
    below = passed_along(edge(CY - SIDE), "gy", 1)
    biases = jnp.tile(conv_biases, (1, Z))
    wide = Z * chans
    rows = CX + 2 * HALO
    grid = call(
        grid_kernel,
        "grid",
        jax.ShapeDtypeStruct((2, CX // 2, 3 * Z, LO), BF),
        [
            pltpu.VMEM((rows * SIDE, wide), F32),
            pltpu.VMEM((rows * SIDE, wide), F32),
            pltpu.VMEM((3, rows * PITCH, wide), BF),
            pltpu.VMEM((3, (rows - 2) * PITCH, wide), BF),
            pltpu.VMEM((3, (rows - 4) * CY, wide), BF),
            pltpu.VMEM((CX * CY, wide), BF),
        ],
        8 << 30,
        9,
    )(mean, before, after, below, above, band, spread, biases, decoder)
    out = call(
        pick_kernel,
        "pick",
        jax.ShapeDtypeStruct((3, stay + 8 * cap), F32),
        [pltpu.VMEM((CX * 3 * Z, LO), BF)],
        5 << 30,
        5,
    )(grid, own_feats, own_slots, held, self_weight)
    return out.reshape(3, 1, 1, stay + 8 * cap)


def solution(mesh):
    placed = (
        P(None, "gx", "gy", "groups"),
        P("gx", "gy", "groups"),
        P(None, "gx", "gy", None, "groups"),
        P("gx", "gy", None, "groups"),
        P("gx", "gy", "groups"),
        P(),
        P(),
        P(),
        P(),
        P(),
    )
    return jax.shard_map(
        on_device,
        mesh=mesh,
        in_specs=placed,
        out_specs=P(None, "gx", "gy", "groups"),
        check_vma=False,
    )
```

```python
import functools

import jax
import jax.numpy as jnp
from jax import lax
from jax.experimental import pallas as pl
from jax.experimental.pallas import tpu as pltpu
from jax.sharding import PartitionSpec as P

Z = 8
CX = 8
CY = 128
CELLS = Z * CX * CY
LO = 2 * CY
HI = CELLS // LO
DEAD = 2 * HI
HALO = 3
SIDE = 8
PITCH = CY + 2 * SIDE
BF = jnp.bfloat16
F32 = jnp.float32
NT = (((1,), (1,)), ((), ()))
NN = (((1,), (0,)), ((), ()))


CHUNK = 1024
COUNTS = (4, 5, 4)


def repeat(count, body):
    for step in range(count):
        body(step)


def aligned(start, length):
    return slice(start, start + length)


def cell_codes(slots):
    cell = slots & (CELLS - 1)
    low = cell & (LO - 1)
    zx = cell // LO
    return (zx & (CX // 2 - 1)) * Z + zx // (CX // 2), low


def passed_along(x, axis, by):
    length = lax.axis_size(axis)
    return lax.ppermute(x, axis, [(i, (i + by) % length) for i in range(length)])


def dot(a, b, dims=NN):
    return lax.dot_general(a, b, dims, preferred_element_type=F32)


def vmem():
    return pl.BlockSpec(memory_space=pltpu.VMEM)


def smem():
    return pl.BlockSpec(memory_space=pltpu.SMEM)


def call(kernel, name, ins, outs, scratch, flops, mib):
    return pl.pallas_call(
        kernel,
        name=name,
        out_shape=[jax.ShapeDtypeStruct(*shape) for shape, _ in outs],
        in_specs=ins,
        out_specs=[spec for _, spec in outs],
        scratch_shapes=scratch,
        cost_estimate=pl.CostEstimate(flops=flops, bytes_accessed=1 << 20, transcendentals=0),
        compiler_params=pltpu.CompilerParams(vmem_limit_bytes=mib << 20),
    )


def onehot(code, count):
    rows = lax.broadcasted_iota(jnp.int32, (count, code.shape[1]), 0).astype(F32).astype(BF)
    same = rows == jnp.broadcast_to(code, rows.shape)
    return jnp.where(same, jnp.ones_like(rows), jnp.zeros_like(rows))


def scatter_part(feats, high, low):
    spread = jnp.broadcast_to(high, feats.shape)
    zero = jnp.zeros_like(feats)
    parts = [jnp.where(spread == jnp.asarray(h, BF), feats, zero) for h in range(HI)]
    parts.append(onehot(high, HI))
    return dot(jnp.concatenate(parts, 0), onehot(low, LO), NT)


def pack_kernel(feat_ref, slot_ref, count_ref, west_ref, east_ref, middle_ref):
    feat_dim, buckets, cap = feat_ref.shape
    turned = jnp.swapaxes(feat_ref[...].astype(F32), 0, 1)
    high, low = cell_codes(slot_ref[...])
    lane = lax.broadcasted_iota(jnp.int32, (1, cap), 1)
    high = high.astype(F32)
    low = low.astype(F32)
    for bucket in range(buckets):
        out_ref, place = (
            (west_ref, bucket)
            if bucket < 3
            else (middle_ref, bucket - 3)
            if bucket < 5
            else (east_ref, bucket - 5)
        )
        at = slice(place * cap, (place + 1) * cap)
        code = jnp.where(
            lane < count_ref[bucket], high[bucket : bucket + 1], jnp.full((1, cap), DEAD, F32)
        )
        codes = jnp.concatenate([code, low[bucket : bucket + 1]], 0)
        out_ref[:feat_dim, at] = turned[bucket].astype(BF)
        out_ref[feat_dim:, at] = codes.astype(BF)


def stay_kernel(feat_ref, slot_ref, sum_ref):
    chunk = CHUNK
    sum_ref[...] = jnp.zeros_like(sum_ref)

    def body(step):
        at = aligned(step * chunk, chunk)
        high, low = cell_codes(slot_ref[:, at])
        sum_ref[...] += scatter_part(
            feat_ref[:, at], high.astype(F32).astype(BF), low.astype(F32).astype(BF)
        )

    repeat(feat_ref.shape[1] // chunk, body)


def tiled_rows(small, count):
    width = small.shape[1]
    pick = lax.broadcasted_iota(jnp.int32, (width, count * width), 0)
    column = lax.broadcasted_iota(jnp.int32, (width, count * width), 1) % width
    return dot(small, jnp.where(pick == column, 1.0, 0.0).astype(BF))


def build_spread(encoder):
    chans, feat_dim = encoder.shape
    tiled = tiled_rows(encoder, Z)
    group = lax.broadcasted_iota(jnp.int32, tiled.shape, 1) // feat_dim
    return jnp.concatenate([jnp.where(group == layer, tiled, 0.0) for layer in range(Z)], 0).astype(
        BF
    )


def build_band(weight_ref, layer, band_ref):
    _, chans, width = weight_ref.shape
    taps = 9
    per = 128 // chans
    lane = lax.broadcasted_iota(jnp.int32, (chans, 128), 1) // chans
    weight = weight_ref[layer].astype(F32)
    turned = []
    for start in range(0, width, 128):
        source = weight[:, start : start + 128]
        if source.shape[1] < 128:
            source = jnp.concatenate([source, jnp.zeros((chans, 128 - source.shape[1]), F32)], 1)
        turned.append(
            [(source if k == 0 else pltpu.roll(source, k * chans, 1)).astype(BF) for k in range(per)]
        )
    for out_z in range(Z):
        for tap in range(taps):
            for part in range(Z // per):
                tile = jnp.zeros((chans, 128), BF)
                for depth in range(3):
                    in_z = out_z + depth - 1
                    if in_z < 0 or in_z >= Z or in_z // per != part:
                        continue
                    index = depth * taps + tap
                    moved = turned[index // per][(in_z - index) % per]
                    tile = jnp.where(lane == in_z % per, moved, tile)
                lanes = tap * Z * chans + part * 128
                band_ref[layer, out_z * chans : (out_z + 1) * chans, lanes : lanes + 128] = tile


def mean_kernel(
    west_ref, east_ref, down_ref, up_ref, part_ref, mean_ref, first_ref, last_ref, held_ref, total
):
    cap = west_ref.shape[1] // 3
    order = [
        (down_ref, 0),
        (west_ref, 1),
        (up_ref, 0),
        (down_ref, 1),
        (up_ref, 1),
        (down_ref, 2),
        (east_ref, 1),
        (up_ref, 2),
    ]
    for place, (ref, which) in enumerate(order):
        held_ref[:, place * cap : (place + 1) * cap] = ref[:, which * cap : (which + 1) * cap]
    total[...] = part_ref[...]
    chunk = CHUNK
    feat_dim = held_ref.shape[0] - 2

    def body(step):
        at = aligned(step * chunk, chunk)
        rows = held_ref[:, at]
        total[...] += scatter_part(
            rows[:feat_dim], rows[feat_dim : feat_dim + 1], rows[feat_dim + 1 : feat_dim + 2]
        )

    repeat(held_ref.shape[1] // chunk, body)
    inverse = 1.0 / jnp.maximum(total[HI * feat_dim :, :], 1.0)
    for pair in range(CX // 2):
        blocks = []
        for layer in range(Z):
            code = pair * Z + layer
            blocks.append(
                total[code * feat_dim : (code + 1) * feat_dim, :] * inverse[code : code + 1, :]
            )
        block = jnp.concatenate(blocks, 0)
        for odd in range(2):
            x = pair * 2 + odd
            turned = jnp.transpose(block[:, odd * CY : (odd + 1) * CY]).astype(BF)
            mean_ref[x * CY : (x + 1) * CY, :] = turned
            if x < HALO:
                first_ref[x * CY : (x + 1) * CY, :] = turned
            if x >= CX - HALO:
                at = x - (CX - HALO)
                last_ref[at * CY : (at + 1) * CY, :] = turned


def gelu(v):
    inner = 0.7978845608028654 * (v + 0.044715 * (v * v * v))
    return 0.5 * v * (1.0 + jnp.tanh(inner))


def grid_kernel(
    mean_ref,
    before_ref,
    after_ref,
    below_ref,
    above_ref,
    weight_ref,
    encoder_ref,
    bias_ref,
    decoder_ref,
    grid_ref,
    left,
    right,
    input_one,
    input_two,
    input_three,
    own,
    band_ref,
):
    spread = build_spread(encoder_ref[...])
    left[...] = dot(below_ref[...], spread, NT).astype(BF).astype(F32)
    right[...] = dot(above_ref[...], spread, NT).astype(BF).astype(F32)

    def store_shifted(target, x, block, lead, length):
        rows = aligned(x * length, length)
        for s, by in enumerate((1, 0, block.shape[0] - 1)):
            moved = pltpu.roll(block, by, 0) if by else block
            target[s, rows, :] = moved[lead : lead + length].astype(BF)

    def encode(ref, count, base, keep):
        def body(x):
            rows = aligned(x * CY, CY)
            inside = dot(ref[rows, :], spread, NT).astype(BF)
            if keep:
                own[rows, :] = inside
            at = x + base
            side = aligned(at * SIDE, SIDE)
            block = jnp.concatenate([left[side, :], inside.astype(F32), right[side, :]], 0)
            store_shifted(input_one, at, block, 0, PITCH)

        repeat(count, body)

    encode(before_ref, HALO, 0, False)
    encode(mean_ref, CX, HALO, True)
    encode(after_ref, HALO, HALO + CX, False)

    def conv(source, layer, x, count, length):
        pieces = []
        for q in range(3):
            rows = aligned((x + q) * length, count * length)
            for s in range(3):
                pieces.append(source[s, rows, :])
        return dot(jnp.concatenate(pieces, 1), band_ref[layer], NT) + bias_ref[layer : layer + 1, :]

    def hidden(source, layer, target, outs, count, lead, length):
        def body(step):
            x = step * count
            value = gelu(conv(source, layer, x, count, PITCH)).astype(BF).astype(F32)
            for k in range(count):
                store_shifted(
                    target, x + k, value[k * PITCH : (k + 1) * PITCH], lead, length
                )

        repeat(outs // count, body)

    build_band(weight_ref, 0, band_ref)
    hidden(input_one, 0, input_two, CX + 4, COUNTS[0], 0, PITCH)
    build_band(weight_ref, 1, band_ref)
    hidden(input_two, 1, input_three, CX + 2, COUNTS[1], SIDE, CY)

    chans = decoder_ref.shape[1]
    wide = Z * chans
    tiled = tiled_rows(decoder_ref[...], Z)
    group = lax.broadcasted_iota(jnp.int32, (Z, wide), 1) // chans
    level = lax.broadcasted_iota(jnp.int32, (Z, wide), 0)
    decode = jnp.concatenate(
        [jnp.where(group == level, tiled[k : k + 1, :], 0.0) for k in range(3)], 0
    ).astype(BF)

    def last(step):
        count = COUNTS[2]
        rows = aligned(step * count * CY, count * CY)
        value = conv(input_three, 2, step * count, count, CY) + own[rows, :].astype(F32)
        flow = dot(decode, value.astype(BF), NT)
        top = flow.astype(BF)
        low = (flow - top.astype(F32)).astype(BF)
        for pair in range(count // 2):
            lanes = slice(pair * LO, (pair + 1) * LO)
            grid_ref[0, step * (count // 2) + pair] = top[:, lanes]
            grid_ref[1, step * (count // 2) + pair] = low[:, lanes]

    build_band(weight_ref, 2, band_ref)
    repeat(CX // COUNTS[2], last)


def pick_rows(table, feats, high, low, self_weight):
    count = feats.shape[1]
    both = dot(table, onehot(low, LO))
    half = both.shape[0] // 2
    values = both[:half] + both[half:]
    level = lax.broadcasted_iota(jnp.int32, (Z, count), 0).astype(F32)
    spread = jnp.broadcast_to(high, (Z, count))
    masks = [spread == (level + float(pair * Z)) for pair in range(CX // 2)]
    live = high < float(DEAD)
    wide = feats.astype(F32)
    rows = []
    for k in range(3):
        total = jnp.zeros((Z, count), F32)
        for pair in range(CX // 2):
            at = (pair * 3 + k) * Z
            total = total + jnp.where(masks[pair], values[at : at + Z], 0.0)
        for part in range(feats.shape[0] // Z):
            part_rows = slice(part * Z, (part + 1) * Z)
            total = total + wide[part_rows] * self_weight[part_rows, k : k + 1]
        rows.append(jnp.where(live, jnp.sum(total, 0, keepdims=True), 0.0))
    return rows


def pick_kernel(grid_ref, feat_ref, slot_ref, held_ref, self_ref, out_ref, table):
    table[...] = grid_ref[...].reshape(table.shape)
    chunk = CHUNK
    feat_dim, stay = feat_ref.shape
    eye = jnp.where(
        lax.broadcasted_iota(jnp.int32, (feat_dim, feat_dim), 0)
        == lax.broadcasted_iota(jnp.int32, (feat_dim, feat_dim), 1),
        1.0,
        0.0,
    ).astype(BF)
    weight = dot(eye, self_ref[...], NT)

    def staying(step):
        at = aligned(step * chunk, chunk)
        high, low = cell_codes(slot_ref[:, at])
        rows = pick_rows(
            table[...], feat_ref[:, at], high.astype(F32), low.astype(F32).astype(BF), weight
        )
        for k in range(3):
            out_ref[k, :, at] = rows[k]

    repeat(stay // chunk, staying)

    def arrived(step):
        at = aligned(step * chunk, chunk)
        block = held_ref[:, at]
        rows = pick_rows(
            table[...],
            block[:feat_dim],
            block[feat_dim : feat_dim + 1].astype(F32),
            block[feat_dim + 1 : feat_dim + 2],
            weight,
        )
        to = aligned(stay + step * chunk, chunk)
        for k in range(3):
            out_ref[k, :, to] = rows[k]

    repeat(held_ref.shape[1] // chunk, arrived)


def on_device(
    stay_feats,
    stay_slots,
    move_feats,
    move_slots,
    move_counts,
    encoder,
    conv_weights,
    conv_biases,
    decoder,
    self_weight,
):
    feat_dim = stay_feats.shape[0]
    stay = stay_feats.shape[3]
    cap = move_feats.shape[4]
    chans = encoder.shape[0]
    own_feats = stay_feats.reshape(feat_dim, stay)
    own_slots = stay_slots.reshape(1, stay)

    width = feat_dim + 2
    west, east, middle = call(
        pack_kernel,
        "pack",
        [vmem(), vmem(), smem()],
        [
            (((width, 3 * cap), BF), vmem()),
            (((width, 3 * cap), BF), vmem()),
            (((width, 2 * cap), BF), vmem()),
        ],
        [],
        1 << 20,
        4,
    )(
        move_feats.reshape(feat_dim, 8, cap),
        move_slots.reshape(8, cap),
        move_counts.reshape(8),
    )
    west = passed_along(west, "gx", -1)
    east = passed_along(east, "gx", 1)
    down = passed_along(
        jnp.concatenate([west[:, :cap], middle[:, :cap], east[:, :cap]], 1), "gy", -1
    )
    up = passed_along(
        jnp.concatenate([west[:, 2 * cap :], middle[:, cap:], east[:, 2 * cap :]], 1), "gy", 1
    )
    sums = (HI * (feat_dim + 1), LO)
    (part,) = call(
        stay_kernel, "stay", [vmem(), vmem()], [((sums, F32), vmem())], [], 5 << 30, 8
    )(own_feats, own_slots)
    wide = Z * chans
    lanes = Z * feat_dim
    mean, first, last, held = call(
        mean_kernel,
        "mean",
        [vmem()] * 5,
        [
            (((CX * CY, lanes), BF), vmem()),
            (((HALO * CY, lanes), BF), vmem()),
            (((HALO * CY, lanes), BF), vmem()),
            (((width, 8 * cap), BF), vmem()),
        ],
        [pltpu.VMEM(sums, F32)],
        3 << 30,
        8,
    )(west, east, down, up, part)
    after = passed_along(first, "gx", -1)
    before = passed_along(last, "gx", 1)

    def edge(start):
        blocks = [
            value.reshape(-1, CY, lanes)[:, start : start + SIDE] for value in (before, mean, after)
        ]
        return jnp.concatenate(blocks, 0).reshape((CX + 2 * HALO) * SIDE, lanes)

    above = passed_along(edge(0), "gy", -1)
    below = passed_along(edge(CY - SIDE), "gy", 1)
    biases = jnp.tile(conv_biases, (1, Z))
    rows = CX + 2 * HALO
    (grid,) = call(
        grid_kernel,
        "grid",
        [vmem()] * 9,
        [(((2, CX // 2, 3 * Z, LO), BF), vmem())],
        [
            pltpu.VMEM((rows * SIDE, wide), F32),
            pltpu.VMEM((rows * SIDE, wide), F32),
            pltpu.VMEM((3, rows * PITCH, wide), BF),
            pltpu.VMEM((3, (rows - 2) * PITCH, wide), BF),
            pltpu.VMEM((3, (rows - 4) * CY, wide), BF),
            pltpu.VMEM((CX * CY, wide), BF),
            pltpu.VMEM((3, wide, 9 * wide), BF),
        ],
        8 << 30,
        32,
    )(mean, before, after, below, above, conv_weights, encoder, biases, decoder)
    (out,) = call(
        pick_kernel,
        "pick",
        [vmem()] * 5,
        [(((3, 1, stay + 8 * cap), F32), vmem())],
        [pltpu.VMEM((CX * 3 * Z, LO), BF)],
        5 << 30,
        8,
    )(grid, own_feats, own_slots, held, self_weight)
    return out.reshape(3, 1, 1, stay + 8 * cap)


def solution(mesh):
    placed = (
        P(None, "gx", "gy", "groups"),
        P("gx", "gy", "groups"),
        P(None, "gx", "gy", None, "groups"),
        P("gx", "gy", None, "groups"),
        P("gx", "gy", "groups"),
        P(),
        P(),
        P(),
        P(),
        P(),
    )
    return jax.shard_map(
        on_device,
        mesh=mesh,
        in_specs=placed,
        out_specs=P(None, "gx", "gy", "groups"),
        check_vma=False,
    )
```

```python
import functools

import jax
import jax.numpy as jnp
from jax import lax
from jax.experimental import pallas as pl
from jax.experimental.pallas import tpu as pltpu
from jax.sharding import PartitionSpec as P

Z = 8
CX = 8
CY = 128
CELLS = Z * CX * CY
LO = 2 * CY
HI = CELLS // LO
DEAD = 2 * HI
HALO = 3
SIDE = 8
KEPT = SIDE // 2
STRIP = 4 * SIDE
BF = jnp.bfloat16
F32 = jnp.float32
NT = (((1,), (1,)), ((), ()))
NN = (((1,), (0,)), ((), ()))


CHUNK = 1024
COUNTS = (4, 5, 4)


def repeat(count, body):
    for step in range(count):
        body(step)


def aligned(start, length):
    return slice(start, start + length)


def cell_codes(slots):
    cell = slots & (CELLS - 1)
    low = cell & (LO - 1)
    zx = cell // LO
    return (zx & (CX // 2 - 1)) * Z + zx // (CX // 2), low


def passed_along(x, axis, by):
    length = lax.axis_size(axis)
    return lax.ppermute(x, axis, [(i, (i + by) % length) for i in range(length)])


def dot(a, b, dims=NN):
    return lax.dot_general(a, b, dims, preferred_element_type=F32)


def vmem():
    return pl.BlockSpec(memory_space=pltpu.VMEM)


def hbm():
    return pl.BlockSpec(memory_space=pl.ANY)


def call(kernel, name, ins, outs, scratch, flops, mib):
    return pl.pallas_call(
        kernel,
        name=name,
        out_shape=[jax.ShapeDtypeStruct(*shape) for shape, _ in outs],
        in_specs=ins,
        out_specs=[spec for _, spec in outs],
        scratch_shapes=scratch,
        cost_estimate=pl.CostEstimate(flops=flops, bytes_accessed=1 << 20, transcendentals=0),
        compiler_params=pltpu.CompilerParams(vmem_limit_bytes=mib << 20),
    )


def onehot(code, count):
    rows = lax.broadcasted_iota(jnp.int32, (count, code.shape[1]), 0).astype(F32).astype(BF)
    same = rows == jnp.broadcast_to(code, rows.shape)
    return jnp.where(same, jnp.ones_like(rows), jnp.zeros_like(rows))


def scatter_part(feats, high, low):
    spread = jnp.broadcast_to(high, feats.shape)
    zero = jnp.zeros_like(feats)
    parts = [jnp.where(spread == jnp.asarray(h, BF), feats, zero) for h in range(HI)]
    parts.append(onehot(high, HI))
    return dot(jnp.concatenate(parts, 0), onehot(low, LO), NT)


def pack_kernel(
    feat_in, slot_in, count_in, west_ref, east_ref, middle_ref, feat_ref, slot_ref, count_ref, sems
):
    pairs = ((count_in, count_ref), (slot_in, slot_ref), (feat_in, feat_ref))
    copies = [pltpu.make_async_copy(a, b, sems.at[k]) for k, (a, b) in enumerate(pairs)]
    for copy in copies:
        copy.start()
    for copy in copies:
        copy.wait()
    feat_dim, buckets, cap = feat_ref.shape
    turned = jnp.swapaxes(feat_ref[...].astype(F32), 0, 1)
    high, low = cell_codes(slot_ref[...])
    lane = lax.broadcasted_iota(jnp.int32, (1, cap), 1)
    high = high.astype(F32)
    low = low.astype(F32)
    for bucket in range(buckets):
        out_ref, place = (
            (west_ref, bucket)
            if bucket < 3
            else (middle_ref, bucket - 3)
            if bucket < 5
            else (east_ref, bucket - 5)
        )
        at = slice(place * cap, (place + 1) * cap)
        code = jnp.where(
            lane < count_ref[bucket], high[bucket : bucket + 1], jnp.full((1, cap), DEAD, F32)
        )
        codes = jnp.concatenate([code, low[bucket : bucket + 1]], 0)
        out_ref[:feat_dim, at] = turned[bucket].astype(BF)
        out_ref[feat_dim:, at] = codes.astype(BF)


def stay_kernel(feat_ref, slot_ref, sum_ref):
    chunk = CHUNK
    sum_ref[...] = jnp.zeros_like(sum_ref)

    def body(step):
        at = aligned(step * chunk, chunk)
        high, low = cell_codes(slot_ref[:, at])
        sum_ref[...] += scatter_part(
            feat_ref[:, at], high.astype(F32).astype(BF), low.astype(F32).astype(BF)
        )

    repeat(feat_ref.shape[1] // chunk, body)


def tiled_rows(small, count):
    width = small.shape[1]
    pick = lax.broadcasted_iota(jnp.int32, (width, count * width), 0)
    column = lax.broadcasted_iota(jnp.int32, (width, count * width), 1) % width
    return dot(small, jnp.where(pick == column, 1.0, 0.0).astype(BF))


def build_spread(encoder):
    chans, feat_dim = encoder.shape
    tiled = tiled_rows(encoder, Z)
    group = lax.broadcasted_iota(jnp.int32, tiled.shape, 1) // feat_dim
    return jnp.concatenate([jnp.where(group == layer, tiled, 0.0) for layer in range(Z)], 0).astype(
        BF
    )


def build_band(weight_ref, layer, band_ref):
    _, chans, width = weight_ref.shape
    taps = 9
    per = 128 // chans
    lane = lax.broadcasted_iota(jnp.int32, (chans, 128), 1) // chans
    weight = weight_ref[layer].astype(F32)
    turned = []
    for start in range(0, width, 128):
        source = weight[:, start : start + 128]
        if source.shape[1] < 128:
            source = jnp.concatenate([source, jnp.zeros((chans, 128 - source.shape[1]), F32)], 1)
        turned.append(
            [(source if k == 0 else pltpu.roll(source, k * chans, 1)).astype(BF) for k in range(per)]
        )
    for out_z in range(Z):
        for tap in range(taps):
            for part in range(Z // per):
                tile = jnp.zeros((chans, 128), BF)
                for depth in range(3):
                    in_z = out_z + depth - 1
                    if in_z < 0 or in_z >= Z or in_z // per != part:
                        continue
                    index = depth * taps + tap
                    moved = turned[index // per][(in_z - index) % per]
                    tile = jnp.where(lane == in_z % per, moved, tile)
                lanes = tap * Z * chans + part * 128
                band_ref[layer, out_z * chans : (out_z + 1) * chans, lanes : lanes + 128] = tile


def mean_kernel(
    west_ref, east_ref, down_ref, up_ref, part_ref, mean_ref, first_ref, last_ref, held_ref, total
):
    cap = west_ref.shape[1] // 3
    order = [
        (down_ref, 0),
        (west_ref, 1),
        (up_ref, 0),
        (down_ref, 1),
        (up_ref, 1),
        (down_ref, 2),
        (east_ref, 1),
        (up_ref, 2),
    ]
    for place, (ref, which) in enumerate(order):
        held_ref[:, place * cap : (place + 1) * cap] = ref[:, which * cap : (which + 1) * cap]
    total[...] = part_ref[...]
    chunk = CHUNK
    feat_dim = held_ref.shape[0] - 2

    def body(step):
        at = aligned(step * chunk, chunk)
        rows = held_ref[:, at]
        total[...] += scatter_part(
            rows[:feat_dim], rows[feat_dim : feat_dim + 1], rows[feat_dim + 1 : feat_dim + 2]
        )

    repeat(held_ref.shape[1] // chunk, body)
    inverse = 1.0 / jnp.maximum(total[HI * feat_dim :, :], 1.0)
    for pair in range(CX // 2):
        blocks = []
        for layer in range(Z):
            code = pair * Z + layer
            blocks.append(
                total[code * feat_dim : (code + 1) * feat_dim, :] * inverse[code : code + 1, :]
            )
        block = jnp.concatenate(blocks, 0)
        for odd in range(2):
            x = pair * 2 + odd
            turned = jnp.transpose(block[:, odd * CY : (odd + 1) * CY]).astype(BF)
            mean_ref[x * CY : (x + 1) * CY, :] = turned
            if x < HALO:
                first_ref[x * CY : (x + 1) * CY, :] = turned
            if x >= CX - HALO:
                at = x - (CX - HALO)
                last_ref[at * CY : (at + 1) * CY, :] = turned


def gelu(v):
    inner = 0.7978845608028654 * (v + 0.044715 * (v * v * v))
    return 0.5 * v * (1.0 + jnp.tanh(inner))


def store_shifted(target, start, block):
    rows = block.shape[0]
    for s, by in enumerate((1, 0, rows - 1)):
        moved = pltpu.roll(block, by, 0) if by else block
        target[s, start : start + rows, :] = moved.astype(BF)


def conv(source, band_ref, bias_ref, layer, x, count, pitch):
    pieces = [
        source[s, (x + q) * pitch : (x + q + count) * pitch, :] for q in range(3) for s in range(3)
    ]
    return dot(jnp.concatenate(pieces, 1), band_ref[layer], NT) + bias_ref[layer : layer + 1, :]


def hidden(source, band_ref, bias_ref, layer, target, outs, count, pitch):
    for x in range(0, outs, count):
        value = gelu(conv(source, band_ref, bias_ref, layer, x, count, pitch))
        store_shifted(target, x * pitch, value.astype(BF).astype(F32))


def build_decode(decoder):
    chans = decoder.shape[1]
    tiled = tiled_rows(decoder, Z)
    group = lax.broadcasted_iota(jnp.int32, (Z, Z * chans), 1) // chans
    level = lax.broadcasted_iota(jnp.int32, (Z, Z * chans), 0)
    return jnp.concatenate(
        [jnp.where(group == level, tiled[k : k + 1, :], 0.0) for k in range(3)], 0
    ).astype(BF)


def inner_kernel(
    mean_ref,
    before_ref,
    after_ref,
    weight_ref,
    encoder_ref,
    bias_ref,
    decoder_ref,
    flow_ref,
    band_ref,
    input_one,
    input_two,
    input_three,
    own,
):
    spread = build_spread(encoder_ref[...])

    def encode(ref, base, keep):
        inside = dot(ref[...], spread, NT).astype(BF)
        if keep:
            own[...] = inside
        store_shifted(input_one, base * CY, inside.astype(F32))

    encode(before_ref, 0, False)
    encode(mean_ref, HALO, True)
    encode(after_ref, HALO + CX, False)
    build_band(weight_ref, 0, band_ref)
    hidden(input_one, band_ref, bias_ref, 0, input_two, CX + 4, COUNTS[0], CY)
    build_band(weight_ref, 1, band_ref)
    hidden(input_two, band_ref, bias_ref, 1, input_three, CX + 2, COUNTS[1], CY)
    build_band(weight_ref, 2, band_ref)
    decode = build_decode(decoder_ref[...])
    count = COUNTS[2]
    for x in range(0, CX, count):
        rows = slice(x * CY, (x + count) * CY)
        value = conv(input_three, band_ref, bias_ref, 2, x, count, CY) + own[rows, :].astype(F32)
        flow = dot(decode, value.astype(BF), NT)
        for pair in range(count // 2):
            flow_ref[x // 2 + pair] = flow[:, pair * LO : (pair + 1) * LO]


def pick_rows(table, feats, high, low, self_weight):
    count = feats.shape[1]
    both = dot(table, onehot(low, LO))
    half = both.shape[0] // 2
    values = both[:half] + both[half:]
    level = lax.broadcasted_iota(jnp.int32, (Z, count), 0).astype(F32)
    spread = jnp.broadcast_to(high, (Z, count))
    masks = [spread == (level + float(pair * Z)) for pair in range(CX // 2)]
    live = high < float(DEAD)
    wide = feats.astype(F32)
    rows = []
    for k in range(3):
        total = jnp.zeros((Z, count), F32)
        for pair in range(CX // 2):
            at = (pair * 3 + k) * Z
            total = total + jnp.where(masks[pair], values[at : at + Z], 0.0)
        for part in range(feats.shape[0] // Z):
            part_rows = slice(part * Z, (part + 1) * Z)
            total = total + wide[part_rows] * self_weight[part_rows, k : k + 1]
        rows.append(jnp.where(live, jnp.sum(total, 0, keepdims=True), 0.0))
    return rows


def pick_kernel(
    flow_ref,
    below_ref,
    low_ref,
    high_ref,
    above_ref,
    band_ref,
    encoder_ref,
    bias_ref,
    decoder_ref,
    feat_ref,
    slot_ref,
    held_ref,
    self_ref,
    out_ref,
    input_one,
    input_two,
    input_three,
    table,
):
    spread = build_spread(encoder_ref[...])
    sides = [
        dot(ref[...], spread, NT).astype(BF).astype(F32)
        for ref in (below_ref, low_ref, high_ref, above_ref)
    ]
    rows = CX + 2 * HALO
    strips = jnp.concatenate(
        [side[x * SIDE : (x + 1) * SIDE] for x in range(rows) for side in sides], 0
    )
    store_shifted(input_one, 0, strips)
    hidden(input_one, band_ref, bias_ref, 0, input_two, rows - 2, rows - 2, STRIP)
    hidden(input_two, band_ref, bias_ref, 1, input_three, rows - 4, rows - 4, STRIP)
    value = conv(input_three, band_ref, bias_ref, 2, 0, CX, STRIP)
    value = value + strips[HALO * STRIP : (HALO + CX) * STRIP]
    ends = dot(build_decode(decoder_ref[...]), value.astype(BF), NT)
    lane = lax.broadcasted_iota(jnp.int32, (ends.shape[0], CY), 1)
    for pair in range(CX // 2):
        halves = []
        for x in (2 * pair, 2 * pair + 1):
            place = x * STRIP
            source = ends[:, place // 128 * 128 : (place // 128 + 1) * 128]
            inside = place % 128
            start = pltpu.roll(source, (128 - inside - SIDE) % 128, 1)
            end = pltpu.roll(source, (CY - 3 * SIDE - inside) % 128, 1)
            middle = flow_ref[pair, :, (x % 2) * CY : (x % 2 + 1) * CY]
            halves.append(
                jnp.where(lane < KEPT, start, jnp.where(lane >= CY - KEPT, end, middle))
            )
        flow = jnp.concatenate(halves, 1)
        top = flow.astype(BF)
        size = flow.shape[0]
        table[pair * size : (pair + 1) * size, :] = top
        table[(CX // 2 + pair) * size : (CX // 2 + pair + 1) * size, :] = (
            flow - top.astype(F32)
        ).astype(BF)
    chunk = CHUNK
    feat_dim, stay = feat_ref.shape
    eye = jnp.where(
        lax.broadcasted_iota(jnp.int32, (feat_dim, feat_dim), 0)
        == lax.broadcasted_iota(jnp.int32, (feat_dim, feat_dim), 1),
        1.0,
        0.0,
    ).astype(BF)
    weight = dot(eye, self_ref[...], NT)

    def staying(step):
        at = aligned(step * chunk, chunk)
        high, low = cell_codes(slot_ref[:, at])
        rows = pick_rows(
            table[...], feat_ref[:, at], high.astype(F32), low.astype(F32).astype(BF), weight
        )
        for k in range(3):
            out_ref[k, :, at] = rows[k]

    repeat(stay // chunk, staying)

    def arrived(step):
        at = aligned(step * chunk, chunk)
        block = held_ref[:, at]
        rows = pick_rows(
            table[...],
            block[:feat_dim],
            block[feat_dim : feat_dim + 1].astype(F32),
            block[feat_dim + 1 : feat_dim + 2],
            weight,
        )
        to = aligned(stay + step * chunk, chunk)
        for k in range(3):
            out_ref[k, :, to] = rows[k]

    repeat(held_ref.shape[1] // chunk, arrived)


def on_device(
    stay_feats,
    stay_slots,
    move_feats,
    move_slots,
    move_counts,
    encoder,
    conv_weights,
    conv_biases,
    decoder,
    self_weight,
):
    feat_dim = stay_feats.shape[0]
    stay = stay_feats.shape[3]
    cap = move_feats.shape[4]
    chans = encoder.shape[0]
    own_feats = stay_feats.reshape(feat_dim, stay)
    own_slots = stay_slots.reshape(1, stay)

    width = feat_dim + 2
    west, east, middle = call(
        pack_kernel,
        "pack",
        [hbm()] * 3,
        [
            (((width, 3 * cap), BF), vmem()),
            (((width, 3 * cap), BF), vmem()),
            (((width, 2 * cap), BF), vmem()),
        ],
        [
            pltpu.VMEM((feat_dim, 8, cap), BF),
            pltpu.VMEM((8, cap), jnp.int32),
            pltpu.SMEM((8,), jnp.int32),
            pltpu.SemaphoreType.DMA((3,)),
        ],
        1 << 20,
        61,
    )(
        move_feats.reshape(feat_dim, 8, cap),
        move_slots.reshape(8, cap),
        move_counts.reshape(8),
    )
    west = passed_along(west, "gx", -1)
    east = passed_along(east, "gx", 1)
    down = passed_along(
        jnp.concatenate([west[:, :cap], middle[:, :cap], east[:, :cap]], 1), "gy", -1
    )
    up = passed_along(
        jnp.concatenate([west[:, 2 * cap :], middle[:, cap:], east[:, 2 * cap :]], 1), "gy", 1
    )
    sums = (HI * (feat_dim + 1), LO)
    (part,) = call(
        stay_kernel, "stay", [vmem(), vmem()], [((sums, F32), vmem())], [], 5 << 30, 8
    )(own_feats, own_slots)
    wide = Z * chans
    lanes = Z * feat_dim
    mean, first, last, held = call(
        mean_kernel,
        "mean",
        [vmem()] * 5,
        [
            (((CX * CY, lanes), BF), vmem()),
            (((HALO * CY, lanes), BF), vmem()),
            (((HALO * CY, lanes), BF), vmem()),
            (((width, 8 * cap), BF), vmem()),
        ],
        [pltpu.VMEM(sums, F32)],
        3 << 30,
        8,
    )(west, east, down, up, part)
    after = passed_along(first, "gx", -1)
    before = passed_along(last, "gx", 1)

    def edge(start):
        blocks = [
            value.reshape(-1, CY, lanes)[:, start : start + SIDE] for value in (before, mean, after)
        ]
        return jnp.concatenate(blocks, 0).reshape((CX + 2 * HALO) * SIDE, lanes)

    low, high = edge(0), edge(CY - SIDE)
    above = passed_along(low, "gy", -1)
    below = passed_along(high, "gy", 1)
    biases = jnp.tile(conv_biases, (1, Z))
    rows = CX + 2 * HALO
    flow, band = call(
        inner_kernel,
        "inner",
        [vmem()] * 7,
        [
            (((CX // 2, 3 * Z, LO), F32), vmem()),
            (((3, wide, 9 * wide), BF), vmem()),
        ],
        [
            pltpu.VMEM((3, rows * CY, wide), BF),
            pltpu.VMEM((3, (rows - 2) * CY, wide), BF),
            pltpu.VMEM((3, (rows - 4) * CY, wide), BF),
            pltpu.VMEM((CX * CY, wide), BF),
        ],
        8 << 30,
        24,
    )(mean, before, after, conv_weights, encoder, biases, decoder)
    (out,) = call(
        pick_kernel,
        "pick",
        [vmem()] * 13,
        [(((3, 1, stay + 8 * cap), F32), vmem())],
        [
            pltpu.VMEM((3, rows * STRIP, wide), BF),
            pltpu.VMEM((3, (rows - 2) * STRIP, wide), BF),
            pltpu.VMEM((3, (rows - 4) * STRIP, wide), BF),
            pltpu.VMEM((2 * CX // 2 * 3 * Z, LO), BF),
        ],
        5 << 30,
        16,
    )(
        flow,
        below,
        low,
        high,
        above,
        band,
        encoder,
        biases,
        decoder,
        own_feats,
        own_slots,
        held,
        self_weight,
    )
    return out.reshape(3, 1, 1, stay + 8 * cap)


def solution(mesh):
    placed = (
        P(None, "gx", "gy", "groups"),
        P("gx", "gy", "groups"),
        P(None, "gx", "gy", None, "groups"),
        P("gx", "gy", None, "groups"),
        P("gx", "gy", "groups"),
        P(),
        P(),
        P(),
        P(),
        P(),
    )
    return jax.shard_map(
        on_device,
        mesh=mesh,
        in_specs=placed,
        out_specs=P(None, "gx", "gy", "groups"),
        check_vma=False,
    )
```

```python
import functools

import jax
import jax.numpy as jnp
from jax import lax
from jax.experimental import pallas as pl
from jax.experimental.pallas import tpu as pltpu
from jax.sharding import PartitionSpec as P

Z = 8
CX = 8
CY = 128
CELLS = Z * CX * CY
LO = 2 * CY
HI = CELLS // LO
DEAD = 2 * HI
HALO = 3
SIDE = 8
KEPT = SIDE // 2
STRIP = 4 * SIDE
BF = jnp.bfloat16
F32 = jnp.float32
NT = (((1,), (1,)), ((), ()))
NN = (((1,), (0,)), ((), ()))


CHUNK = 1024
GRANT = 24
CORE_PARTS = ((0, 3), (3, 3))
INNER_PARTS = ((0, 5), (5, 5))
LAST_PARTS = ((0, 4), (4, 4))


def repeat(count, body):
    for step in range(count):
        body(step)


def aligned(start, length):
    return slice(start, start + length)


def cell_codes(slots):
    cell = slots & (CELLS - 1)
    low = cell & (LO - 1)
    zx = cell // LO
    return (zx & (CX // 2 - 1)) * Z + zx // (CX // 2), low


def passed_along(x, axis, by):
    length = lax.axis_size(axis)
    return lax.ppermute(x, axis, [(i, (i + by) % length) for i in range(length)])


def dot(a, b, dims=NN):
    return lax.dot_general(a, b, dims, preferred_element_type=F32)


def vmem():
    return pl.BlockSpec(memory_space=pltpu.VMEM)


def hbm():
    return pl.BlockSpec(memory_space=pl.ANY)


def call(kernel, name, ins, outs, scratch, flops, mib):
    return pl.pallas_call(
        kernel,
        name=name,
        out_shape=[jax.ShapeDtypeStruct(*shape) for shape, _ in outs],
        in_specs=ins,
        out_specs=[spec for _, spec in outs],
        scratch_shapes=scratch,
        cost_estimate=pl.CostEstimate(flops=flops, bytes_accessed=1 << 20, transcendentals=0),
        compiler_params=pltpu.CompilerParams(vmem_limit_bytes=mib << 20),
    )


def onehot(code, count):
    rows = lax.broadcasted_iota(jnp.int32, (count, code.shape[1]), 0).astype(F32).astype(BF)
    same = rows == jnp.broadcast_to(code, rows.shape)
    return jnp.where(same, jnp.ones_like(rows), jnp.zeros_like(rows))


def scatter_part(feats, high, low):
    spread = jnp.broadcast_to(high, feats.shape)
    zero = jnp.zeros_like(feats)
    parts = [jnp.where(spread == jnp.asarray(h, BF), feats, zero) for h in range(HI)]
    parts.append(onehot(high, HI))
    return dot(jnp.concatenate(parts, 0), onehot(low, LO), NT)


def pack_kernel(
    feat_in, slot_in, count_in, west_ref, east_ref, middle_ref, feat_ref, slot_ref, count_ref, sems
):
    pairs = ((count_in, count_ref), (slot_in, slot_ref), (feat_in, feat_ref))
    copies = [pltpu.make_async_copy(a, b, sems.at[k]) for k, (a, b) in enumerate(pairs)]
    for copy in copies:
        copy.start()
    for copy in copies:
        copy.wait()
    feat_dim, buckets, cap = feat_ref.shape
    turned = jnp.swapaxes(feat_ref[...].astype(F32), 0, 1)
    high, low = cell_codes(slot_ref[...])
    lane = lax.broadcasted_iota(jnp.int32, (1, cap), 1)
    high = high.astype(F32)
    low = low.astype(F32)
    for bucket in range(buckets):
        out_ref, place = (
            (west_ref, bucket)
            if bucket < 3
            else (middle_ref, bucket - 3)
            if bucket < 5
            else (east_ref, bucket - 5)
        )
        at = slice(place * cap, (place + 1) * cap)
        code = jnp.where(
            lane < count_ref[bucket], high[bucket : bucket + 1], jnp.full((1, cap), DEAD, F32)
        )
        codes = jnp.concatenate([code, low[bucket : bucket + 1]], 0)
        out_ref[:feat_dim, at] = turned[bucket].astype(BF)
        out_ref[feat_dim:, at] = codes.astype(BF)


def stay_kernel(feat_ref, slot_ref, sum_ref):
    chunk = CHUNK
    sum_ref[...] = jnp.zeros_like(sum_ref)

    def body(step):
        at = aligned(step * chunk, chunk)
        high, low = cell_codes(slot_ref[:, at])
        sum_ref[...] += scatter_part(
            feat_ref[:, at], high.astype(F32).astype(BF), low.astype(F32).astype(BF)
        )

    repeat(feat_ref.shape[1] // chunk, body)


def tiled_rows(small, count):
    width = small.shape[1]
    pick = lax.broadcasted_iota(jnp.int32, (width, count * width), 0)
    column = lax.broadcasted_iota(jnp.int32, (width, count * width), 1) % width
    return dot(small, jnp.where(pick == column, 1.0, 0.0).astype(BF))


def build_spread(encoder):
    chans, feat_dim = encoder.shape
    tiled = tiled_rows(encoder, Z)
    group = lax.broadcasted_iota(jnp.int32, tiled.shape, 1) // feat_dim
    return jnp.concatenate([jnp.where(group == layer, tiled, 0.0) for layer in range(Z)], 0).astype(
        BF
    )


def build_band(weight_ref, layer, band_ref):
    _, chans, width = weight_ref.shape
    taps = 9
    per = 128 // chans
    lane = lax.broadcasted_iota(jnp.int32, (chans, 128), 1) // chans
    weight = weight_ref[layer].astype(F32)
    turned = []
    for start in range(0, width, 128):
        source = weight[:, start : start + 128]
        if source.shape[1] < 128:
            source = jnp.concatenate([source, jnp.zeros((chans, 128 - source.shape[1]), F32)], 1)
        turned.append(
            [(source if k == 0 else pltpu.roll(source, k * chans, 1)).astype(BF) for k in range(per)]
        )
    for out_z in range(Z):
        for tap in range(taps):
            for part in range(Z // per):
                tile = jnp.zeros((chans, 128), BF)
                for depth in range(3):
                    in_z = out_z + depth - 1
                    if in_z < 0 or in_z >= Z or in_z // per != part:
                        continue
                    index = depth * taps + tap
                    moved = turned[index // per][(in_z - index) % per]
                    tile = jnp.where(lane == in_z % per, moved, tile)
                lanes = tap * Z * chans + part * 128
                band_ref[layer, out_z * chans : (out_z + 1) * chans, lanes : lanes + 128] = tile


def mean_kernel(
    west_ref, east_ref, down_ref, up_ref, part_ref, mean_ref, first_ref, last_ref, held_ref, total
):
    cap = west_ref.shape[1] // 3
    order = [
        (down_ref, 0),
        (west_ref, 1),
        (up_ref, 0),
        (down_ref, 1),
        (up_ref, 1),
        (down_ref, 2),
        (east_ref, 1),
        (up_ref, 2),
    ]
    for place, (ref, which) in enumerate(order):
        held_ref[:, place * cap : (place + 1) * cap] = ref[:, which * cap : (which + 1) * cap]
    total[...] = part_ref[...]
    chunk = CHUNK
    feat_dim = held_ref.shape[0] - 2

    def body(step):
        at = aligned(step * chunk, chunk)
        rows = held_ref[:, at]
        total[...] += scatter_part(
            rows[:feat_dim], rows[feat_dim : feat_dim + 1], rows[feat_dim + 1 : feat_dim + 2]
        )

    repeat(held_ref.shape[1] // chunk, body)
    inverse = 1.0 / jnp.maximum(total[HI * feat_dim :, :], 1.0)
    for pair in range(CX // 2):
        blocks = []
        for layer in range(Z):
            code = pair * Z + layer
            blocks.append(
                total[code * feat_dim : (code + 1) * feat_dim, :] * inverse[code : code + 1, :]
            )
        block = jnp.concatenate(blocks, 0)
        for odd in range(2):
            x = pair * 2 + odd
            turned = jnp.transpose(block[:, odd * CY : (odd + 1) * CY]).astype(BF)
            mean_ref[x * CY : (x + 1) * CY, :] = turned
            if x < HALO:
                first_ref[x * CY : (x + 1) * CY, :] = turned
            if x >= CX - HALO:
                at = x - (CX - HALO)
                last_ref[at * CY : (at + 1) * CY, :] = turned


def gelu(v):
    inner = 0.7978845608028654 * (v + 0.044715 * (v * v * v))
    return 0.5 * v * (1.0 + jnp.tanh(inner))


def store_shifted(target, start, block):
    rows = block.shape[0]
    for s, by in enumerate((1, 0, rows - 1)):
        moved = pltpu.roll(block, by, 0) if by else block
        target[s, start : start + rows, :] = moved.astype(BF)


def rows_of(source, pitch):
    return lambda s, x, count: source[s, x * pitch : (x + count) * pitch, :]


def conv(pick, band_ref, bias_ref, layer, x, count):
    pieces = [pick(s, x + q, count) for q in range(3) for s in range(3)]
    return dot(jnp.concatenate(pieces, 1), band_ref[layer], NT) + bias_ref[layer : layer + 1, :]


def hidden(pick, band_ref, bias_ref, layer, target, parts, pitch, base=0):
    for x, count in parts:
        value = gelu(conv(pick, band_ref, bias_ref, layer, x, count))
        store_shifted(target, (x - base) * pitch, value.astype(BF).astype(F32))


def build_decode(decoder):
    chans = decoder.shape[1]
    tiled = tiled_rows(decoder, Z)
    group = lax.broadcasted_iota(jnp.int32, (Z, Z * chans), 1) // chans
    level = lax.broadcasted_iota(jnp.int32, (Z, Z * chans), 0)
    return jnp.concatenate(
        [jnp.where(group == level, tiled[k : k + 1, :], 0.0) for k in range(3)], 0
    ).astype(BF)


def core_kernel(
    mean_ref, weight_ref, encoder_ref, bias_ref, middle_ref, band_ref, input_one
):
    inside = dot(mean_ref[...], build_spread(encoder_ref[...]), NT).astype(BF)
    store_shifted(input_one, 0, inside.astype(F32))
    build_band(weight_ref, 0, band_ref)
    hidden(
        rows_of(input_one, CY), band_ref, bias_ref, 0, middle_ref, CORE_PARTS, CY
    )
    build_band(weight_ref, 1, band_ref)
    build_band(weight_ref, 2, band_ref)


def inner_kernel(
    mean_ref,
    before_ref,
    after_ref,
    middle_ref,
    band_ref,
    encoder_ref,
    bias_ref,
    decoder_ref,
    flow_ref,
    input_one,
    input_two,
    input_three,
    own,
):
    spread = build_spread(encoder_ref[...])

    def encode(ref, base, keep):
        inside = dot(ref[...], spread, NT).astype(BF)
        if keep:
            own[...] = inside
        store_shifted(input_one, base * CY, inside.astype(F32))

    encode(before_ref, 0, False)
    encode(mean_ref, HALO, True)
    encode(after_ref, HALO + CX, False)
    hidden(
        rows_of(input_one, CY),
        band_ref,
        bias_ref,
        0,
        input_two,
        ((0, HALO), (HALO + CX - 2, HALO)),
        CY,
    )

    def mixed(s, x, count):
        blocks = []
        for ref, low, high, base in (
            (input_two, 0, HALO, 0),
            (middle_ref, HALO, HALO + CX - 2, HALO),
            (input_two, HALO + CX - 2, 2 * HALO + CX - 2, 0),
        ):
            start, end = max(low, x), min(high, x + count)
            if start < end:
                blocks.append(ref[s, (start - base) * CY : (end - base) * CY, :])
        return jnp.concatenate(blocks, 0)

    hidden(mixed, band_ref, bias_ref, 1, input_three, INNER_PARTS, CY)
    decode = build_decode(decoder_ref[...])
    source = rows_of(input_three, CY)
    for x, count in LAST_PARTS:
        rows = slice(x * CY, (x + count) * CY)
        value = conv(source, band_ref, bias_ref, 2, x, count) + own[rows, :].astype(F32)
        flow = dot(decode, value.astype(BF), NT)
        for pair in range(count // 2):
            flow_ref[x // 2 + pair] = flow[:, pair * LO : (pair + 1) * LO]


def pick_rows(table, feats, high, low, self_weight):
    count = feats.shape[1]
    both = dot(table, onehot(low, LO))
    half = both.shape[0] // 2
    values = both[:half] + both[half:]
    level = lax.broadcasted_iota(jnp.int32, (Z, count), 0).astype(F32)
    spread = jnp.broadcast_to(high, (Z, count))
    masks = [spread == (level + float(pair * Z)) for pair in range(CX // 2)]
    live = high < float(DEAD)
    wide = feats.astype(F32)
    rows = []
    for k in range(3):
        total = jnp.zeros((Z, count), F32)
        for pair in range(CX // 2):
            at = (pair * 3 + k) * Z
            total = total + jnp.where(masks[pair], values[at : at + Z], 0.0)
        for part in range(feats.shape[0] // Z):
            part_rows = slice(part * Z, (part + 1) * Z)
            total = total + wide[part_rows] * self_weight[part_rows, k : k + 1]
        rows.append(jnp.where(live, jnp.sum(total, 0, keepdims=True), 0.0))
    return rows


def pick_kernel(
    flow_ref,
    below_ref,
    low_ref,
    high_ref,
    above_ref,
    band_ref,
    encoder_ref,
    bias_ref,
    decoder_ref,
    feat_ref,
    slot_ref,
    held_ref,
    self_ref,
    out_ref,
    input_one,
    input_two,
    input_three,
    table,
):
    spread = build_spread(encoder_ref[...])
    sides = [
        dot(ref[...], spread, NT).astype(BF).astype(F32)
        for ref in (below_ref, low_ref, high_ref, above_ref)
    ]
    rows = CX + 2 * HALO
    strips = jnp.concatenate(
        [side[x * SIDE : (x + 1) * SIDE] for x in range(rows) for side in sides], 0
    )
    store_shifted(input_one, 0, strips)
    first, second, third = (rows_of(ref, STRIP) for ref in (input_one, input_two, input_three))
    hidden(first, band_ref, bias_ref, 0, input_two, ((0, rows - 2),), STRIP)
    hidden(second, band_ref, bias_ref, 1, input_three, ((0, rows - 4),), STRIP)
    value = conv(third, band_ref, bias_ref, 2, 0, CX)
    value = value + strips[HALO * STRIP : (HALO + CX) * STRIP]
    ends = dot(build_decode(decoder_ref[...]), value.astype(BF), NT)
    lane = lax.broadcasted_iota(jnp.int32, (ends.shape[0], CY), 1)
    for pair in range(CX // 2):
        halves = []
        for x in (2 * pair, 2 * pair + 1):
            place = x * STRIP
            source = ends[:, place // 128 * 128 : (place // 128 + 1) * 128]
            inside = place % 128
            start = pltpu.roll(source, (128 - inside - SIDE) % 128, 1)
            end = pltpu.roll(source, (CY - 3 * SIDE - inside) % 128, 1)
            middle = flow_ref[pair, :, (x % 2) * CY : (x % 2 + 1) * CY]
            halves.append(
                jnp.where(lane < KEPT, start, jnp.where(lane >= CY - KEPT, end, middle))
            )
        flow = jnp.concatenate(halves, 1)
        top = flow.astype(BF)
        size = flow.shape[0]
        table[pair * size : (pair + 1) * size, :] = top
        table[(CX // 2 + pair) * size : (CX // 2 + pair + 1) * size, :] = (
            flow - top.astype(F32)
        ).astype(BF)
    chunk = CHUNK
    feat_dim, stay = feat_ref.shape
    eye = jnp.where(
        lax.broadcasted_iota(jnp.int32, (feat_dim, feat_dim), 0)
        == lax.broadcasted_iota(jnp.int32, (feat_dim, feat_dim), 1),
        1.0,
        0.0,
    ).astype(BF)
    weight = dot(eye, self_ref[...], NT)

    def staying(step):
        at = aligned(step * chunk, chunk)
        high, low = cell_codes(slot_ref[:, at])
        rows = pick_rows(
            table[...], feat_ref[:, at], high.astype(F32), low.astype(F32).astype(BF), weight
        )
        for k in range(3):
            out_ref[k, :, at] = rows[k]

    repeat(stay // chunk, staying)

    def arrived(step):
        at = aligned(step * chunk, chunk)
        block = held_ref[:, at]
        rows = pick_rows(
            table[...],
            block[:feat_dim],
            block[feat_dim : feat_dim + 1].astype(F32),
            block[feat_dim + 1 : feat_dim + 2],
            weight,
        )
        to = aligned(stay + step * chunk, chunk)
        for k in range(3):
            out_ref[k, :, to] = rows[k]

    repeat(held_ref.shape[1] // chunk, arrived)


def on_device(
    stay_feats,
    stay_slots,
    move_feats,
    move_slots,
    move_counts,
    encoder,
    conv_weights,
    conv_biases,
    decoder,
    self_weight,
):
    feat_dim = stay_feats.shape[0]
    stay = stay_feats.shape[3]
    cap = move_feats.shape[4]
    chans = encoder.shape[0]
    own_feats = stay_feats.reshape(feat_dim, stay)
    own_slots = stay_slots.reshape(1, stay)

    width = feat_dim + 2
    west, east, middle = call(
        pack_kernel,
        "pack",
        [hbm()] * 3,
        [
            (((width, 3 * cap), BF), vmem()),
            (((width, 3 * cap), BF), vmem()),
            (((width, 2 * cap), BF), vmem()),
        ],
        [
            pltpu.VMEM((feat_dim, 8, cap), BF),
            pltpu.VMEM((8, cap), jnp.int32),
            pltpu.SMEM((8,), jnp.int32),
            pltpu.SemaphoreType.DMA((3,)),
        ],
        1 << 20,
        61,
    )(
        move_feats.reshape(feat_dim, 8, cap),
        move_slots.reshape(8, cap),
        move_counts.reshape(8),
    )
    west = passed_along(west, "gx", -1)
    east = passed_along(east, "gx", 1)
    down = passed_along(
        jnp.concatenate([west[:, :cap], middle[:, :cap], east[:, :cap]], 1), "gy", -1
    )
    up = passed_along(
        jnp.concatenate([west[:, 2 * cap :], middle[:, cap:], east[:, 2 * cap :]], 1), "gy", 1
    )
    sums = (HI * (feat_dim + 1), LO)
    (part,) = call(
        stay_kernel, "stay", [vmem(), vmem()], [((sums, F32), vmem())], [], 5 << 30, 8
    )(own_feats, own_slots)
    wide = Z * chans
    lanes = Z * feat_dim
    mean, first, last, held = call(
        mean_kernel,
        "mean",
        [vmem()] * 5,
        [
            (((CX * CY, lanes), BF), vmem()),
            (((HALO * CY, lanes), BF), vmem()),
            (((HALO * CY, lanes), BF), vmem()),
            (((width, 8 * cap), BF), vmem()),
        ],
        [pltpu.VMEM(sums, F32)],
        3 << 30,
        8,
    )(west, east, down, up, part)
    after = passed_along(first, "gx", -1)
    before = passed_along(last, "gx", 1)

    def edge(start):
        blocks = [
            value.reshape(-1, CY, lanes)[:, start : start + SIDE] for value in (before, mean, after)
        ]
        return jnp.concatenate(blocks, 0).reshape((CX + 2 * HALO) * SIDE, lanes)

    low, high = edge(0), edge(CY - SIDE)
    above = passed_along(low, "gy", -1)
    below = passed_along(high, "gy", 1)
    biases = jnp.tile(conv_biases, (1, Z))
    rows = CX + 2 * HALO
    middle, band = call(
        core_kernel,
        "core",
        [vmem()] * 4,
        [(((3, (CX - 2) * CY, wide), BF), vmem()), (((3, wide, 9 * wide), BF), vmem())],
        [pltpu.VMEM((3, CX * CY, wide), BF)],
        2 << 30,
        GRANT,
    )(mean, conv_weights, encoder, biases)
    (flow,) = call(
        inner_kernel,
        "inner",
        [vmem()] * 8,
        [(((CX // 2, 3 * Z, LO), F32), vmem())],
        [
            pltpu.VMEM((3, rows * CY, wide), BF),
            pltpu.VMEM((3, (rows - 2) * CY, wide), BF),
            pltpu.VMEM((3, (rows - 4) * CY, wide), BF),
            pltpu.VMEM((CX * CY, wide), BF),
        ],
        8 << 30,
        GRANT,
    )(mean, before, after, middle, band, encoder, biases, decoder)
    (out,) = call(
        pick_kernel,
        "pick",
        [vmem()] * 13,
        [(((3, 1, stay + 8 * cap), F32), vmem())],
        [
            pltpu.VMEM((3, rows * STRIP, wide), BF),
            pltpu.VMEM((3, (rows - 2) * STRIP, wide), BF),
            pltpu.VMEM((3, (rows - 4) * STRIP, wide), BF),
            pltpu.VMEM((2 * CX // 2 * 3 * Z, LO), BF),
        ],
        5 << 30,
        GRANT,
    )(
        flow,
        below,
        low,
        high,
        above,
        band,
        encoder,
        biases,
        decoder,
        own_feats,
        own_slots,
        held,
        self_weight,
    )
    return out.reshape(3, 1, 1, stay + 8 * cap)


def solution(mesh):
    placed = (
        P(None, "gx", "gy", "groups"),
        P("gx", "gy", "groups"),
        P(None, "gx", "gy", None, "groups"),
        P("gx", "gy", None, "groups"),
        P("gx", "gy", "groups"),
        P(),
        P(),
        P(),
        P(),
        P(),
    )
    return jax.shard_map(
        on_device,
        mesh=mesh,
        in_specs=placed,
        out_specs=P(None, "gx", "gy", "groups"),
        check_vma=False,
    )
```

```python
import functools

import jax
import jax.numpy as jnp
from jax import lax
from jax.experimental import pallas as pl
from jax.experimental.pallas import tpu as pltpu
from jax.sharding import PartitionSpec as P

Z = 8
CX = 8
CY = 128
CELLS = Z * CX * CY
LO = 2 * CY
HI = CELLS // LO
DEAD = 2 * HI
HALO = 3
SIDE = 8
PITCH = CY + 2 * SIDE
KEPT = SIDE // 2
STRIP = 4 * SIDE
BF = jnp.bfloat16
F32 = jnp.float32
NT = (((1,), (1,)), ((), ()))
NN = (((1,), (0,)), ((), ()))


CHUNK = 1024
GRANT = 24
CORE_PARTS = ((0, 3), (3, 3))
INNER_PARTS = ((0, 5), (5, 5))
LAST_PARTS = ((0, 4), (4, 4))


def repeat(count, body):
    for step in range(count):
        body(step)


def aligned(start, length):
    return slice(start, start + length)


def cell_codes(slots):
    cell = slots & (CELLS - 1)
    low = cell & (LO - 1)
    zx = cell // LO
    return (zx & (CX // 2 - 1)) * Z + zx // (CX // 2), low


def passed_along(x, axis, by):
    length = lax.axis_size(axis)
    return lax.ppermute(x, axis, [(i, (i + by) % length) for i in range(length)])


def dot(a, b, dims=NN):
    return lax.dot_general(a, b, dims, preferred_element_type=F32)


def vmem():
    return pl.BlockSpec(memory_space=pltpu.VMEM)


def hbm():
    return pl.BlockSpec(memory_space=pltpu.HBM)


def in_hbm(x):
    return pltpu.with_memory_space_constraint(x, pltpu.HBM)


def call(kernel, name, ins, outs, scratch, flops, mib):
    return pl.pallas_call(
        kernel,
        name=name,
        out_shape=[jax.ShapeDtypeStruct(*shape) for shape, _ in outs],
        in_specs=ins,
        out_specs=[spec for _, spec in outs],
        scratch_shapes=scratch,
        cost_estimate=pl.CostEstimate(flops=flops, bytes_accessed=1 << 20, transcendentals=0),
        compiler_params=pltpu.CompilerParams(vmem_limit_bytes=mib << 20),
    )


def onehot(code, count):
    rows = lax.broadcasted_iota(jnp.int32, (count, code.shape[1]), 0).astype(F32).astype(BF)
    same = rows == jnp.broadcast_to(code, rows.shape)
    return jnp.where(same, jnp.ones_like(rows), jnp.zeros_like(rows))


def scatter_part(feats, high, low):
    spread = jnp.broadcast_to(high, feats.shape)
    zero = jnp.zeros_like(feats)
    parts = [jnp.where(spread == jnp.asarray(h, BF), feats, zero) for h in range(HI)]
    parts.append(onehot(high, HI))
    return dot(jnp.concatenate(parts, 0), onehot(low, LO), NT)


def pack_kernel(
    feat_in, slot_in, count_in, west_ref, east_ref, middle_ref, feat_ref, slot_ref, count_ref, sems
):
    pairs = ((count_in, count_ref), (slot_in, slot_ref), (feat_in, feat_ref))
    copies = [pltpu.make_async_copy(a, b, sems.at[k]) for k, (a, b) in enumerate(pairs)]
    for copy in copies:
        copy.start()
    for copy in copies:
        copy.wait()
    feat_dim, buckets, cap = feat_ref.shape
    turned = jnp.swapaxes(feat_ref[...].astype(F32), 0, 1)
    high, low = cell_codes(slot_ref[...])
    lane = lax.broadcasted_iota(jnp.int32, (1, cap), 1)
    high = high.astype(F32)
    low = low.astype(F32)
    for bucket in range(buckets):
        out_ref, place = (
            (west_ref, bucket)
            if bucket < 3
            else (middle_ref, bucket - 3)
            if bucket < 5
            else (east_ref, bucket - 5)
        )
        at = slice(place * cap, (place + 1) * cap)
        code = jnp.where(
            lane < count_ref[bucket], high[bucket : bucket + 1], jnp.full((1, cap), DEAD, F32)
        )
        codes = jnp.concatenate([code, low[bucket : bucket + 1]], 0)
        out_ref[:feat_dim, at] = turned[bucket].astype(BF)
        out_ref[feat_dim:, at] = codes.astype(BF)


def stay_kernel(feat_in, slot_in, sum_ref, feat_ref, slot_ref, sems):
    copies = [
        pltpu.make_async_copy(slot_in, slot_ref, sems.at[0]),
        pltpu.make_async_copy(feat_in, feat_ref, sems.at[1]),
    ]
    for copy in copies:
        copy.start()
    for copy in copies:
        copy.wait()
    chunk = CHUNK
    for step in range(feat_ref.shape[1] // chunk):
        at = aligned(step * chunk, chunk)
        high, low = cell_codes(slot_ref[:, at])
        part = scatter_part(
            feat_ref[:, at], high.astype(F32).astype(BF), low.astype(F32).astype(BF)
        )
        sum_ref[...] = sum_ref[...] + part if step else part


def tiled_rows(small, count):
    width = small.shape[1]
    pick = lax.broadcasted_iota(jnp.int32, (width, count * width), 0)
    column = lax.broadcasted_iota(jnp.int32, (width, count * width), 1) % width
    return dot(small, jnp.where(pick == column, 1.0, 0.0).astype(BF))


def build_spread(encoder):
    chans, feat_dim = encoder.shape
    tiled = tiled_rows(encoder, Z)
    group = lax.broadcasted_iota(jnp.int32, tiled.shape, 1) // feat_dim
    return jnp.concatenate([jnp.where(group == layer, tiled, 0.0) for layer in range(Z)], 0).astype(
        BF
    )


def build_band(weight_ref, layer, band_ref):
    _, chans, width = weight_ref.shape
    taps = 9
    per = 128 // chans
    lane = lax.broadcasted_iota(jnp.int32, (chans, 128), 1) // chans
    weight = weight_ref[layer].astype(F32)
    turned = []
    for start in range(0, width, 128):
        source = weight[:, start : start + 128]
        if source.shape[1] < 128:
            source = jnp.concatenate([source, jnp.zeros((chans, 128 - source.shape[1]), F32)], 1)
        turned.append(
            [(source if k == 0 else pltpu.roll(source, k * chans, 1)).astype(BF) for k in range(per)]
        )
    for out_z in range(Z):
        for tap in range(taps):
            for part in range(Z // per):
                tile = jnp.zeros((chans, 128), BF)
                for depth in range(3):
                    in_z = out_z + depth - 1
                    if in_z < 0 or in_z >= Z or in_z // per != part:
                        continue
                    index = depth * taps + tap
                    moved = turned[index // per][(in_z - index) % per]
                    tile = jnp.where(lane == in_z % per, moved, tile)
                lanes = tap * Z * chans + part * 128
                band_ref[layer, out_z * chans : (out_z + 1) * chans, lanes : lanes + 128] = tile


def mean_kernel(
    west_ref, east_ref, down_ref, up_ref, part_ref, mean_ref, first_ref, last_ref, held_ref, total
):
    cap = west_ref.shape[1] // 3
    order = [
        (down_ref, 0),
        (west_ref, 1),
        (up_ref, 0),
        (down_ref, 1),
        (up_ref, 1),
        (down_ref, 2),
        (east_ref, 1),
        (up_ref, 2),
    ]
    for place, (ref, which) in enumerate(order):
        held_ref[:, place * cap : (place + 1) * cap] = ref[:, which * cap : (which + 1) * cap]
    total[...] = part_ref[...]
    chunk = CHUNK
    feat_dim = held_ref.shape[0] - 2

    def body(step):
        at = aligned(step * chunk, chunk)
        rows = held_ref[:, at]
        total[...] += scatter_part(
            rows[:feat_dim], rows[feat_dim : feat_dim + 1], rows[feat_dim + 1 : feat_dim + 2]
        )

    repeat(held_ref.shape[1] // chunk, body)
    inverse = 1.0 / jnp.maximum(total[HI * feat_dim :, :], 1.0)
    for pair in range(CX // 2):
        blocks = []
        for layer in range(Z):
            code = pair * Z + layer
            blocks.append(
                total[code * feat_dim : (code + 1) * feat_dim, :] * inverse[code : code + 1, :]
            )
        block = jnp.concatenate(blocks, 0)
        for odd in range(2):
            x = pair * 2 + odd
            turned = jnp.transpose(block[:, odd * CY : (odd + 1) * CY]).astype(BF)
            mean_ref[x * CY : (x + 1) * CY, :] = turned
            if x < HALO:
                first_ref[x * CY : (x + 1) * CY, :] = turned
            if x >= CX - HALO:
                at = x - (CX - HALO)
                last_ref[at * CY : (at + 1) * CY, :] = turned


def gelu(v):
    inner = 0.7978845608028654 * (v + 0.044715 * (v * v * v))
    return 0.5 * v * (1.0 + jnp.tanh(inner))


def store_shifted(target, start, block):
    rows = block.shape[0]
    for s, by in enumerate((1, 0, rows - 1)):
        moved = pltpu.roll(block, by, 0) if by else block
        target[s, start : start + rows, :] = moved.astype(BF)


def rows_of(source, pitch):
    return lambda s, x, count: source[s, x * pitch : (x + count) * pitch, :]


def conv(pick, band_ref, bias_ref, layer, x, count):
    pieces = [pick(s, x + q, count) for q in range(3) for s in range(3)]
    return dot(jnp.concatenate(pieces, 1), band_ref[layer], NT) + bias_ref[layer : layer + 1, :]


def hidden(pick, band_ref, bias_ref, layer, target, parts, pitch, base=0):
    for x, count in parts:
        value = gelu(conv(pick, band_ref, bias_ref, layer, x, count))
        store_shifted(target, (x - base) * pitch, value.astype(BF).astype(F32))


def build_decode(decoder):
    chans = decoder.shape[1]
    tiled = tiled_rows(decoder, Z)
    group = lax.broadcasted_iota(jnp.int32, (Z, Z * chans), 1) // chans
    level = lax.broadcasted_iota(jnp.int32, (Z, Z * chans), 0)
    return jnp.concatenate(
        [jnp.where(group == level, tiled[k : k + 1, :], 0.0) for k in range(3)], 0
    ).astype(BF)


def store_padded(target, x, value):
    side = jnp.zeros((SIDE, value.shape[1]), F32)
    for k in range(value.shape[0] // CY):
        block = jnp.concatenate([side, value[k * CY : (k + 1) * CY], side], 0)
        store_shifted(target, (x + k) * PITCH, block)


def core_kernel(
    mean_ref, weight_ref, encoder_ref, bias_ref, middle_ref, own_ref, band_ref, input_one
):
    inside = dot(mean_ref[...], build_spread(encoder_ref[...]), NT).astype(BF)
    own_ref[...] = inside
    store_shifted(input_one, 0, inside.astype(F32))
    build_band(weight_ref, 0, band_ref)
    source = rows_of(input_one, CY)
    for x, count in CORE_PARTS:
        value = gelu(conv(source, band_ref, bias_ref, 0, x, count))
        store_padded(middle_ref, x, value.astype(BF).astype(F32))
    build_band(weight_ref, 1, band_ref)
    build_band(weight_ref, 2, band_ref)


def outer_kernel(
    own_ref, before_ref, after_ref, band_ref, encoder_ref, bias_ref, outer_ref, input_one
):
    spread = build_spread(encoder_ref[...])
    near = (HALO - 1) * CY
    first = dot(before_ref[...], spread, NT).astype(BF).astype(F32)
    last = dot(after_ref[...], spread, NT).astype(BF).astype(F32)
    low = jnp.concatenate([first, own_ref[:near].astype(F32)], 0)
    high = jnp.concatenate([own_ref[CX * CY - near :].astype(F32), last], 0)
    store_shifted(input_one, 0, low)
    store_shifted(input_one, low.shape[0], high)
    source = rows_of(input_one, CY)
    for side in range(2):
        x = side * (2 * HALO - 1)
        value = gelu(conv(source, band_ref, bias_ref, 0, x, HALO))
        store_padded(outer_ref, side * HALO, value.astype(BF).astype(F32))


def pick_rows(table, feats, high, low, self_weight):
    count = feats.shape[1]
    both = dot(table, onehot(low, LO))
    half = both.shape[0] // 2
    values = both[:half] + both[half:]
    level = lax.broadcasted_iota(jnp.int32, (Z, count), 0).astype(F32)
    spread = jnp.broadcast_to(high, (Z, count))
    masks = [spread == (level + float(pair * Z)) for pair in range(CX // 2)]
    live = high < float(DEAD)
    wide = feats.astype(F32)
    rows = []
    for k in range(3):
        total = jnp.zeros((Z, count), F32)
        for pair in range(CX // 2):
            at = (pair * 3 + k) * Z
            total = total + jnp.where(masks[pair], values[at : at + Z], 0.0)
        for part in range(feats.shape[0] // Z):
            part_rows = slice(part * Z, (part + 1) * Z)
            total = total + wide[part_rows] * self_weight[part_rows, k : k + 1]
        rows.append(jnp.where(live, jnp.sum(total, 0, keepdims=True), 0.0))
    return rows


def pick_kernel(
    middle_ref,
    outer_ref,
    own_ref,
    below_ref,
    low_ref,
    high_ref,
    above_ref,
    band_ref,
    encoder_ref,
    bias_ref,
    decoder_ref,
    feat_in,
    slot_in,
    held_ref,
    self_ref,
    out_ref,
    strip_ref,
    ends_ref,
    input_three,
    table,
    feat_ref,
    slot_ref,
    sems,
):
    copies = [
        pltpu.make_async_copy(slot_in, slot_ref, sems.at[0]),
        pltpu.make_async_copy(feat_in, feat_ref, sems.at[1]),
    ]
    for copy in copies:
        copy.start()
    spread = build_spread(encoder_ref[...])
    sides = [
        dot(ref[...], spread, NT).astype(BF).astype(F32)
        for ref in (below_ref, low_ref, high_ref, above_ref)
    ]
    rows = CX + 2 * HALO
    strips = jnp.concatenate(
        [side[x * SIDE : (x + 1) * SIDE] for x in range(rows) for side in sides], 0
    )
    store_shifted(strip_ref, 0, strips)
    value = gelu(conv(rows_of(strip_ref, STRIP), band_ref, bias_ref, 0, 0, rows - 2))
    store_shifted(ends_ref, 0, value.astype(BF).astype(F32))
    wide = own_ref.shape[1]
    half = STRIP // 2
    row = lax.broadcasted_iota(jnp.int32, (half, wide), 0)

    def mixed(s, x, count):
        blocks = []
        for at in range(x, x + count):
            if at < HALO:
                ref, base = outer_ref, at
            elif at < HALO + CX - 2:
                ref, base = middle_ref, at - HALO
            else:
                ref, base = outer_ref, at - (CX - 2)
            base = base * PITCH
            low = ends_ref[s, at * STRIP : at * STRIP + half, :]
            high = ends_ref[s, at * STRIP + half : (at + 1) * STRIP, :]
            blocks.append(jnp.where(row < half - KEPT, low, ref[s, base : base + half, :]))
            blocks.append(ref[s, base + half : base + PITCH - half, :])
            blocks.append(
                jnp.where(row >= KEPT, high, ref[s, base + PITCH - half : base + PITCH, :])
            )
        return jnp.concatenate(blocks, 0)

    for x, count in INNER_PARTS:
        value = gelu(conv(mixed, band_ref, bias_ref, 1, x, count)).astype(BF).astype(F32)
        for k in range(count):
            block = value[k * PITCH : (k + 1) * PITCH]
            for s, by in enumerate((1, 0, PITCH - 1)):
                moved = pltpu.roll(block, by, 0) if by else block
                input_three[s, (x + k) * CY : (x + k + 1) * CY, :] = moved[
                    SIDE : SIDE + CY
                ].astype(BF)
    decode = build_decode(decoder_ref[...])
    source = rows_of(input_three, CY)
    size = decode.shape[0]
    for x, count in LAST_PARTS:
        own = own_ref[x * CY : (x + count) * CY, :].astype(F32)
        value = conv(source, band_ref, bias_ref, 2, x, count) + own
        flow = dot(decode, value.astype(BF), NT)
        top = flow.astype(BF)
        rest = (flow - top.astype(F32)).astype(BF)
        for k in range(count // 2):
            pair = x // 2 + k
            lanes = slice(k * LO, (k + 1) * LO)
            table[pair * size : (pair + 1) * size, :] = top[:, lanes]
            table[(CX // 2 + pair) * size : (CX // 2 + pair + 1) * size, :] = rest[:, lanes]
    for copy in copies:
        copy.wait()
    chunk = CHUNK
    feat_dim, stay = feat_ref.shape
    eye = jnp.where(
        lax.broadcasted_iota(jnp.int32, (feat_dim, feat_dim), 0)
        == lax.broadcasted_iota(jnp.int32, (feat_dim, feat_dim), 1),
        1.0,
        0.0,
    ).astype(BF)
    weight = dot(eye, self_ref[...], NT)

    def staying(step):
        at = aligned(step * chunk, chunk)
        high, low = cell_codes(slot_ref[:, at])
        rows = pick_rows(
            table[...], feat_ref[:, at], high.astype(F32), low.astype(F32).astype(BF), weight
        )
        for k in range(3):
            out_ref[k, :, at] = rows[k]

    repeat(stay // chunk, staying)

    def arrived(step):
        at = aligned(step * chunk, chunk)
        block = held_ref[:, at]
        rows = pick_rows(
            table[...],
            block[:feat_dim],
            block[feat_dim : feat_dim + 1].astype(F32),
            block[feat_dim + 1 : feat_dim + 2],
            weight,
        )
        to = aligned(stay + step * chunk, chunk)
        for k in range(3):
            out_ref[k, :, to] = rows[k]

    repeat(held_ref.shape[1] // chunk, arrived)


def on_device(
    stay_feats,
    stay_slots,
    move_feats,
    move_slots,
    move_counts,
    encoder,
    conv_weights,
    conv_biases,
    decoder,
    self_weight,
):
    feat_dim = stay_feats.shape[0]
    stay = stay_feats.shape[3]
    cap = move_feats.shape[4]
    chans = encoder.shape[0]
    own_feats = stay_feats.reshape(feat_dim, stay)
    own_slots = stay_slots.reshape(1, stay)

    width = feat_dim + 2
    west, east, middle = call(
        pack_kernel,
        "pack",
        [hbm()] * 3,
        [
            (((width, 3 * cap), BF), vmem()),
            (((width, 3 * cap), BF), vmem()),
            (((width, 2 * cap), BF), vmem()),
        ],
        [
            pltpu.VMEM((feat_dim, 8, cap), BF),
            pltpu.VMEM((8, cap), jnp.int32),
            pltpu.SMEM((8,), jnp.int32),
            pltpu.SemaphoreType.DMA((3,)),
        ],
        1 << 20,
        4,
    )(
        in_hbm(move_feats.reshape(feat_dim, 8, cap)),
        in_hbm(move_slots.reshape(8, cap)),
        in_hbm(move_counts.reshape(8)),
    )
    west = passed_along(west, "gx", -1)
    east = passed_along(east, "gx", 1)
    sums = (HI * (feat_dim + 1), LO)
    (part,) = call(
        stay_kernel,
        "stay",
        [hbm()] * 2,
        [((sums, F32), vmem())],
        [
            pltpu.VMEM((feat_dim, stay), BF),
            pltpu.VMEM((1, stay), jnp.int32),
            pltpu.SemaphoreType.DMA((2,)),
        ],
        5 << 30,
        8,
    )(in_hbm(own_feats), in_hbm(own_slots))
    west, east, part = lax.optimization_barrier((west, east, part))
    down = passed_along(
        jnp.concatenate([west[:, :cap], middle[:, :cap], east[:, :cap]], 1), "gy", -1
    )
    up = passed_along(
        jnp.concatenate([west[:, 2 * cap :], middle[:, cap:], east[:, 2 * cap :]], 1), "gy", 1
    )
    wide = Z * chans
    lanes = Z * feat_dim
    mean, first, last, held = call(
        mean_kernel,
        "mean",
        [vmem()] * 5,
        [
            (((CX * CY, lanes), BF), vmem()),
            (((HALO * CY, lanes), BF), vmem()),
            (((HALO * CY, lanes), BF), vmem()),
            (((width, 8 * cap), BF), vmem()),
        ],
        [pltpu.VMEM(sums, F32)],
        3 << 30,
        8,
    )(west, east, down, up, part)
    after = passed_along(first, "gx", -1)
    before = passed_along(last, "gx", 1)

    def edge(start):
        blocks = [
            value.reshape(-1, CY, lanes)[:, start : start + SIDE] for value in (before, mean, after)
        ]
        return jnp.concatenate(blocks, 0).reshape((CX + 2 * HALO) * SIDE, lanes)

    low, high = edge(0), edge(CY - SIDE)
    above = passed_along(low, "gy", -1)
    below = passed_along(high, "gy", 1)
    biases = jnp.tile(conv_biases, (1, Z))
    rows = CX + 2 * HALO
    taken, own, band = call(
        core_kernel,
        "core",
        [vmem()] * 4,
        [
            (((3, (CX - 2) * PITCH, wide), BF), vmem()),
            (((CX * CY, wide), BF), vmem()),
            (((3, wide, 9 * wide), BF), vmem()),
        ],
        [pltpu.VMEM((3, CX * CY, wide), BF)],
        2 << 30,
        GRANT,
    )(mean, conv_weights, encoder, biases)
    (outer,) = call(
        outer_kernel,
        "outer",
        [vmem()] * 6,
        [(((3, 2 * HALO * PITCH, wide), BF), vmem())],
        [pltpu.VMEM((3, (4 * HALO - 2) * CY, wide), BF)],
        2 << 30,
        GRANT,
    )(own, before, after, band, encoder, biases)
    (out,) = call(
        pick_kernel,
        "pick",
        [vmem()] * 11 + [hbm()] * 2 + [vmem()] * 2,
        [(((3, 1, stay + 8 * cap), F32), vmem())],
        [
            pltpu.VMEM((3, rows * STRIP, wide), BF),
            pltpu.VMEM((3, (rows - 2) * STRIP, wide), BF),
            pltpu.VMEM((3, (rows - 4) * CY, wide), BF),
            pltpu.VMEM((2 * CX // 2 * 3 * Z, LO), BF),
            pltpu.VMEM((feat_dim, stay), BF),
            pltpu.VMEM((1, stay), jnp.int32),
            pltpu.SemaphoreType.DMA((2,)),
        ],
        8 << 30,
        GRANT,
    )(
        taken,
        outer,
        own,
        below,
        low,
        high,
        above,
        band,
        encoder,
        biases,
        decoder,
        in_hbm(own_feats),
        in_hbm(own_slots),
        held,
        self_weight,
    )
    return out.reshape(3, 1, 1, stay + 8 * cap)


def solution(mesh):
    placed = (
        P(None, "gx", "gy", "groups"),
        P("gx", "gy", "groups"),
        P(None, "gx", "gy", None, "groups"),
        P("gx", "gy", None, "groups"),
        P("gx", "gy", "groups"),
        P(),
        P(),
        P(),
        P(),
        P(),
    )
    return jax.shard_map(
        on_device,
        mesh=mesh,
        in_specs=placed,
        out_specs=P(None, "gx", "gy", "groups"),
        check_vma=False,
    )
```

```python
import functools

import jax
import jax.numpy as jnp
from jax import lax
from jax.experimental import pallas as pl
from jax.experimental.pallas import tpu as pltpu
from jax.sharding import PartitionSpec as P

Z = 8
CX = 8
CY = 128
CELLS = Z * CX * CY
LO = 2 * CY
HI = CELLS // LO
DEAD = 2 * HI
HALO = 3
SIDE = 8
PITCH = CY + 2 * SIDE
KEPT = SIDE // 2
STRIP = 4 * SIDE
BF = jnp.bfloat16
F32 = jnp.float32
NT = (((1,), (1,)), ((), ()))
NN = (((1,), (0,)), ((), ()))


CHUNK = 1024
GRANT = 24
CORE_PARTS = ((0, 3), (3, 3))
ORDER = (
    (0, 0, 4),
    (0, 4, 4),
    (1, 0, 3),
    (0, 8, 4),
    (1, 3, 3),
    (2, 0, 2),
    (1, 6, 2),
    (2, 2, 2),
    (1, 8, 2),
    (2, 4, 2),
    (2, 6, 2),
)


def repeat(count, body):
    for step in range(count):
        body(step)


def aligned(start, length):
    return slice(start, start + length)


def cell_codes(slots):
    cell = slots & (CELLS - 1)
    low = cell & (LO - 1)
    zx = cell // LO
    return (zx & (CX // 2 - 1)) * Z + zx // (CX // 2), low


def passed_along(x, axis, by):
    length = lax.axis_size(axis)
    return lax.ppermute(x, axis, [(i, (i + by) % length) for i in range(length)])


def dot(a, b, dims=NN):
    return lax.dot_general(a, b, dims, preferred_element_type=F32)


def vmem():
    return pl.BlockSpec(memory_space=pltpu.VMEM)


def hbm():
    return pl.BlockSpec(memory_space=pltpu.HBM)


def in_hbm(x):
    return pltpu.with_memory_space_constraint(x, pltpu.HBM)


def call(kernel, name, ins, outs, scratch, flops, mib):
    return pl.pallas_call(
        kernel,
        name=name,
        out_shape=[jax.ShapeDtypeStruct(*shape) for shape, _ in outs],
        in_specs=ins,
        out_specs=[spec for _, spec in outs],
        scratch_shapes=scratch,
        cost_estimate=pl.CostEstimate(flops=flops, bytes_accessed=1 << 20, transcendentals=0),
        compiler_params=pltpu.CompilerParams(vmem_limit_bytes=mib << 20),
    )


def onehot(code, count):
    rows = lax.broadcasted_iota(jnp.int32, (count, code.shape[1]), 0).astype(F32).astype(BF)
    same = rows == jnp.broadcast_to(code, rows.shape)
    return jnp.where(same, jnp.ones_like(rows), jnp.zeros_like(rows))


def scatter_part(feats, high, low):
    spread = jnp.broadcast_to(high, feats.shape)
    zero = jnp.zeros_like(feats)
    parts = [jnp.where(spread == jnp.asarray(h, BF), feats, zero) for h in range(HI)]
    parts.append(onehot(high, HI))
    return dot(jnp.concatenate(parts, 0), onehot(low, LO), NT)


def pack_kernel(
    feat_in, slot_in, count_in, west_ref, east_ref, middle_ref, feat_ref, slot_ref, count_ref, sems
):
    pairs = ((count_in, count_ref), (slot_in, slot_ref), (feat_in, feat_ref))
    copies = [pltpu.make_async_copy(a, b, sems.at[k]) for k, (a, b) in enumerate(pairs)]
    for copy in copies:
        copy.start()
    for copy in copies:
        copy.wait()
    feat_dim, buckets, cap = feat_ref.shape
    turned = jnp.swapaxes(feat_ref[...].astype(F32), 0, 1)
    high, low = cell_codes(slot_ref[...])
    lane = lax.broadcasted_iota(jnp.int32, (1, cap), 1)
    high = high.astype(F32)
    low = low.astype(F32)
    for bucket in range(buckets):
        out_ref, place = (
            (west_ref, bucket)
            if bucket < 3
            else (middle_ref, bucket - 3)
            if bucket < 5
            else (east_ref, bucket - 5)
        )
        at = slice(place * cap, (place + 1) * cap)
        code = jnp.where(
            lane < count_ref[bucket], high[bucket : bucket + 1], jnp.full((1, cap), DEAD, F32)
        )
        codes = jnp.concatenate([code, low[bucket : bucket + 1]], 0)
        out_ref[:feat_dim, at] = turned[bucket].astype(BF)
        out_ref[feat_dim:, at] = codes.astype(BF)


def stay_kernel(feat_in, slot_in, sum_ref, feat_ref, slot_ref, sems):
    copies = [
        pltpu.make_async_copy(slot_in, slot_ref, sems.at[0]),
        pltpu.make_async_copy(feat_in, feat_ref, sems.at[1]),
    ]
    for copy in copies:
        copy.start()
    for copy in copies:
        copy.wait()
    chunk = CHUNK
    for step in range(feat_ref.shape[1] // chunk):
        at = aligned(step * chunk, chunk)
        high, low = cell_codes(slot_ref[:, at])
        part = scatter_part(
            feat_ref[:, at], high.astype(F32).astype(BF), low.astype(F32).astype(BF)
        )
        sum_ref[...] = sum_ref[...] + part if step else part


def tiled_rows(small, count):
    width = small.shape[1]
    pick = lax.broadcasted_iota(jnp.int32, (width, count * width), 0)
    column = lax.broadcasted_iota(jnp.int32, (width, count * width), 1) % width
    return dot(small, jnp.where(pick == column, 1.0, 0.0).astype(BF))


def build_spread(encoder):
    chans, feat_dim = encoder.shape
    tiled = tiled_rows(encoder, Z)
    group = lax.broadcasted_iota(jnp.int32, tiled.shape, 1) // feat_dim
    return jnp.concatenate([jnp.where(group == layer, tiled, 0.0) for layer in range(Z)], 0).astype(
        BF
    )


def build_band(weight_ref, layer, band_ref):
    _, chans, width = weight_ref.shape
    taps = 9
    per = 128 // chans
    lane = lax.broadcasted_iota(jnp.int32, (chans, 128), 1) // chans
    weight = weight_ref[layer].astype(F32)
    turned = []
    for start in range(0, width, 128):
        source = weight[:, start : start + 128]
        if source.shape[1] < 128:
            source = jnp.concatenate([source, jnp.zeros((chans, 128 - source.shape[1]), F32)], 1)
        turned.append(
            [(source if k == 0 else pltpu.roll(source, k * chans, 1)).astype(BF) for k in range(per)]
        )
    for out_z in range(Z):
        for tap in range(taps):
            for part in range(Z // per):
                tile = jnp.zeros((chans, 128), BF)
                for depth in range(3):
                    in_z = out_z + depth - 1
                    if in_z < 0 or in_z >= Z or in_z // per != part:
                        continue
                    index = depth * taps + tap
                    moved = turned[index // per][(in_z - index) % per]
                    tile = jnp.where(lane == in_z % per, moved, tile)
                lanes = tap * Z * chans + part * 128
                band_ref[layer, out_z * chans : (out_z + 1) * chans, lanes : lanes + 128] = tile


def mean_kernel(
    west_ref, east_ref, down_ref, up_ref, part_ref, mean_ref, first_ref, last_ref, held_ref, total
):
    cap = west_ref.shape[1] // 3
    order = [
        (down_ref, 0),
        (west_ref, 1),
        (up_ref, 0),
        (down_ref, 1),
        (up_ref, 1),
        (down_ref, 2),
        (east_ref, 1),
        (up_ref, 2),
    ]
    for place, (ref, which) in enumerate(order):
        held_ref[:, place * cap : (place + 1) * cap] = ref[:, which * cap : (which + 1) * cap]
    total[...] = part_ref[...]
    chunk = CHUNK
    feat_dim = held_ref.shape[0] - 2

    def body(step):
        at = aligned(step * chunk, chunk)
        rows = held_ref[:, at]
        total[...] += scatter_part(
            rows[:feat_dim], rows[feat_dim : feat_dim + 1], rows[feat_dim + 1 : feat_dim + 2]
        )

    repeat(held_ref.shape[1] // chunk, body)
    inverse = 1.0 / jnp.maximum(total[HI * feat_dim :, :], 1.0)
    for pair in range(CX // 2):
        blocks = []
        for layer in range(Z):
            code = pair * Z + layer
            blocks.append(
                total[code * feat_dim : (code + 1) * feat_dim, :] * inverse[code : code + 1, :]
            )
        block = jnp.concatenate(blocks, 0)
        for odd in range(2):
            x = pair * 2 + odd
            turned = jnp.transpose(block[:, odd * CY : (odd + 1) * CY]).astype(BF)
            mean_ref[x * CY : (x + 1) * CY, :] = turned
            if x < HALO:
                first_ref[x * CY : (x + 1) * CY, :] = turned
            if x >= CX - HALO:
                at = x - (CX - HALO)
                last_ref[at * CY : (at + 1) * CY, :] = turned


def gelu(v):
    inner = 0.7978845608028654 * (v + 0.044715 * (v * v * v))
    return 0.5 * v * (1.0 + jnp.tanh(inner))


def store_shifted(target, start, block):
    rows = block.shape[0]
    for s, by in enumerate((1, 0, rows - 1)):
        moved = pltpu.roll(block, by, 0) if by else block
        target[s, start : start + rows, :] = moved.astype(BF)


def rows_of(source, pitch):
    return lambda s, x, count: source[s, x * pitch : (x + count) * pitch, :]


def conv(pick, band_ref, bias_ref, layer, x, count):
    pieces = [pick(s, x + q, count) for q in range(3) for s in range(3)]
    return dot(jnp.concatenate(pieces, 1), band_ref[layer], NT) + bias_ref[layer : layer + 1, :]


def hidden(pick, band_ref, bias_ref, layer, target, parts, pitch, base=0):
    for x, count in parts:
        value = gelu(conv(pick, band_ref, bias_ref, layer, x, count))
        store_shifted(target, (x - base) * pitch, value.astype(BF).astype(F32))


def build_decode(decoder):
    chans = decoder.shape[1]
    tiled = tiled_rows(decoder, Z)
    group = lax.broadcasted_iota(jnp.int32, (Z, Z * chans), 1) // chans
    level = lax.broadcasted_iota(jnp.int32, (Z, Z * chans), 0)
    return jnp.concatenate(
        [jnp.where(group == level, tiled[k : k + 1, :], 0.0) for k in range(3)], 0
    ).astype(BF)


def store_padded(target, x, value):
    side = jnp.zeros((SIDE, value.shape[1]), F32)
    for k in range(value.shape[0] // CY):
        block = jnp.concatenate([side, value[k * CY : (k + 1) * CY], side], 0)
        store_shifted(target, (x + k) * PITCH, block)


def core_kernel(
    mean_ref,
    weight_ref,
    encoder_ref,
    bias_ref,
    decoder_ref,
    middle_ref,
    own_ref,
    band_ref,
    spread_ref,
    decode_ref,
    input_one,
):
    spread = build_spread(encoder_ref[...])
    spread_ref[...] = spread
    decode_ref[...] = build_decode(decoder_ref[...])
    inside = dot(mean_ref[...], spread, NT).astype(BF)
    own_ref[...] = inside
    store_shifted(input_one, 0, inside.astype(F32))
    build_band(weight_ref, 0, band_ref)
    source = rows_of(input_one, CY)
    for x, count in CORE_PARTS:
        value = gelu(conv(source, band_ref, bias_ref, 0, x, count))
        store_padded(middle_ref, x, value.astype(BF).astype(F32))
    build_band(weight_ref, 1, band_ref)
    build_band(weight_ref, 2, band_ref)


def outer_kernel(
    own_ref, before_ref, after_ref, band_ref, spread_ref, bias_ref, outer_ref, input_one
):
    spread = spread_ref[...]
    near = (HALO - 1) * CY
    first = dot(before_ref[...], spread, NT).astype(BF).astype(F32)
    last = dot(after_ref[...], spread, NT).astype(BF).astype(F32)
    low = jnp.concatenate([first, own_ref[:near].astype(F32)], 0)
    high = jnp.concatenate([own_ref[CX * CY - near :].astype(F32), last], 0)
    store_shifted(input_one, 0, low)
    store_shifted(input_one, low.shape[0], high)
    source = rows_of(input_one, CY)
    for side in range(2):
        x = side * (2 * HALO - 1)
        value = gelu(conv(source, band_ref, bias_ref, 0, x, HALO))
        store_padded(outer_ref, side * HALO, value.astype(BF).astype(F32))


def pick_rows(table, feats, high, low, self_weight):
    count = feats.shape[1]
    both = dot(table, onehot(low, LO))
    half = both.shape[0] // 2
    values = both[:half] + both[half:]
    level = lax.broadcasted_iota(jnp.int32, (Z, count), 0).astype(F32)
    spread = jnp.broadcast_to(high, (Z, count))
    masks = [spread == (level + float(pair * Z)) for pair in range(CX // 2)]
    live = high < float(DEAD)
    wide = feats.astype(F32)
    rows = []
    for k in range(3):
        total = jnp.zeros((Z, count), F32)
        for pair in range(CX // 2):
            at = (pair * 3 + k) * Z
            total = total + jnp.where(masks[pair], values[at : at + Z], 0.0)
        for part in range(feats.shape[0] // Z):
            part_rows = slice(part * Z, (part + 1) * Z)
            total = total + wide[part_rows] * self_weight[part_rows, k : k + 1]
        rows.append(jnp.where(live, jnp.sum(total, 0, keepdims=True), 0.0))
    return rows


def pick_kernel(
    middle_ref,
    outer_ref,
    own_ref,
    below_ref,
    low_ref,
    high_ref,
    above_ref,
    band_ref,
    spread_ref,
    bias_ref,
    decode_ref,
    feat_in,
    slot_in,
    held_ref,
    self_ref,
    out_ref,
    strip_ref,
    ends_ref,
    input_three,
    table,
    feat_ref,
    slot_ref,
    sems,
):
    copies = [
        pltpu.make_async_copy(slot_in, slot_ref, sems.at[0]),
        pltpu.make_async_copy(feat_in, feat_ref, sems.at[1]),
    ]
    for copy in copies:
        copy.start()
    spread = spread_ref[...]
    sides = [
        dot(ref[...], spread, NT).astype(BF).astype(F32)
        for ref in (below_ref, low_ref, high_ref, above_ref)
    ]
    rows = CX + 2 * HALO
    strips = jnp.concatenate(
        [side[x * SIDE : (x + 1) * SIDE] for x in range(rows) for side in sides], 0
    )
    store_shifted(strip_ref, 0, strips)

    def end_rows(x, count):
        value = gelu(conv(rows_of(strip_ref, STRIP), band_ref, bias_ref, 0, x, count))
        store_shifted(ends_ref, x * STRIP, value.astype(BF).astype(F32))

    wide = own_ref.shape[1]
    half = STRIP // 2
    row = lax.broadcasted_iota(jnp.int32, (half, wide), 0)

    def mixed(s, x, count):
        blocks = []
        for at in range(x, x + count):
            if at < HALO:
                ref, base = outer_ref, at
            elif at < HALO + CX - 2:
                ref, base = middle_ref, at - HALO
            else:
                ref, base = outer_ref, at - (CX - 2)
            base = base * PITCH
            low = ends_ref[s, at * STRIP : at * STRIP + half, :]
            high = ends_ref[s, at * STRIP + half : (at + 1) * STRIP, :]
            blocks.append(jnp.where(row < half - KEPT, low, ref[s, base : base + half, :]))
            blocks.append(ref[s, base + half : base + PITCH - half, :])
            blocks.append(
                jnp.where(row >= KEPT, high, ref[s, base + PITCH - half : base + PITCH, :])
            )
        return jnp.concatenate(blocks, 0)

    def inner_rows(x, count):
        value = gelu(conv(mixed, band_ref, bias_ref, 1, x, count)).astype(BF).astype(F32)
        for k in range(count):
            block = value[k * PITCH : (k + 1) * PITCH]
            for s, by in enumerate((1, 0, PITCH - 1)):
                moved = pltpu.roll(block, by, 0) if by else block
                input_three[s, (x + k) * CY : (x + k + 1) * CY, :] = moved[
                    SIDE : SIDE + CY
                ].astype(BF)
    decode = decode_ref[...]
    source = rows_of(input_three, CY)
    size = decode.shape[0]

    def last_rows(x, count):
        own = own_ref[x * CY : (x + count) * CY, :].astype(F32)
        value = conv(source, band_ref, bias_ref, 2, x, count) + own
        flow = dot(decode, value.astype(BF), NT)
        top = flow.astype(BF)
        rest = (flow - top.astype(F32)).astype(BF)
        for k in range(count // 2):
            pair = x // 2 + k
            lanes = slice(k * LO, (k + 1) * LO)
            table[pair * size : (pair + 1) * size, :] = top[:, lanes]
            table[(CX // 2 + pair) * size : (CX // 2 + pair + 1) * size, :] = rest[:, lanes]

    steps = (end_rows, inner_rows, last_rows)
    for step, x, count in ORDER:
        steps[step](x, count)
    for copy in copies:
        copy.wait()
    chunk = CHUNK
    feat_dim, stay = feat_ref.shape
    eye = jnp.where(
        lax.broadcasted_iota(jnp.int32, (feat_dim, feat_dim), 0)
        == lax.broadcasted_iota(jnp.int32, (feat_dim, feat_dim), 1),
        1.0,
        0.0,
    ).astype(BF)
    weight = dot(eye, self_ref[...], NT)

    def staying(step):
        at = aligned(step * chunk, chunk)
        high, low = cell_codes(slot_ref[:, at])
        rows = pick_rows(
            table[...], feat_ref[:, at], high.astype(F32), low.astype(F32).astype(BF), weight
        )
        for k in range(3):
            out_ref[k, :, at] = rows[k]

    repeat(stay // chunk, staying)

    def arrived(step):
        at = aligned(step * chunk, chunk)
        block = held_ref[:, at]
        rows = pick_rows(
            table[...],
            block[:feat_dim],
            block[feat_dim : feat_dim + 1].astype(F32),
            block[feat_dim + 1 : feat_dim + 2],
            weight,
        )
        to = aligned(stay + step * chunk, chunk)
        for k in range(3):
            out_ref[k, :, to] = rows[k]

    repeat(held_ref.shape[1] // chunk, arrived)


def on_device(
    stay_feats,
    stay_slots,
    move_feats,
    move_slots,
    move_counts,
    encoder,
    conv_weights,
    conv_biases,
    decoder,
    self_weight,
):
    feat_dim = stay_feats.shape[0]
    stay = stay_feats.shape[3]
    cap = move_feats.shape[4]
    chans = encoder.shape[0]
    own_feats = stay_feats.reshape(feat_dim, stay)
    own_slots = stay_slots.reshape(1, stay)

    width = feat_dim + 2
    west, east, middle = call(
        pack_kernel,
        "pack",
        [hbm()] * 3,
        [
            (((width, 3 * cap), BF), vmem()),
            (((width, 3 * cap), BF), vmem()),
            (((width, 2 * cap), BF), vmem()),
        ],
        [
            pltpu.VMEM((feat_dim, 8, cap), BF),
            pltpu.VMEM((8, cap), jnp.int32),
            pltpu.SMEM((8,), jnp.int32),
            pltpu.SemaphoreType.DMA((3,)),
        ],
        1 << 20,
        4,
    )(
        in_hbm(move_feats.reshape(feat_dim, 8, cap)),
        in_hbm(move_slots.reshape(8, cap)),
        in_hbm(move_counts.reshape(8)),
    )
    west = passed_along(west, "gx", -1)
    east = passed_along(east, "gx", 1)
    sums = (HI * (feat_dim + 1), LO)
    (part,) = call(
        stay_kernel,
        "stay",
        [hbm()] * 2,
        [((sums, F32), vmem())],
        [
            pltpu.VMEM((feat_dim, stay), BF),
            pltpu.VMEM((1, stay), jnp.int32),
            pltpu.SemaphoreType.DMA((2,)),
        ],
        5 << 30,
        8,
    )(in_hbm(own_feats), in_hbm(own_slots))
    west, east, part = lax.optimization_barrier((west, east, part))
    down = passed_along(
        jnp.concatenate([west[:, :cap], middle[:, :cap], east[:, :cap]], 1), "gy", -1
    )
    up = passed_along(
        jnp.concatenate([west[:, 2 * cap :], middle[:, cap:], east[:, 2 * cap :]], 1), "gy", 1
    )
    wide = Z * chans
    lanes = Z * feat_dim
    mean, first, last, held = call(
        mean_kernel,
        "mean",
        [vmem()] * 5,
        [
            (((CX * CY, lanes), BF), vmem()),
            (((HALO * CY, lanes), BF), vmem()),
            (((HALO * CY, lanes), BF), vmem()),
            (((width, 8 * cap), BF), vmem()),
        ],
        [pltpu.VMEM(sums, F32)],
        3 << 30,
        8,
    )(west, east, down, up, part)
    after = passed_along(first, "gx", -1)
    before = passed_along(last, "gx", 1)

    def edge(start):
        blocks = [
            value.reshape(-1, CY, lanes)[:, start : start + SIDE] for value in (before, mean, after)
        ]
        return jnp.concatenate(blocks, 0).reshape((CX + 2 * HALO) * SIDE, lanes)

    low, high = edge(0), edge(CY - SIDE)
    above = passed_along(low, "gy", -1)
    below = passed_along(high, "gy", 1)
    biases = jnp.tile(conv_biases, (1, Z))
    rows = CX + 2 * HALO
    taken, own, band, spread, decode = call(
        core_kernel,
        "core",
        [vmem()] * 5,
        [
            (((3, (CX - 2) * PITCH, wide), BF), vmem()),
            (((CX * CY, wide), BF), vmem()),
            (((3, wide, 9 * wide), BF), vmem()),
            (((wide, lanes), BF), vmem()),
            (((3 * Z, wide), BF), vmem()),
        ],
        [pltpu.VMEM((3, CX * CY, wide), BF)],
        2 << 30,
        GRANT,
    )(mean, conv_weights, encoder, biases, decoder)
    (outer,) = call(
        outer_kernel,
        "outer",
        [vmem()] * 6,
        [(((3, 2 * HALO * PITCH, wide), BF), vmem())],
        [pltpu.VMEM((3, (4 * HALO - 2) * CY, wide), BF)],
        2 << 30,
        GRANT,
    )(own, before, after, band, spread, biases)
    (out,) = call(
        pick_kernel,
        "pick",
        [vmem()] * 11 + [hbm()] * 2 + [vmem()] * 2,
        [(((3, 1, stay + 8 * cap), F32), vmem())],
        [
            pltpu.VMEM((3, rows * STRIP, wide), BF),
            pltpu.VMEM((3, (rows - 2) * STRIP, wide), BF),
            pltpu.VMEM((3, (rows - 4) * CY, wide), BF),
            pltpu.VMEM((2 * CX // 2 * 3 * Z, LO), BF),
            pltpu.VMEM((feat_dim, stay), BF),
            pltpu.VMEM((1, stay), jnp.int32),
            pltpu.SemaphoreType.DMA((2,)),
        ],
        8 << 30,
        GRANT,
    )(
        taken,
        outer,
        own,
        below,
        low,
        high,
        above,
        band,
        spread,
        biases,
        decode,
        in_hbm(own_feats),
        in_hbm(own_slots),
        held,
        self_weight,
    )
    return out.reshape(3, 1, 1, stay + 8 * cap)


def solution(mesh):
    placed = (
        P(None, "gx", "gy", "groups"),
        P("gx", "gy", "groups"),
        P(None, "gx", "gy", None, "groups"),
        P("gx", "gy", None, "groups"),
        P("gx", "gy", "groups"),
        P(),
        P(),
        P(),
        P(),
        P(),
    )
    return jax.shard_map(
        on_device,
        mesh=mesh,
        in_specs=placed,
        out_specs=P(None, "gx", "gy", "groups"),
        check_vma=False,
    )
```

```python
import functools

import jax
import jax.numpy as jnp
from jax import lax
from jax.experimental import pallas as pl
from jax.experimental.pallas import tpu as pltpu
from jax.sharding import PartitionSpec as P

Z = 8
CX = 8
CY = 128
CELLS = Z * CX * CY
LO = 2 * CY
HI = CELLS // LO
DEAD = 2 * HI
HALO = 3
SIDE = 8
PITCH = CY + 2 * SIDE
KEPT = SIDE // 2
STRIP = 4 * SIDE
BF = jnp.bfloat16
F32 = jnp.float32
NT = (((1,), (1,)), ((), ()))
NN = (((1,), (0,)), ((), ()))


CHUNK = 1024
GRANT = 24
CORE_PARTS = ((0, 3), (3, 3))
ORDER = (
    (0, 0, 4),
    (0, 4, 4),
    (1, 0, 3),
    (0, 8, 4),
    (1, 3, 3),
    (2, 0, 2),
    (1, 6, 2),
    (2, 2, 2),
    (1, 8, 2),
    (2, 4, 2),
    (2, 6, 2),
)


def repeat(count, body):
    for step in range(count):
        body(step)


def aligned(start, length):
    return slice(start, start + length)


def cell_codes(slots):
    cell = slots & (CELLS - 1)
    low = cell & (LO - 1)
    zx = cell // LO
    return (zx & (CX // 2 - 1)) * Z + zx // (CX // 2), low


def passed_along(x, axis, by):
    length = lax.axis_size(axis)
    return lax.ppermute(x, axis, [(i, (i + by) % length) for i in range(length)])


def dot(a, b, dims=NN):
    return lax.dot_general(a, b, dims, preferred_element_type=F32)


def vmem():
    return pl.BlockSpec(memory_space=pltpu.VMEM)


def hbm():
    return pl.BlockSpec(memory_space=pltpu.HBM)


def in_hbm(x):
    return pltpu.with_memory_space_constraint(x, pltpu.HBM)


def call(kernel, name, ins, outs, scratch, flops, mib):
    return pl.pallas_call(
        kernel,
        name=name,
        out_shape=[jax.ShapeDtypeStruct(*shape) for shape, _ in outs],
        in_specs=ins,
        out_specs=[spec for _, spec in outs],
        scratch_shapes=scratch,
        cost_estimate=pl.CostEstimate(flops=flops, bytes_accessed=1 << 20, transcendentals=0),
        compiler_params=pltpu.CompilerParams(vmem_limit_bytes=mib << 20),
    )


def onehot(code, count):
    rows = lax.broadcasted_iota(jnp.int32, (count, code.shape[1]), 0).astype(F32).astype(BF)
    same = rows == jnp.broadcast_to(code, rows.shape)
    return jnp.where(same, jnp.ones_like(rows), jnp.zeros_like(rows))


def scatter_part(feats, high, low):
    spread = jnp.broadcast_to(high, feats.shape)
    zero = jnp.zeros_like(feats)
    parts = [jnp.where(spread == jnp.asarray(h, BF), feats, zero) for h in range(HI)]
    parts.append(onehot(high, HI))
    return dot(jnp.concatenate(parts, 0), onehot(low, LO), NT)


def pack_kernel(
    feat_in, slot_in, count_in, west_ref, east_ref, middle_ref, feat_ref, slot_ref, count_ref, sems
):
    pairs = ((count_in, count_ref), (slot_in, slot_ref), (feat_in, feat_ref))
    copies = [pltpu.make_async_copy(a, b, sems.at[k]) for k, (a, b) in enumerate(pairs)]
    for copy in copies:
        copy.start()
    for copy in copies:
        copy.wait()
    feat_dim, buckets, cap = feat_ref.shape
    turned = jnp.swapaxes(feat_ref[...].astype(F32), 0, 1)
    high, low = cell_codes(slot_ref[...])
    lane = lax.broadcasted_iota(jnp.int32, (1, cap), 1)
    high = high.astype(F32)
    low = low.astype(F32)
    blocks = cap // 128
    step = (feat_dim + 2) * blocks
    for out_ref, start, end in ((west_ref, 0, 3), (middle_ref, 3, 5), (east_ref, 5, buckets)):
        for bucket in range(start, end):
            code = jnp.where(
                lane < count_ref[bucket], high[bucket : bucket + 1], jnp.full((1, cap), DEAD, F32)
            )
            base = (bucket - start) * step
            pieces = []
            for value in (turned[bucket], code, low[bucket : bucket + 1]):
                pieces += [value[:, k * 128 : (k + 1) * 128] for k in range(blocks)]
            out_ref[base : base + step, :] = jnp.concatenate(pieces, 0).astype(BF)


def stay_kernel(feat_in, slot_in, sum_ref, feat_ref, slot_ref, sems):
    copies = [
        pltpu.make_async_copy(slot_in, slot_ref, sems.at[0]),
        pltpu.make_async_copy(feat_in, feat_ref, sems.at[1]),
    ]
    for copy in copies:
        copy.start()
    for copy in copies:
        copy.wait()
    chunk = CHUNK
    for step in range(feat_ref.shape[1] // chunk):
        at = aligned(step * chunk, chunk)
        high, low = cell_codes(slot_ref[:, at])
        part = scatter_part(
            feat_ref[:, at], high.astype(F32).astype(BF), low.astype(F32).astype(BF)
        )
        sum_ref[...] = sum_ref[...] + part if step else part


def tiled_rows(small, count):
    width = small.shape[1]
    pick = lax.broadcasted_iota(jnp.int32, (width, count * width), 0)
    column = lax.broadcasted_iota(jnp.int32, (width, count * width), 1) % width
    return dot(small, jnp.where(pick == column, 1.0, 0.0).astype(BF))


def build_spread(encoder):
    chans, feat_dim = encoder.shape
    tiled = tiled_rows(encoder, Z)
    group = lax.broadcasted_iota(jnp.int32, tiled.shape, 1) // feat_dim
    return jnp.concatenate([jnp.where(group == layer, tiled, 0.0) for layer in range(Z)], 0).astype(
        BF
    )


def build_band(weight_ref, layer, band_ref):
    _, chans, width = weight_ref.shape
    taps = 9
    per = 128 // chans
    lane = lax.broadcasted_iota(jnp.int32, (chans, 128), 1) // chans
    weight = weight_ref[layer].astype(F32)
    turned = []
    for start in range(0, width, 128):
        source = weight[:, start : start + 128]
        if source.shape[1] < 128:
            source = jnp.concatenate([source, jnp.zeros((chans, 128 - source.shape[1]), F32)], 1)
        turned.append(
            [(source if k == 0 else pltpu.roll(source, k * chans, 1)).astype(BF) for k in range(per)]
        )
    for out_z in range(Z):
        for tap in range(taps):
            for part in range(Z // per):
                tile = jnp.zeros((chans, 128), BF)
                for depth in range(3):
                    in_z = out_z + depth - 1
                    if in_z < 0 or in_z >= Z or in_z // per != part:
                        continue
                    index = depth * taps + tap
                    moved = turned[index // per][(in_z - index) % per]
                    tile = jnp.where(lane == in_z % per, moved, tile)
                lanes = tap * Z * chans + part * 128
                band_ref[layer, out_z * chans : (out_z + 1) * chans, lanes : lanes + 128] = tile


def mean_kernel(
    west_ref, east_ref, down_ref, up_ref, part_ref, mean_ref, first_ref, last_ref, held_ref, total
):
    cap = held_ref.shape[1] // 8
    feat_dim = held_ref.shape[0] - 2
    blocks = cap // 128
    order = [
        (down_ref, 0),
        (west_ref, 1),
        (up_ref, 0),
        (down_ref, 1),
        (up_ref, 1),
        (down_ref, 2),
        (east_ref, 1),
        (up_ref, 2),
    ]
    for place, (ref, which) in enumerate(order):
        step = (feat_dim + 2) * blocks
        block = ref[which * step : (which + 1) * step, :].astype(F32)
        feats = jnp.concatenate(
            [block[k * feat_dim : (k + 1) * feat_dim] for k in range(blocks)], 1
        )
        codes = block[blocks * feat_dim :]
        pair = [
            jnp.concatenate([codes[j * blocks + k][None] for k in range(blocks)], 1)
            for j in range(2)
        ]
        at = slice(place * cap, (place + 1) * cap)
        held_ref[:feat_dim, at] = feats.astype(BF)
        held_ref[feat_dim:, at] = jnp.concatenate(pair, 0).astype(BF)
    total[...] = part_ref[...]
    chunk = CHUNK

    def body(step):
        at = aligned(step * chunk, chunk)
        rows = held_ref[:, at]
        total[...] += scatter_part(
            rows[:feat_dim], rows[feat_dim : feat_dim + 1], rows[feat_dim + 1 : feat_dim + 2]
        )

    repeat(held_ref.shape[1] // chunk, body)
    inverse = 1.0 / jnp.maximum(total[HI * feat_dim :, :], 1.0)
    for pair in range(CX // 2):
        blocks = []
        for layer in range(Z):
            code = pair * Z + layer
            blocks.append(
                total[code * feat_dim : (code + 1) * feat_dim, :] * inverse[code : code + 1, :]
            )
        block = jnp.concatenate(blocks, 0)
        for odd in range(2):
            x = pair * 2 + odd
            turned = jnp.transpose(block[:, odd * CY : (odd + 1) * CY]).astype(BF)
            mean_ref[x * CY : (x + 1) * CY, :] = turned
            if x < HALO:
                first_ref[x * CY : (x + 1) * CY, :] = turned
            if x >= CX - HALO:
                at = x - (CX - HALO)
                last_ref[at * CY : (at + 1) * CY, :] = turned


def gelu(v):
    inner = 0.7978845608028654 * (v + 0.044715 * (v * v * v))
    return 0.5 * v * (1.0 + jnp.tanh(inner))


def store_shifted(target, start, block):
    rows = block.shape[0]
    for s, by in enumerate((1, 0, rows - 1)):
        moved = pltpu.roll(block, by, 0) if by else block
        target[s, start : start + rows, :] = moved.astype(BF)


def rows_of(source, pitch):
    return lambda s, x, count: source[s, x * pitch : (x + count) * pitch, :]


def conv(pick, band_ref, bias_ref, layer, x, count):
    pieces = [pick(s, x + q, count) for q in range(3) for s in range(3)]
    return dot(jnp.concatenate(pieces, 1), band_ref[layer], NT) + bias_ref[layer : layer + 1, :]


def hidden(pick, band_ref, bias_ref, layer, target, parts, pitch, base=0):
    for x, count in parts:
        value = gelu(conv(pick, band_ref, bias_ref, layer, x, count))
        store_shifted(target, (x - base) * pitch, value.astype(BF).astype(F32))


def build_decode(decoder):
    chans = decoder.shape[1]
    tiled = tiled_rows(decoder, Z)
    group = lax.broadcasted_iota(jnp.int32, (Z, Z * chans), 1) // chans
    level = lax.broadcasted_iota(jnp.int32, (Z, Z * chans), 0)
    return jnp.concatenate(
        [jnp.where(group == level, tiled[k : k + 1, :], 0.0) for k in range(3)], 0
    ).astype(BF)


def store_padded(target, x, value):
    side = jnp.zeros((SIDE, value.shape[1]), F32)
    for k in range(value.shape[0] // CY):
        block = jnp.concatenate([side, value[k * CY : (k + 1) * CY], side], 0)
        store_shifted(target, (x + k) * PITCH, block)


def core_kernel(
    mean_ref,
    weight_ref,
    encoder_ref,
    bias_ref,
    decoder_ref,
    middle_ref,
    own_ref,
    band_ref,
    spread_ref,
    decode_ref,
    input_one,
):
    spread = build_spread(encoder_ref[...])
    spread_ref[...] = spread
    decode_ref[...] = build_decode(decoder_ref[...])
    inside = dot(mean_ref[...], spread, NT).astype(BF)
    own_ref[...] = inside
    store_shifted(input_one, 0, inside.astype(F32))
    build_band(weight_ref, 0, band_ref)
    source = rows_of(input_one, CY)
    for x, count in CORE_PARTS:
        value = gelu(conv(source, band_ref, bias_ref, 0, x, count))
        store_padded(middle_ref, x, value.astype(BF).astype(F32))
    build_band(weight_ref, 1, band_ref)
    build_band(weight_ref, 2, band_ref)


def outer_kernel(
    own_ref, before_ref, after_ref, band_ref, spread_ref, bias_ref, outer_ref, input_one
):
    spread = spread_ref[...]
    near = (HALO - 1) * CY
    first = dot(before_ref[...], spread, NT).astype(BF).astype(F32)
    last = dot(after_ref[...], spread, NT).astype(BF).astype(F32)
    low = jnp.concatenate([first, own_ref[:near].astype(F32)], 0)
    high = jnp.concatenate([own_ref[CX * CY - near :].astype(F32), last], 0)
    store_shifted(input_one, 0, low)
    store_shifted(input_one, low.shape[0], high)
    source = rows_of(input_one, CY)
    for side in range(2):
        x = side * (2 * HALO - 1)
        value = gelu(conv(source, band_ref, bias_ref, 0, x, HALO))
        store_padded(outer_ref, side * HALO, value.astype(BF).astype(F32))


def pick_rows(table, feats, high, low, self_weight):
    count = feats.shape[1]
    both = dot(table, onehot(low, LO))
    half = both.shape[0] // 2
    values = both[:half] + both[half:]
    level = lax.broadcasted_iota(jnp.int32, (Z, count), 0).astype(F32)
    spread = jnp.broadcast_to(high, (Z, count))
    masks = [spread == (level + float(pair * Z)) for pair in range(CX // 2)]
    live = high < float(DEAD)
    wide = feats.astype(F32)
    rows = []
    for k in range(3):
        total = jnp.zeros((Z, count), F32)
        for pair in range(CX // 2):
            at = (pair * 3 + k) * Z
            total = total + jnp.where(masks[pair], values[at : at + Z], 0.0)
        for part in range(feats.shape[0] // Z):
            part_rows = slice(part * Z, (part + 1) * Z)
            total = total + wide[part_rows] * self_weight[part_rows, k : k + 1]
        rows.append(jnp.where(live, jnp.sum(total, 0, keepdims=True), 0.0))
    return rows


def pick_kernel(
    middle_ref,
    outer_ref,
    own_ref,
    below_ref,
    low_ref,
    high_ref,
    above_ref,
    band_ref,
    spread_ref,
    bias_ref,
    decode_ref,
    feat_in,
    slot_in,
    held_ref,
    self_ref,
    out_ref,
    strip_ref,
    ends_ref,
    input_three,
    table,
    feat_ref,
    slot_ref,
    sems,
):
    copies = [
        pltpu.make_async_copy(slot_in, slot_ref, sems.at[0]),
        pltpu.make_async_copy(feat_in, feat_ref, sems.at[1]),
    ]
    for copy in copies:
        copy.start()
    spread = spread_ref[...]
    sides = [
        dot(ref[...], spread, NT).astype(BF).astype(F32)
        for ref in (below_ref, low_ref, high_ref, above_ref)
    ]
    rows = CX + 2 * HALO
    strips = jnp.concatenate(
        [side[x * SIDE : (x + 1) * SIDE] for x in range(rows) for side in sides], 0
    )
    store_shifted(strip_ref, 0, strips)

    def end_rows(x, count):
        value = gelu(conv(rows_of(strip_ref, STRIP), band_ref, bias_ref, 0, x, count))
        store_shifted(ends_ref, x * STRIP, value.astype(BF).astype(F32))

    wide = own_ref.shape[1]
    half = STRIP // 2
    row = lax.broadcasted_iota(jnp.int32, (half, wide), 0)

    def mixed(s, x, count):
        blocks = []
        for at in range(x, x + count):
            if at < HALO:
                ref, base = outer_ref, at
            elif at < HALO + CX - 2:
                ref, base = middle_ref, at - HALO
            else:
                ref, base = outer_ref, at - (CX - 2)
            base = base * PITCH
            low = ends_ref[s, at * STRIP : at * STRIP + half, :]
            high = ends_ref[s, at * STRIP + half : (at + 1) * STRIP, :]
            blocks.append(jnp.where(row < half - KEPT, low, ref[s, base : base + half, :]))
            blocks.append(ref[s, base + half : base + PITCH - half, :])
            blocks.append(
                jnp.where(row >= KEPT, high, ref[s, base + PITCH - half : base + PITCH, :])
            )
        return jnp.concatenate(blocks, 0)

    def inner_rows(x, count):
        value = gelu(conv(mixed, band_ref, bias_ref, 1, x, count)).astype(BF).astype(F32)
        for k in range(count):
            block = value[k * PITCH : (k + 1) * PITCH]
            for s, by in enumerate((1, 0, PITCH - 1)):
                moved = pltpu.roll(block, by, 0) if by else block
                input_three[s, (x + k) * CY : (x + k + 1) * CY, :] = moved[
                    SIDE : SIDE + CY
                ].astype(BF)
    decode = decode_ref[...]
    source = rows_of(input_three, CY)
    size = decode.shape[0]

    def last_rows(x, count):
        own = own_ref[x * CY : (x + count) * CY, :].astype(F32)
        value = conv(source, band_ref, bias_ref, 2, x, count) + own
        flow = dot(decode, value.astype(BF), NT)
        top = flow.astype(BF)
        rest = (flow - top.astype(F32)).astype(BF)
        for k in range(count // 2):
            pair = x // 2 + k
            lanes = slice(k * LO, (k + 1) * LO)
            table[pair * size : (pair + 1) * size, :] = top[:, lanes]
            table[(CX // 2 + pair) * size : (CX // 2 + pair + 1) * size, :] = rest[:, lanes]

    steps = (end_rows, inner_rows, last_rows)
    for step, x, count in ORDER:
        steps[step](x, count)
    for copy in copies:
        copy.wait()
    chunk = CHUNK
    feat_dim, stay = feat_ref.shape
    eye = jnp.where(
        lax.broadcasted_iota(jnp.int32, (feat_dim, feat_dim), 0)
        == lax.broadcasted_iota(jnp.int32, (feat_dim, feat_dim), 1),
        1.0,
        0.0,
    ).astype(BF)
    weight = dot(eye, self_ref[...], NT)

    def staying(step):
        at = aligned(step * chunk, chunk)
        high, low = cell_codes(slot_ref[:, at])
        rows = pick_rows(
            table[...], feat_ref[:, at], high.astype(F32), low.astype(F32).astype(BF), weight
        )
        for k in range(3):
            out_ref[k, :, at] = rows[k]

    repeat(stay // chunk, staying)

    def arrived(step):
        at = aligned(step * chunk, chunk)
        block = held_ref[:, at]
        rows = pick_rows(
            table[...],
            block[:feat_dim],
            block[feat_dim : feat_dim + 1].astype(F32),
            block[feat_dim + 1 : feat_dim + 2],
            weight,
        )
        to = aligned(stay + step * chunk, chunk)
        for k in range(3):
            out_ref[k, :, to] = rows[k]

    repeat(held_ref.shape[1] // chunk, arrived)


def on_device(
    stay_feats,
    stay_slots,
    move_feats,
    move_slots,
    move_counts,
    encoder,
    conv_weights,
    conv_biases,
    decoder,
    self_weight,
):
    feat_dim = stay_feats.shape[0]
    stay = stay_feats.shape[3]
    cap = move_feats.shape[4]
    chans = encoder.shape[0]
    own_feats = stay_feats.reshape(feat_dim, stay)
    own_slots = stay_slots.reshape(1, stay)

    width = feat_dim + 2
    west, east, middle = call(
        pack_kernel,
        "pack",
        [hbm()] * 3,
        [
            (((3 * width * cap // 128, 128), BF), vmem()),
            (((3 * width * cap // 128, 128), BF), vmem()),
            (((2 * width * cap // 128, 128), BF), vmem()),
        ],
        [
            pltpu.VMEM((feat_dim, 8, cap), BF),
            pltpu.VMEM((8, cap), jnp.int32),
            pltpu.SMEM((8,), jnp.int32),
            pltpu.SemaphoreType.DMA((3,)),
        ],
        1 << 20,
        4,
    )(
        in_hbm(move_feats.reshape(feat_dim, 8, cap)),
        in_hbm(move_slots.reshape(8, cap)),
        in_hbm(move_counts.reshape(8)),
    )
    west = passed_along(west, "gx", -1)
    east = passed_along(east, "gx", 1)
    sums = (HI * (feat_dim + 1), LO)
    (part,) = call(
        stay_kernel,
        "stay",
        [hbm()] * 2,
        [((sums, F32), vmem())],
        [
            pltpu.VMEM((feat_dim, stay), BF),
            pltpu.VMEM((1, stay), jnp.int32),
            pltpu.SemaphoreType.DMA((2,)),
        ],
        5 << 30,
        8,
    )(in_hbm(own_feats), in_hbm(own_slots))
    west, east, part = lax.optimization_barrier((west, east, part))
    step = width * cap // 128

    def joined(place, inner):
        pieces = ((west, place), (middle, inner), (east, place))
        return jnp.concatenate([ref[k * step : (k + 1) * step] for ref, k in pieces], 0)

    down = passed_along(joined(0, 0), "gy", -1)
    up = passed_along(joined(2, 1), "gy", 1)
    wide = Z * chans
    lanes = Z * feat_dim
    mean, first, last, held = call(
        mean_kernel,
        "mean",
        [vmem()] * 5,
        [
            (((CX * CY, lanes), BF), vmem()),
            (((HALO * CY, lanes), BF), vmem()),
            (((HALO * CY, lanes), BF), vmem()),
            (((width, 8 * cap), BF), vmem()),
        ],
        [pltpu.VMEM(sums, F32)],
        3 << 30,
        8,
    )(west, east, down, up, part)
    after = passed_along(first, "gx", -1)
    before = passed_along(last, "gx", 1)

    def edge(start):
        blocks = [
            value.reshape(-1, CY, lanes)[:, start : start + SIDE] for value in (before, mean, after)
        ]
        return jnp.concatenate(blocks, 0).reshape((CX + 2 * HALO) * SIDE, lanes)

    low, high = edge(0), edge(CY - SIDE)
    above = passed_along(low, "gy", -1)
    below = passed_along(high, "gy", 1)
    biases = jnp.tile(conv_biases, (1, Z))
    rows = CX + 2 * HALO
    taken, own, band, spread, decode = call(
        core_kernel,
        "core",
        [vmem()] * 5,
        [
            (((3, (CX - 2) * PITCH, wide), BF), vmem()),
            (((CX * CY, wide), BF), vmem()),
            (((3, wide, 9 * wide), BF), vmem()),
            (((wide, lanes), BF), vmem()),
            (((3 * Z, wide), BF), vmem()),
        ],
        [pltpu.VMEM((3, CX * CY, wide), BF)],
        2 << 30,
        GRANT,
    )(mean, conv_weights, encoder, biases, decoder)
    (outer,) = call(
        outer_kernel,
        "outer",
        [vmem()] * 6,
        [(((3, 2 * HALO * PITCH, wide), BF), vmem())],
        [pltpu.VMEM((3, (4 * HALO - 2) * CY, wide), BF)],
        2 << 30,
        GRANT,
    )(own, before, after, band, spread, biases)
    (out,) = call(
        pick_kernel,
        "pick",
        [vmem()] * 11 + [hbm()] * 2 + [vmem()] * 2,
        [(((3, 1, stay + 8 * cap), F32), vmem())],
        [
            pltpu.VMEM((3, rows * STRIP, wide), BF),
            pltpu.VMEM((3, (rows - 2) * STRIP, wide), BF),
            pltpu.VMEM((3, (rows - 4) * CY, wide), BF),
            pltpu.VMEM((2 * CX // 2 * 3 * Z, LO), BF),
            pltpu.VMEM((feat_dim, stay), BF),
            pltpu.VMEM((1, stay), jnp.int32),
            pltpu.SemaphoreType.DMA((2,)),
        ],
        8 << 30,
        GRANT,
    )(
        taken,
        outer,
        own,
        below,
        low,
        high,
        above,
        band,
        spread,
        biases,
        decode,
        in_hbm(own_feats),
        in_hbm(own_slots),
        held,
        self_weight,
    )
    return out.reshape(3, 1, 1, stay + 8 * cap)


def solution(mesh):
    placed = (
        P(None, "gx", "gy", "groups"),
        P("gx", "gy", "groups"),
        P(None, "gx", "gy", None, "groups"),
        P("gx", "gy", None, "groups"),
        P("gx", "gy", "groups"),
        P(),
        P(),
        P(),
        P(),
        P(),
    )
    return jax.shard_map(
        on_device,
        mesh=mesh,
        in_specs=placed,
        out_specs=P(None, "gx", "gy", "groups"),
        check_vma=False,
    )
```

```python
import functools

import jax
import jax.numpy as jnp
from jax import lax
from jax.experimental import pallas as pl
from jax.experimental.pallas import tpu as pltpu
from jax.sharding import PartitionSpec as P

Z = 8
CX = 8
CY = 128
CELLS = Z * CX * CY
LO = 2 * CY
HI = CELLS // LO
DEAD = 2 * HI
HALO = 3
SIDE = 8
PITCH = CY + 2 * SIDE
KEPT = SIDE // 2
STRIP = 4 * SIDE
BF = jnp.bfloat16
F32 = jnp.float32
NT = (((1,), (1,)), ((), ()))
NN = (((1,), (0,)), ((), ()))


CHUNK = 1024
GRANT = 24
CORE_PARTS = ((0, 3), (3, 3))
ORDER = (
    (0, 0, 4),
    (0, 4, 4),
    (1, 0, 3),
    (0, 8, 4),
    (1, 3, 3),
    (2, 0, 2),
    (1, 6, 2),
    (2, 2, 2),
    (1, 8, 2),
    (2, 4, 2),
    (2, 6, 2),
)


def repeat(count, body):
    for step in range(count):
        body(step)


def aligned(start, length):
    return slice(start, start + length)


def cell_codes(slots):
    cell = slots & (CELLS - 1)
    low = cell & (LO - 1)
    zx = cell // LO
    return (zx & (CX // 2 - 1)) * Z + zx // (CX // 2), low


def passed_along(x, axis, by):
    length = lax.axis_size(axis)
    return lax.ppermute(x, axis, [(i, (i + by) % length) for i in range(length)])


def exchanged(up, down, axis):
    length = lax.axis_size(axis)
    if length % 2:
        return passed_along(down, axis, -1), passed_along(up, axis, 1)
    even = lax.axis_index(axis) % 2 == 0
    within = [(i, i + 1 - 2 * (i % 2)) for i in range(length)]
    between = [(i, (i - 1 + 2 * (i % 2)) % length) for i in range(length)]
    inner = lax.ppermute(jnp.where(even, up, down), axis, within)
    outer = lax.ppermute(jnp.where(even, down, up), axis, between)
    return jnp.where(even, inner, outer), jnp.where(even, outer, inner)


def dot(a, b, dims=NN):
    return lax.dot_general(a, b, dims, preferred_element_type=F32)


def vmem():
    return pl.BlockSpec(memory_space=pltpu.VMEM)


def hbm():
    return pl.BlockSpec(memory_space=pltpu.HBM)


def in_hbm(x):
    return pltpu.with_memory_space_constraint(x, pltpu.HBM)


def call(kernel, name, ins, outs, scratch, flops, mib):
    return pl.pallas_call(
        kernel,
        name=name,
        out_shape=[jax.ShapeDtypeStruct(*shape) for shape, _ in outs],
        in_specs=ins,
        out_specs=[spec for _, spec in outs],
        scratch_shapes=scratch,
        cost_estimate=pl.CostEstimate(flops=flops, bytes_accessed=1 << 20, transcendentals=0),
        compiler_params=pltpu.CompilerParams(vmem_limit_bytes=mib << 20),
    )


def onehot(code, count):
    rows = lax.broadcasted_iota(jnp.int32, (count, code.shape[1]), 0).astype(F32).astype(BF)
    same = rows == jnp.broadcast_to(code, rows.shape)
    return jnp.where(same, jnp.ones_like(rows), jnp.zeros_like(rows))


def scatter_part(feats, high, low):
    spread = jnp.broadcast_to(high, feats.shape)
    zero = jnp.zeros_like(feats)
    parts = [jnp.where(spread == jnp.asarray(h, BF), feats, zero) for h in range(HI)]
    parts.append(onehot(high, HI))
    return dot(jnp.concatenate(parts, 0), onehot(low, LO), NT)


def pack_kernel(
    feat_in, slot_in, count_in, west_ref, east_ref, middle_ref, feat_ref, slot_ref, count_ref, sems
):
    pairs = ((count_in, count_ref), (slot_in, slot_ref), (feat_in, feat_ref))
    copies = [pltpu.make_async_copy(a, b, sems.at[k]) for k, (a, b) in enumerate(pairs)]
    for copy in copies:
        copy.start()
    for copy in copies:
        copy.wait()
    feat_dim, buckets, cap = feat_ref.shape
    turned = jnp.swapaxes(feat_ref[...].astype(F32), 0, 1)
    high, low = cell_codes(slot_ref[...])
    lane = lax.broadcasted_iota(jnp.int32, (1, cap), 1)
    high = high.astype(F32)
    low = low.astype(F32)
    blocks = cap // 128
    step = (feat_dim + 2) * blocks
    for out_ref, start, end in ((west_ref, 0, 3), (middle_ref, 3, 5), (east_ref, 5, buckets)):
        for bucket in range(start, end):
            code = jnp.where(
                lane < count_ref[bucket], high[bucket : bucket + 1], jnp.full((1, cap), DEAD, F32)
            )
            base = (bucket - start) * step
            pieces = []
            for value in (turned[bucket], code, low[bucket : bucket + 1]):
                pieces += [value[:, k * 128 : (k + 1) * 128] for k in range(blocks)]
            out_ref[base : base + step, :] = jnp.concatenate(pieces, 0).astype(BF)


def stay_kernel(feat_in, slot_in, sum_ref, feat_ref, slot_ref, sems):
    copies = [
        pltpu.make_async_copy(slot_in, slot_ref, sems.at[0]),
        pltpu.make_async_copy(feat_in, feat_ref, sems.at[1]),
    ]
    for copy in copies:
        copy.start()
    for copy in copies:
        copy.wait()
    chunk = CHUNK
    for step in range(feat_ref.shape[1] // chunk):
        at = aligned(step * chunk, chunk)
        high, low = cell_codes(slot_ref[:, at])
        part = scatter_part(
            feat_ref[:, at], high.astype(F32).astype(BF), low.astype(F32).astype(BF)
        )
        sum_ref[...] = sum_ref[...] + part if step else part


def tiled_rows(small, count):
    width = small.shape[1]
    pick = lax.broadcasted_iota(jnp.int32, (width, count * width), 0)
    column = lax.broadcasted_iota(jnp.int32, (width, count * width), 1) % width
    return dot(small, jnp.where(pick == column, 1.0, 0.0).astype(BF))


def build_spread(encoder):
    chans, feat_dim = encoder.shape
    tiled = tiled_rows(encoder, Z)
    group = lax.broadcasted_iota(jnp.int32, tiled.shape, 1) // feat_dim
    return jnp.concatenate([jnp.where(group == layer, tiled, 0.0) for layer in range(Z)], 0).astype(
        BF
    )


def build_band(weight_ref, layer, band_ref):
    _, chans, width = weight_ref.shape
    taps = 9
    per = 128 // chans
    lane = lax.broadcasted_iota(jnp.int32, (chans, 128), 1) // chans
    weight = weight_ref[layer].astype(F32)
    turned = []
    for start in range(0, width, 128):
        source = weight[:, start : start + 128]
        if source.shape[1] < 128:
            source = jnp.concatenate([source, jnp.zeros((chans, 128 - source.shape[1]), F32)], 1)
        turned.append(
            [(source if k == 0 else pltpu.roll(source, k * chans, 1)).astype(BF) for k in range(per)]
        )
    for out_z in range(Z):
        for tap in range(taps):
            for part in range(Z // per):
                tile = jnp.zeros((chans, 128), BF)
                for depth in range(3):
                    in_z = out_z + depth - 1
                    if in_z < 0 or in_z >= Z or in_z // per != part:
                        continue
                    index = depth * taps + tap
                    moved = turned[index // per][(in_z - index) % per]
                    tile = jnp.where(lane == in_z % per, moved, tile)
                lanes = tap * Z * chans + part * 128
                band_ref[layer, out_z * chans : (out_z + 1) * chans, lanes : lanes + 128] = tile


def mean_kernel(
    west_ref, east_ref, down_ref, up_ref, part_ref, mean_ref, first_ref, last_ref, held_ref, total
):
    cap = held_ref.shape[1] // 8
    feat_dim = held_ref.shape[0] - 2
    blocks = cap // 128
    order = [
        (down_ref, 0),
        (west_ref, 1),
        (up_ref, 0),
        (down_ref, 1),
        (up_ref, 1),
        (down_ref, 2),
        (east_ref, 1),
        (up_ref, 2),
    ]
    for place, (ref, which) in enumerate(order):
        step = (feat_dim + 2) * blocks
        block = ref[which * step : (which + 1) * step, :].astype(F32)
        feats = jnp.concatenate(
            [block[k * feat_dim : (k + 1) * feat_dim] for k in range(blocks)], 1
        )
        codes = block[blocks * feat_dim :]
        pair = [
            jnp.concatenate([codes[j * blocks + k][None] for k in range(blocks)], 1)
            for j in range(2)
        ]
        at = slice(place * cap, (place + 1) * cap)
        held_ref[:feat_dim, at] = feats.astype(BF)
        held_ref[feat_dim:, at] = jnp.concatenate(pair, 0).astype(BF)
    total[...] = part_ref[...]
    chunk = CHUNK

    def body(step):
        at = aligned(step * chunk, chunk)
        rows = held_ref[:, at]
        total[...] += scatter_part(
            rows[:feat_dim], rows[feat_dim : feat_dim + 1], rows[feat_dim + 1 : feat_dim + 2]
        )

    repeat(held_ref.shape[1] // chunk, body)
    inverse = 1.0 / jnp.maximum(total[HI * feat_dim :, :], 1.0)
    for pair in range(CX // 2):
        blocks = []
        for layer in range(Z):
            code = pair * Z + layer
            blocks.append(
                total[code * feat_dim : (code + 1) * feat_dim, :] * inverse[code : code + 1, :]
            )
        block = jnp.concatenate(blocks, 0)
        for odd in range(2):
            x = pair * 2 + odd
            turned = jnp.transpose(block[:, odd * CY : (odd + 1) * CY]).astype(BF)
            mean_ref[x * CY : (x + 1) * CY, :] = turned
            if x < HALO:
                first_ref[x * CY : (x + 1) * CY, :] = turned
            if x >= CX - HALO:
                at = x - (CX - HALO)
                last_ref[at * CY : (at + 1) * CY, :] = turned


def gelu(v):
    inner = 0.7978845608028654 * (v + 0.044715 * (v * v * v))
    return 0.5 * v * (1.0 + jnp.tanh(inner))


def store_shifted(target, start, block):
    rows = block.shape[0]
    for s, by in enumerate((1, 0, rows - 1)):
        moved = pltpu.roll(block, by, 0) if by else block
        target[s, start : start + rows, :] = moved.astype(BF)


def rows_of(source, pitch):
    return lambda s, x, count: source[s, x * pitch : (x + count) * pitch, :]


def conv(pick, band_ref, bias_ref, layer, x, count):
    pieces = [pick(s, x + q, count) for q in range(3) for s in range(3)]
    return dot(jnp.concatenate(pieces, 1), band_ref[layer], NT) + bias_ref[layer : layer + 1, :]


def hidden(pick, band_ref, bias_ref, layer, target, parts, pitch, base=0):
    for x, count in parts:
        value = gelu(conv(pick, band_ref, bias_ref, layer, x, count))
        store_shifted(target, (x - base) * pitch, value.astype(BF).astype(F32))


def build_decode(decoder):
    chans = decoder.shape[1]
    tiled = tiled_rows(decoder, Z)
    group = lax.broadcasted_iota(jnp.int32, (Z, Z * chans), 1) // chans
    level = lax.broadcasted_iota(jnp.int32, (Z, Z * chans), 0)
    return jnp.concatenate(
        [jnp.where(group == level, tiled[k : k + 1, :], 0.0) for k in range(3)], 0
    ).astype(BF)


def store_padded(target, x, value):
    side = jnp.zeros((SIDE, value.shape[1]), F32)
    for k in range(value.shape[0] // CY):
        block = jnp.concatenate([side, value[k * CY : (k + 1) * CY], side], 0)
        store_shifted(target, (x + k) * PITCH, block)


def core_kernel(
    mean_ref,
    weight_ref,
    encoder_ref,
    bias_ref,
    decoder_ref,
    middle_ref,
    own_ref,
    band_ref,
    spread_ref,
    decode_ref,
    input_one,
):
    spread = build_spread(encoder_ref[...])
    spread_ref[...] = spread
    decode_ref[...] = build_decode(decoder_ref[...])
    inside = dot(mean_ref[...], spread, NT).astype(BF)
    own_ref[...] = inside
    store_shifted(input_one, 0, inside.astype(F32))
    build_band(weight_ref, 0, band_ref)
    source = rows_of(input_one, CY)
    for x, count in CORE_PARTS:
        value = gelu(conv(source, band_ref, bias_ref, 0, x, count))
        store_padded(middle_ref, x, value.astype(BF).astype(F32))
    build_band(weight_ref, 1, band_ref)
    build_band(weight_ref, 2, band_ref)


def outer_kernel(
    own_ref, before_ref, after_ref, band_ref, spread_ref, bias_ref, outer_ref, input_one
):
    spread = spread_ref[...]
    near = (HALO - 1) * CY
    first = dot(before_ref[...], spread, NT).astype(BF).astype(F32)
    last = dot(after_ref[...], spread, NT).astype(BF).astype(F32)
    low = jnp.concatenate([first, own_ref[:near].astype(F32)], 0)
    high = jnp.concatenate([own_ref[CX * CY - near :].astype(F32), last], 0)
    store_shifted(input_one, 0, low)
    store_shifted(input_one, low.shape[0], high)
    source = rows_of(input_one, CY)
    for side in range(2):
        x = side * (2 * HALO - 1)
        value = gelu(conv(source, band_ref, bias_ref, 0, x, HALO))
        store_padded(outer_ref, side * HALO, value.astype(BF).astype(F32))


def pick_rows(table, feats, high, low, self_weight):
    count = feats.shape[1]
    both = dot(table, onehot(low, LO))
    half = both.shape[0] // 2
    values = both[:half] + both[half:]
    level = lax.broadcasted_iota(jnp.int32, (Z, count), 0).astype(F32)
    spread = jnp.broadcast_to(high, (Z, count))
    masks = [spread == (level + float(pair * Z)) for pair in range(CX // 2)]
    live = high < float(DEAD)
    wide = feats.astype(F32)
    rows = []
    for k in range(3):
        total = jnp.zeros((Z, count), F32)
        for pair in range(CX // 2):
            at = (pair * 3 + k) * Z
            total = total + jnp.where(masks[pair], values[at : at + Z], 0.0)
        for part in range(feats.shape[0] // Z):
            part_rows = slice(part * Z, (part + 1) * Z)
            total = total + wide[part_rows] * self_weight[part_rows, k : k + 1]
        rows.append(jnp.where(live, jnp.sum(total, 0, keepdims=True), 0.0))
    return rows


def pick_kernel(
    middle_ref,
    outer_ref,
    own_ref,
    below_ref,
    low_ref,
    high_ref,
    above_ref,
    band_ref,
    spread_ref,
    bias_ref,
    decode_ref,
    feat_in,
    slot_in,
    held_ref,
    self_ref,
    out_ref,
    strip_ref,
    ends_ref,
    input_three,
    table,
    feat_ref,
    slot_ref,
    sems,
):
    copies = [
        pltpu.make_async_copy(slot_in, slot_ref, sems.at[0]),
        pltpu.make_async_copy(feat_in, feat_ref, sems.at[1]),
    ]
    for copy in copies:
        copy.start()
    spread = spread_ref[...]
    sides = [
        dot(ref[...], spread, NT).astype(BF).astype(F32)
        for ref in (below_ref, low_ref, high_ref, above_ref)
    ]
    rows = CX + 2 * HALO
    strips = jnp.concatenate(
        [side[x * SIDE : (x + 1) * SIDE] for x in range(rows) for side in sides], 0
    )
    store_shifted(strip_ref, 0, strips)

    def end_rows(x, count):
        value = gelu(conv(rows_of(strip_ref, STRIP), band_ref, bias_ref, 0, x, count))
        store_shifted(ends_ref, x * STRIP, value.astype(BF).astype(F32))

    wide = own_ref.shape[1]
    half = STRIP // 2
    row = lax.broadcasted_iota(jnp.int32, (half, wide), 0)

    def mixed(s, x, count):
        blocks = []
        for at in range(x, x + count):
            if at < HALO:
                ref, base = outer_ref, at
            elif at < HALO + CX - 2:
                ref, base = middle_ref, at - HALO
            else:
                ref, base = outer_ref, at - (CX - 2)
            base = base * PITCH
            low = ends_ref[s, at * STRIP : at * STRIP + half, :]
            high = ends_ref[s, at * STRIP + half : (at + 1) * STRIP, :]
            blocks.append(jnp.where(row < half - KEPT, low, ref[s, base : base + half, :]))
            blocks.append(ref[s, base + half : base + PITCH - half, :])
            blocks.append(
                jnp.where(row >= KEPT, high, ref[s, base + PITCH - half : base + PITCH, :])
            )
        return jnp.concatenate(blocks, 0)

    def inner_rows(x, count):
        value = gelu(conv(mixed, band_ref, bias_ref, 1, x, count)).astype(BF).astype(F32)
        for k in range(count):
            block = value[k * PITCH : (k + 1) * PITCH]
            for s, by in enumerate((1, 0, PITCH - 1)):
                moved = pltpu.roll(block, by, 0) if by else block
                input_three[s, (x + k) * CY : (x + k + 1) * CY, :] = moved[
                    SIDE : SIDE + CY
                ].astype(BF)
    decode = decode_ref[...]
    source = rows_of(input_three, CY)
    size = decode.shape[0]

    def last_rows(x, count):
        own = own_ref[x * CY : (x + count) * CY, :].astype(F32)
        value = conv(source, band_ref, bias_ref, 2, x, count) + own
        flow = dot(decode, value.astype(BF), NT)
        top = flow.astype(BF)
        rest = (flow - top.astype(F32)).astype(BF)
        for k in range(count // 2):
            pair = x // 2 + k
            lanes = slice(k * LO, (k + 1) * LO)
            table[pair * size : (pair + 1) * size, :] = top[:, lanes]
            table[(CX // 2 + pair) * size : (CX // 2 + pair + 1) * size, :] = rest[:, lanes]

    steps = (end_rows, inner_rows, last_rows)
    for step, x, count in ORDER:
        steps[step](x, count)
    for copy in copies:
        copy.wait()
    chunk = CHUNK
    feat_dim, stay = feat_ref.shape
    eye = jnp.where(
        lax.broadcasted_iota(jnp.int32, (feat_dim, feat_dim), 0)
        == lax.broadcasted_iota(jnp.int32, (feat_dim, feat_dim), 1),
        1.0,
        0.0,
    ).astype(BF)
    weight = dot(eye, self_ref[...], NT)

    def staying(step):
        at = aligned(step * chunk, chunk)
        high, low = cell_codes(slot_ref[:, at])
        rows = pick_rows(
            table[...], feat_ref[:, at], high.astype(F32), low.astype(F32).astype(BF), weight
        )
        for k in range(3):
            out_ref[k, :, at] = rows[k]

    repeat(stay // chunk, staying)

    def arrived(step):
        at = aligned(step * chunk, chunk)
        block = held_ref[:, at]
        rows = pick_rows(
            table[...],
            block[:feat_dim],
            block[feat_dim : feat_dim + 1].astype(F32),
            block[feat_dim + 1 : feat_dim + 2],
            weight,
        )
        to = aligned(stay + step * chunk, chunk)
        for k in range(3):
            out_ref[k, :, to] = rows[k]

    repeat(held_ref.shape[1] // chunk, arrived)


def on_device(
    stay_feats,
    stay_slots,
    move_feats,
    move_slots,
    move_counts,
    encoder,
    conv_weights,
    conv_biases,
    decoder,
    self_weight,
):
    feat_dim = stay_feats.shape[0]
    stay = stay_feats.shape[3]
    cap = move_feats.shape[4]
    chans = encoder.shape[0]
    own_feats = stay_feats.reshape(feat_dim, stay)
    own_slots = stay_slots.reshape(1, stay)

    width = feat_dim + 2
    west, east, middle = call(
        pack_kernel,
        "pack",
        [hbm()] * 3,
        [
            (((3 * width * cap // 128, 128), BF), vmem()),
            (((3 * width * cap // 128, 128), BF), vmem()),
            (((2 * width * cap // 128, 128), BF), vmem()),
        ],
        [
            pltpu.VMEM((feat_dim, 8, cap), BF),
            pltpu.VMEM((8, cap), jnp.int32),
            pltpu.SMEM((8,), jnp.int32),
            pltpu.SemaphoreType.DMA((3,)),
        ],
        1 << 20,
        4,
    )(
        in_hbm(move_feats.reshape(feat_dim, 8, cap)),
        in_hbm(move_slots.reshape(8, cap)),
        in_hbm(move_counts.reshape(8)),
    )
    west, east = exchanged(east, west, "gx")
    sums = (HI * (feat_dim + 1), LO)
    (part,) = call(
        stay_kernel,
        "stay",
        [hbm()] * 2,
        [((sums, F32), vmem())],
        [
            pltpu.VMEM((feat_dim, stay), BF),
            pltpu.VMEM((1, stay), jnp.int32),
            pltpu.SemaphoreType.DMA((2,)),
        ],
        5 << 30,
        8,
    )(in_hbm(own_feats), in_hbm(own_slots))
    west, east, part = lax.optimization_barrier((west, east, part))
    step = width * cap // 128

    def joined(place, inner):
        pieces = ((west, place), (middle, inner), (east, place))
        return jnp.concatenate([ref[k * step : (k + 1) * step] for ref, k in pieces], 0)

    down = passed_along(joined(0, 0), "gy", -1)
    up = passed_along(joined(2, 1), "gy", 1)
    wide = Z * chans
    lanes = Z * feat_dim
    mean, first, last, held = call(
        mean_kernel,
        "mean",
        [vmem()] * 5,
        [
            (((CX * CY, lanes), BF), vmem()),
            (((HALO * CY, lanes), BF), vmem()),
            (((HALO * CY, lanes), BF), vmem()),
            (((width, 8 * cap), BF), vmem()),
        ],
        [pltpu.VMEM(sums, F32)],
        3 << 30,
        8,
    )(west, east, down, up, part)
    after, before = exchanged(last, first, "gx")

    def edge(start):
        blocks = [
            value.reshape(-1, CY, lanes)[:, start : start + SIDE] for value in (before, mean, after)
        ]
        return jnp.concatenate(blocks, 0).reshape((CX + 2 * HALO) * SIDE, lanes)

    low, high = edge(0), edge(CY - SIDE)
    above = passed_along(low, "gy", -1)
    below = passed_along(high, "gy", 1)
    biases = jnp.tile(conv_biases, (1, Z))
    rows = CX + 2 * HALO
    taken, own, band, spread, decode = call(
        core_kernel,
        "core",
        [vmem()] * 5,
        [
            (((3, (CX - 2) * PITCH, wide), BF), vmem()),
            (((CX * CY, wide), BF), vmem()),
            (((3, wide, 9 * wide), BF), vmem()),
            (((wide, lanes), BF), vmem()),
            (((3 * Z, wide), BF), vmem()),
        ],
        [pltpu.VMEM((3, CX * CY, wide), BF)],
        2 << 30,
        GRANT,
    )(mean, conv_weights, encoder, biases, decoder)
    (outer,) = call(
        outer_kernel,
        "outer",
        [vmem()] * 6,
        [(((3, 2 * HALO * PITCH, wide), BF), vmem())],
        [pltpu.VMEM((3, (4 * HALO - 2) * CY, wide), BF)],
        2 << 30,
        GRANT,
    )(own, before, after, band, spread, biases)
    (out,) = call(
        pick_kernel,
        "pick",
        [vmem()] * 11 + [hbm()] * 2 + [vmem()] * 2,
        [(((3, 1, stay + 8 * cap), F32), vmem())],
        [
            pltpu.VMEM((3, rows * STRIP, wide), BF),
            pltpu.VMEM((3, (rows - 2) * STRIP, wide), BF),
            pltpu.VMEM((3, (rows - 4) * CY, wide), BF),
            pltpu.VMEM((2 * CX // 2 * 3 * Z, LO), BF),
            pltpu.VMEM((feat_dim, stay), BF),
            pltpu.VMEM((1, stay), jnp.int32),
            pltpu.SemaphoreType.DMA((2,)),
        ],
        8 << 30,
        GRANT,
    )(
        taken,
        outer,
        own,
        below,
        low,
        high,
        above,
        band,
        spread,
        biases,
        decode,
        in_hbm(own_feats),
        in_hbm(own_slots),
        held,
        self_weight,
    )
    return out.reshape(3, 1, 1, stay + 8 * cap)


def solution(mesh):
    placed = (
        P(None, "gx", "gy", "groups"),
        P("gx", "gy", "groups"),
        P(None, "gx", "gy", None, "groups"),
        P("gx", "gy", None, "groups"),
        P("gx", "gy", "groups"),
        P(),
        P(),
        P(),
        P(),
        P(),
    )
    return jax.shard_map(
        on_device,
        mesh=mesh,
        in_specs=placed,
        out_specs=P(None, "gx", "gy", "groups"),
        check_vma=False,
    )
```

```python
import functools

import jax
import jax.numpy as jnp
from jax import lax
from jax.experimental import pallas as pl
from jax.experimental.pallas import tpu as pltpu
from jax.sharding import PartitionSpec as P

Z = 8
CX = 8
CY = 128
CELLS = Z * CX * CY
LO = 2 * CY
HI = CELLS // LO
DEAD = 2 * HI
HALO = 3
SIDE = 8
PITCH = CY + 2 * SIDE
KEPT = SIDE // 2
STRIP = 4 * SIDE
BF = jnp.bfloat16
F32 = jnp.float32
NT = (((1,), (1,)), ((), ()))
NN = (((1,), (0,)), ((), ()))


CHUNK = 1024
GRANT = 24
CORE_PARTS = ((0, 3), (3, 3))
ORDER = (
    (0, 0, 4),
    (0, 4, 4),
    (1, 0, 3),
    (0, 8, 4),
    (1, 3, 3),
    (2, 0, 2),
    (1, 6, 2),
    (2, 2, 2),
    (1, 8, 2),
    (2, 4, 2),
    (2, 6, 2),
)


def repeat(count, body):
    for step in range(count):
        body(step)


def aligned(start, length):
    return slice(start, start + length)


def cell_codes(slots):
    cell = slots & (CELLS - 1)
    low = cell & (LO - 1)
    zx = cell // LO
    return (zx & (CX // 2 - 1)) * Z + zx // (CX // 2), low


def passed_along(x, axis, by):
    length = lax.axis_size(axis)
    return lax.ppermute(x, axis, [(i, (i + by) % length) for i in range(length)])


def dot(a, b, dims=NN):
    return lax.dot_general(a, b, dims, preferred_element_type=F32)


def vmem():
    return pl.BlockSpec(memory_space=pltpu.VMEM)


def hbm():
    return pl.BlockSpec(memory_space=pltpu.HBM)


def in_hbm(x):
    return pltpu.with_memory_space_constraint(x, pltpu.HBM)


def call(kernel, name, ins, outs, scratch, flops, mib):
    return pl.pallas_call(
        kernel,
        name=name,
        out_shape=[jax.ShapeDtypeStruct(*shape) for shape, _ in outs],
        in_specs=ins,
        out_specs=[spec for _, spec in outs],
        scratch_shapes=scratch,
        cost_estimate=pl.CostEstimate(flops=flops, bytes_accessed=1 << 20, transcendentals=0),
        compiler_params=pltpu.CompilerParams(vmem_limit_bytes=mib << 20),
    )


def onehot(code, count):
    rows = lax.broadcasted_iota(jnp.int32, (count, code.shape[1]), 0).astype(F32).astype(BF)
    same = rows == jnp.broadcast_to(code, rows.shape)
    return jnp.where(same, jnp.ones_like(rows), jnp.zeros_like(rows))


def scatter_part(feats, high, low):
    spread = jnp.broadcast_to(high, feats.shape)
    zero = jnp.zeros_like(feats)
    parts = [jnp.where(spread == jnp.asarray(h, BF), feats, zero) for h in range(HI)]
    parts.append(onehot(high, HI))
    return dot(jnp.concatenate(parts, 0), onehot(low, LO), NT)


def pack_kernel(
    feat_in, slot_in, count_in, west_ref, east_ref, middle_ref, feat_ref, slot_ref, count_ref, sems
):
    pairs = ((count_in, count_ref), (slot_in, slot_ref), (feat_in, feat_ref))
    copies = [pltpu.make_async_copy(a, b, sems.at[k]) for k, (a, b) in enumerate(pairs)]
    for copy in copies:
        copy.start()
    for copy in copies:
        copy.wait()
    feat_dim, buckets, cap = feat_ref.shape
    turned = jnp.swapaxes(feat_ref[...].astype(F32), 0, 1)
    high, low = cell_codes(slot_ref[...])
    lane = lax.broadcasted_iota(jnp.int32, (1, cap), 1)
    high = high.astype(F32)
    low = low.astype(F32)
    blocks = cap // 128
    step = (feat_dim + 2) * blocks
    for out_ref, start, end in ((west_ref, 0, 3), (middle_ref, 3, 5), (east_ref, 5, buckets)):
        for bucket in range(start, end):
            code = jnp.where(
                lane < count_ref[bucket], high[bucket : bucket + 1], jnp.full((1, cap), DEAD, F32)
            )
            base = (bucket - start) * step
            pieces = []
            for value in (turned[bucket], code, low[bucket : bucket + 1]):
                pieces += [value[:, k * 128 : (k + 1) * 128] for k in range(blocks)]
            out_ref[base : base + step, :] = jnp.concatenate(pieces, 0).astype(BF)


def stay_kernel(feat_in, slot_in, sum_ref, feat_ref, slot_ref, sems):
    copies = [
        pltpu.make_async_copy(slot_in, slot_ref, sems.at[0]),
        pltpu.make_async_copy(feat_in, feat_ref, sems.at[1]),
    ]
    for copy in copies:
        copy.start()
    for copy in copies:
        copy.wait()
    chunk = CHUNK
    for step in range(feat_ref.shape[1] // chunk):
        at = aligned(step * chunk, chunk)
        high, low = cell_codes(slot_ref[:, at])
        part = scatter_part(
            feat_ref[:, at], high.astype(F32).astype(BF), low.astype(F32).astype(BF)
        )
        sum_ref[...] = sum_ref[...] + part if step else part


def tiled_rows(small, count):
    width = small.shape[1]
    pick = lax.broadcasted_iota(jnp.int32, (width, count * width), 0)
    column = lax.broadcasted_iota(jnp.int32, (width, count * width), 1) % width
    return dot(small, jnp.where(pick == column, 1.0, 0.0).astype(BF))


def build_spread(encoder):
    chans, feat_dim = encoder.shape
    tiled = tiled_rows(encoder, Z)
    group = lax.broadcasted_iota(jnp.int32, tiled.shape, 1) // feat_dim
    return jnp.concatenate([jnp.where(group == layer, tiled, 0.0) for layer in range(Z)], 0).astype(
        BF
    )


def build_band(weight_ref, layer, band_ref):
    _, chans, width = weight_ref.shape
    taps = 9
    per = 128 // chans
    lane = lax.broadcasted_iota(jnp.int32, (chans, 128), 1) // chans
    weight = weight_ref[layer].astype(F32)
    turned = []
    for start in range(0, width, 128):
        source = weight[:, start : start + 128]
        if source.shape[1] < 128:
            source = jnp.concatenate([source, jnp.zeros((chans, 128 - source.shape[1]), F32)], 1)
        turned.append(
            [(source if k == 0 else pltpu.roll(source, k * chans, 1)).astype(BF) for k in range(per)]
        )
    for out_z in range(Z):
        for tap in range(taps):
            for part in range(Z // per):
                tile = jnp.zeros((chans, 128), BF)
                for depth in range(3):
                    in_z = out_z + depth - 1
                    if in_z < 0 or in_z >= Z or in_z // per != part:
                        continue
                    index = depth * taps + tap
                    moved = turned[index // per][(in_z - index) % per]
                    tile = jnp.where(lane == in_z % per, moved, tile)
                lanes = tap * Z * chans + part * 128
                band_ref[layer, out_z * chans : (out_z + 1) * chans, lanes : lanes + 128] = tile


def unpacked(ref, which, feat_dim, blocks):
    step = (feat_dim + 2) * blocks
    block = ref[which * step : (which + 1) * step, :].astype(F32)
    feats = jnp.concatenate([block[k * feat_dim : (k + 1) * feat_dim] for k in range(blocks)], 1)
    codes = block[blocks * feat_dim :]
    pair = [
        jnp.concatenate([codes[j * blocks + k][None] for k in range(blocks)], 1) for j in range(2)
    ]
    return feats.astype(BF), jnp.concatenate(pair, 0).astype(BF)


def near_kernel(west_ref, east_ref, part_ref, sum_ref, held_ref):
    cap = held_ref.shape[1] // 2
    feat_dim = held_ref.shape[0] - 2
    for place, ref in enumerate((west_ref, east_ref)):
        feats, codes = unpacked(ref, 1, feat_dim, cap // 128)
        at = slice(place * cap, (place + 1) * cap)
        held_ref[:feat_dim, at] = feats
        held_ref[feat_dim:, at] = codes
    rows = held_ref[...]
    sum_ref[...] = part_ref[...] + scatter_part(
        rows[:feat_dim], rows[feat_dim : feat_dim + 1], rows[feat_dim + 1 : feat_dim + 2]
    )


def mean_kernel(
    near_ref, down_ref, up_ref, part_ref, mean_ref, first_ref, last_ref, held_ref, total
):
    cap = held_ref.shape[1] // 8
    feat_dim = held_ref.shape[0] - 2
    held_ref[:, cap : 2 * cap] = near_ref[:, :cap]
    held_ref[:, 6 * cap : 7 * cap] = near_ref[:, cap:]
    order = ((down_ref, 0, 0), (up_ref, 0, 2), (down_ref, 1, 3))
    order += ((up_ref, 1, 4), (down_ref, 2, 5), (up_ref, 2, 7))
    for ref, which, place in order:
        feats, codes = unpacked(ref, which, feat_dim, cap // 128)
        at = slice(place * cap, (place + 1) * cap)
        held_ref[:feat_dim, at] = feats
        held_ref[feat_dim:, at] = codes
    for k, (place, count) in enumerate(((0, 1), (2, 2), (4, 2), (7, 1))):
        rows = held_ref[:, place * cap : (place + count) * cap]
        part = scatter_part(
            rows[:feat_dim], rows[feat_dim : feat_dim + 1], rows[feat_dim + 1 : feat_dim + 2]
        )
        total[...] = (total[...] if k else part_ref[...]) + part

    inverse = 1.0 / jnp.maximum(total[HI * feat_dim :, :], 1.0)
    for pair in range(CX // 2):
        blocks = []
        for layer in range(Z):
            code = pair * Z + layer
            blocks.append(
                total[code * feat_dim : (code + 1) * feat_dim, :] * inverse[code : code + 1, :]
            )
        block = jnp.concatenate(blocks, 0)
        for odd in range(2):
            x = pair * 2 + odd
            turned = jnp.transpose(block[:, odd * CY : (odd + 1) * CY]).astype(BF)
            mean_ref[x * CY : (x + 1) * CY, :] = turned
            if x < HALO:
                first_ref[x * CY : (x + 1) * CY, :] = turned
            if x >= CX - HALO:
                at = x - (CX - HALO)
                last_ref[at * CY : (at + 1) * CY, :] = turned


def gelu(v):
    inner = 0.7978845608028654 * (v + 0.044715 * (v * v * v))
    return 0.5 * v * (1.0 + jnp.tanh(inner))


def store_shifted(target, start, block):
    rows = block.shape[0]
    for s, by in enumerate((1, 0, rows - 1)):
        moved = pltpu.roll(block, by, 0) if by else block
        target[s, start : start + rows, :] = moved.astype(BF)


def rows_of(source, pitch):
    return lambda s, x, count: source[s, x * pitch : (x + count) * pitch, :]


def conv(pick, band_ref, bias_ref, layer, x, count):
    pieces = [pick(s, x + q, count) for q in range(3) for s in range(3)]
    return dot(jnp.concatenate(pieces, 1), band_ref[layer], NT) + bias_ref[layer : layer + 1, :]


def hidden(pick, band_ref, bias_ref, layer, target, parts, pitch, base=0):
    for x, count in parts:
        value = gelu(conv(pick, band_ref, bias_ref, layer, x, count))
        store_shifted(target, (x - base) * pitch, value.astype(BF).astype(F32))


def build_decode(decoder):
    chans = decoder.shape[1]
    tiled = tiled_rows(decoder, Z)
    group = lax.broadcasted_iota(jnp.int32, (Z, Z * chans), 1) // chans
    level = lax.broadcasted_iota(jnp.int32, (Z, Z * chans), 0)
    return jnp.concatenate(
        [jnp.where(group == level, tiled[k : k + 1, :], 0.0) for k in range(3)], 0
    ).astype(BF)


def store_padded(target, x, value):
    side = jnp.zeros((SIDE, value.shape[1]), F32)
    for k in range(value.shape[0] // CY):
        block = jnp.concatenate([side, value[k * CY : (k + 1) * CY], side], 0)
        store_shifted(target, (x + k) * PITCH, block)


def core_kernel(
    mean_ref,
    weight_ref,
    encoder_ref,
    bias_ref,
    decoder_ref,
    middle_ref,
    own_ref,
    band_ref,
    spread_ref,
    decode_ref,
    input_one,
):
    spread = build_spread(encoder_ref[...])
    spread_ref[...] = spread
    decode_ref[...] = build_decode(decoder_ref[...])
    inside = dot(mean_ref[...], spread, NT).astype(BF)
    own_ref[...] = inside
    store_shifted(input_one, 0, inside.astype(F32))
    build_band(weight_ref, 0, band_ref)
    source = rows_of(input_one, CY)
    for x, count in CORE_PARTS:
        value = gelu(conv(source, band_ref, bias_ref, 0, x, count))
        store_padded(middle_ref, x, value.astype(BF).astype(F32))
    build_band(weight_ref, 1, band_ref)
    build_band(weight_ref, 2, band_ref)


def outer_kernel(
    own_ref, before_ref, after_ref, band_ref, spread_ref, bias_ref, outer_ref, input_one
):
    spread = spread_ref[...]
    near = (HALO - 1) * CY
    first = dot(before_ref[...], spread, NT).astype(BF).astype(F32)
    last = dot(after_ref[...], spread, NT).astype(BF).astype(F32)
    low = jnp.concatenate([first, own_ref[:near].astype(F32)], 0)
    high = jnp.concatenate([own_ref[CX * CY - near :].astype(F32), last], 0)
    store_shifted(input_one, 0, low)
    store_shifted(input_one, low.shape[0], high)
    source = rows_of(input_one, CY)
    for side in range(2):
        x = side * (2 * HALO - 1)
        value = gelu(conv(source, band_ref, bias_ref, 0, x, HALO))
        store_padded(outer_ref, side * HALO, value.astype(BF).astype(F32))


def pick_rows(table, feats, high, low, self_weight):
    count = feats.shape[1]
    both = dot(table, onehot(low, LO))
    half = both.shape[0] // 2
    values = both[:half] + both[half:]
    level = lax.broadcasted_iota(jnp.int32, (Z, count), 0).astype(F32)
    spread = jnp.broadcast_to(high, (Z, count))
    masks = [spread == (level + float(pair * Z)) for pair in range(CX // 2)]
    live = high < float(DEAD)
    wide = feats.astype(F32)
    rows = []
    for k in range(3):
        total = jnp.zeros((Z, count), F32)
        for pair in range(CX // 2):
            at = (pair * 3 + k) * Z
            total = total + jnp.where(masks[pair], values[at : at + Z], 0.0)
        for part in range(feats.shape[0] // Z):
            part_rows = slice(part * Z, (part + 1) * Z)
            total = total + wide[part_rows] * self_weight[part_rows, k : k + 1]
        rows.append(jnp.where(live, jnp.sum(total, 0, keepdims=True), 0.0))
    return rows


def pick_kernel(
    middle_ref,
    outer_ref,
    own_ref,
    below_ref,
    low_ref,
    high_ref,
    above_ref,
    band_ref,
    spread_ref,
    bias_ref,
    decode_ref,
    feat_in,
    slot_in,
    held_ref,
    self_ref,
    out_ref,
    strip_ref,
    ends_ref,
    input_three,
    table,
    feat_ref,
    slot_ref,
    sems,
):
    copies = [
        pltpu.make_async_copy(slot_in, slot_ref, sems.at[0]),
        pltpu.make_async_copy(feat_in, feat_ref, sems.at[1]),
    ]
    for copy in copies:
        copy.start()
    spread = spread_ref[...]
    sides = [
        dot(ref[...], spread, NT).astype(BF).astype(F32)
        for ref in (below_ref, low_ref, high_ref, above_ref)
    ]
    rows = CX + 2 * HALO
    strips = jnp.concatenate(
        [side[x * SIDE : (x + 1) * SIDE] for x in range(rows) for side in sides], 0
    )
    store_shifted(strip_ref, 0, strips)

    def end_rows(x, count):
        value = gelu(conv(rows_of(strip_ref, STRIP), band_ref, bias_ref, 0, x, count))
        store_shifted(ends_ref, x * STRIP, value.astype(BF).astype(F32))

    wide = own_ref.shape[1]
    half = STRIP // 2
    row = lax.broadcasted_iota(jnp.int32, (half, wide), 0)

    def mixed(s, x, count):
        blocks = []
        for at in range(x, x + count):
            if at < HALO:
                ref, base = outer_ref, at
            elif at < HALO + CX - 2:
                ref, base = middle_ref, at - HALO
            else:
                ref, base = outer_ref, at - (CX - 2)
            base = base * PITCH
            low = ends_ref[s, at * STRIP : at * STRIP + half, :]
            high = ends_ref[s, at * STRIP + half : (at + 1) * STRIP, :]
            blocks.append(jnp.where(row < half - KEPT, low, ref[s, base : base + half, :]))
            blocks.append(ref[s, base + half : base + PITCH - half, :])
            blocks.append(
                jnp.where(row >= KEPT, high, ref[s, base + PITCH - half : base + PITCH, :])
            )
        return jnp.concatenate(blocks, 0)

    def inner_rows(x, count):
        value = gelu(conv(mixed, band_ref, bias_ref, 1, x, count)).astype(BF).astype(F32)
        for k in range(count):
            block = value[k * PITCH : (k + 1) * PITCH]
            for s, by in enumerate((1, 0, PITCH - 1)):
                moved = pltpu.roll(block, by, 0) if by else block
                input_three[s, (x + k) * CY : (x + k + 1) * CY, :] = moved[
                    SIDE : SIDE + CY
                ].astype(BF)
    decode = decode_ref[...]
    source = rows_of(input_three, CY)
    size = decode.shape[0]

    def last_rows(x, count):
        own = own_ref[x * CY : (x + count) * CY, :].astype(F32)
        value = conv(source, band_ref, bias_ref, 2, x, count) + own
        flow = dot(decode, value.astype(BF), NT)
        top = flow.astype(BF)
        rest = (flow - top.astype(F32)).astype(BF)
        for k in range(count // 2):
            pair = x // 2 + k
            lanes = slice(k * LO, (k + 1) * LO)
            table[pair * size : (pair + 1) * size, :] = top[:, lanes]
            table[(CX // 2 + pair) * size : (CX // 2 + pair + 1) * size, :] = rest[:, lanes]

    steps = (end_rows, inner_rows, last_rows)
    for step, x, count in ORDER:
        steps[step](x, count)
    for copy in copies:
        copy.wait()
    chunk = CHUNK
    feat_dim, stay = feat_ref.shape
    eye = jnp.where(
        lax.broadcasted_iota(jnp.int32, (feat_dim, feat_dim), 0)
        == lax.broadcasted_iota(jnp.int32, (feat_dim, feat_dim), 1),
        1.0,
        0.0,
    ).astype(BF)
    weight = dot(eye, self_ref[...], NT)

    def staying(step):
        at = aligned(step * chunk, chunk)
        high, low = cell_codes(slot_ref[:, at])
        rows = pick_rows(
            table[...], feat_ref[:, at], high.astype(F32), low.astype(F32).astype(BF), weight
        )
        for k in range(3):
            out_ref[k, :, at] = rows[k]

    repeat(stay // chunk, staying)

    def arrived(step):
        at = aligned(step * chunk, chunk)
        block = held_ref[:, at]
        rows = pick_rows(
            table[...],
            block[:feat_dim],
            block[feat_dim : feat_dim + 1].astype(F32),
            block[feat_dim + 1 : feat_dim + 2],
            weight,
        )
        to = aligned(stay + step * chunk, chunk)
        for k in range(3):
            out_ref[k, :, to] = rows[k]

    repeat(held_ref.shape[1] // chunk, arrived)


def on_device(
    stay_feats,
    stay_slots,
    move_feats,
    move_slots,
    move_counts,
    encoder,
    conv_weights,
    conv_biases,
    decoder,
    self_weight,
):
    feat_dim = stay_feats.shape[0]
    stay = stay_feats.shape[3]
    cap = move_feats.shape[4]
    chans = encoder.shape[0]
    own_feats = stay_feats.reshape(feat_dim, stay)
    own_slots = stay_slots.reshape(1, stay)

    width = feat_dim + 2
    west, east, middle = call(
        pack_kernel,
        "pack",
        [hbm()] * 3,
        [
            (((3 * width * cap // 128, 128), BF), vmem()),
            (((3 * width * cap // 128, 128), BF), vmem()),
            (((2 * width * cap // 128, 128), BF), vmem()),
        ],
        [
            pltpu.VMEM((feat_dim, 8, cap), BF),
            pltpu.VMEM((8, cap), jnp.int32),
            pltpu.SMEM((8,), jnp.int32),
            pltpu.SemaphoreType.DMA((3,)),
        ],
        1 << 20,
        4,
    )(
        in_hbm(move_feats.reshape(feat_dim, 8, cap)),
        in_hbm(move_slots.reshape(8, cap)),
        in_hbm(move_counts.reshape(8)),
    )
    west = passed_along(west, "gx", -1)
    east = passed_along(east, "gx", 1)
    sums = (HI * (feat_dim + 1), LO)
    (part,) = call(
        stay_kernel,
        "stay",
        [hbm()] * 2,
        [((sums, F32), vmem())],
        [
            pltpu.VMEM((feat_dim, stay), BF),
            pltpu.VMEM((1, stay), jnp.int32),
            pltpu.SemaphoreType.DMA((2,)),
        ],
        5 << 30,
        8,
    )(in_hbm(own_feats), in_hbm(own_slots))
    west, east, part = lax.optimization_barrier((west, east, part))
    step = width * cap // 128

    def joined(place, inner):
        pieces = ((west, place), (middle, inner), (east, place))
        return jnp.concatenate([ref[k * step : (k + 1) * step] for ref, k in pieces], 0)

    down = passed_along(joined(0, 0), "gy", -1)
    up = passed_along(joined(2, 1), "gy", 1)
    wide = Z * chans
    lanes = Z * feat_dim
    part, near = call(
        near_kernel,
        "near",
        [vmem()] * 3,
        [((sums, F32), vmem()), (((width, 2 * cap), BF), vmem())],
        [],
        1 << 30,
        8,
    )(west, east, part)
    mean, first, last, held = call(
        mean_kernel,
        "mean",
        [vmem()] * 4,
        [
            (((CX * CY, lanes), BF), vmem()),
            (((HALO * CY, lanes), BF), vmem()),
            (((HALO * CY, lanes), BF), vmem()),
            (((width, 8 * cap), BF), vmem()),
        ],
        [pltpu.VMEM(sums, F32)],
        3 << 30,
        8,
    )(near, down, up, part)
    after = passed_along(first, "gx", -1)
    before = passed_along(last, "gx", 1)

    def edge(start):
        blocks = [
            value.reshape(-1, CY, lanes)[:, start : start + SIDE] for value in (before, mean, after)
        ]
        return jnp.concatenate(blocks, 0).reshape((CX + 2 * HALO) * SIDE, lanes)

    low, high = edge(0), edge(CY - SIDE)
    above = passed_along(low, "gy", -1)
    below = passed_along(high, "gy", 1)
    biases = jnp.tile(conv_biases, (1, Z))
    rows = CX + 2 * HALO
    taken, own, band, spread, decode = call(
        core_kernel,
        "core",
        [vmem()] * 5,
        [
            (((3, (CX - 2) * PITCH, wide), BF), vmem()),
            (((CX * CY, wide), BF), vmem()),
            (((3, wide, 9 * wide), BF), vmem()),
            (((wide, lanes), BF), vmem()),
            (((3 * Z, wide), BF), vmem()),
        ],
        [pltpu.VMEM((3, CX * CY, wide), BF)],
        2 << 30,
        GRANT,
    )(mean, conv_weights, encoder, biases, decoder)
    (outer,) = call(
        outer_kernel,
        "outer",
        [vmem()] * 6,
        [(((3, 2 * HALO * PITCH, wide), BF), vmem())],
        [pltpu.VMEM((3, (4 * HALO - 2) * CY, wide), BF)],
        2 << 30,
        GRANT,
    )(own, before, after, band, spread, biases)
    (out,) = call(
        pick_kernel,
        "pick",
        [vmem()] * 11 + [hbm()] * 2 + [vmem()] * 2,
        [(((3, 1, stay + 8 * cap), F32), vmem())],
        [
            pltpu.VMEM((3, rows * STRIP, wide), BF),
            pltpu.VMEM((3, (rows - 2) * STRIP, wide), BF),
            pltpu.VMEM((3, (rows - 4) * CY, wide), BF),
            pltpu.VMEM((2 * CX // 2 * 3 * Z, LO), BF),
            pltpu.VMEM((feat_dim, stay), BF),
            pltpu.VMEM((1, stay), jnp.int32),
            pltpu.SemaphoreType.DMA((2,)),
        ],
        8 << 30,
        GRANT,
    )(
        taken,
        outer,
        own,
        below,
        low,
        high,
        above,
        band,
        spread,
        biases,
        decode,
        in_hbm(own_feats),
        in_hbm(own_slots),
        held,
        self_weight,
    )
    return out.reshape(3, 1, 1, stay + 8 * cap)


def solution(mesh):
    placed = (
        P(None, "gx", "gy", "groups"),
        P("gx", "gy", "groups"),
        P(None, "gx", "gy", None, "groups"),
        P("gx", "gy", None, "groups"),
        P("gx", "gy", "groups"),
        P(),
        P(),
        P(),
        P(),
        P(),
    )
    return jax.shard_map(
        on_device,
        mesh=mesh,
        in_specs=placed,
        out_specs=P(None, "gx", "gy", "groups"),
        check_vma=False,
    )
```

```python
import functools

import jax
import jax.numpy as jnp
from jax import lax
from jax.experimental import pallas as pl
from jax.experimental.pallas import tpu as pltpu
from jax.sharding import PartitionSpec as P

Z = 8
CX = 8
CY = 128
CELLS = Z * CX * CY
LO = 2 * CY
HI = CELLS // LO
DEAD = 2 * HI
HALO = 3
SIDE = 8
PITCH = CY + 2 * SIDE
KEPT = SIDE // 2
STRIP = 4 * SIDE
BF = jnp.bfloat16
F32 = jnp.float32
NT = (((1,), (1,)), ((), ()))
NN = (((1,), (0,)), ((), ()))


CHUNK = 1024
GRANT = 24
CORE_PARTS = ((0, 3), (3, 3))
ORDER = (
    (0, 0, 4),
    (0, 4, 4),
    (1, 0, 3),
    (0, 8, 4),
    (1, 3, 3),
    (2, 0, 2),
    (1, 6, 2),
    (2, 2, 2),
    (1, 8, 2),
    (2, 4, 2),
    (2, 6, 2),
)


def repeat(count, body):
    for step in range(count):
        body(step)


def aligned(start, length):
    return slice(start, start + length)


def cell_codes(slots):
    cell = slots & (CELLS - 1)
    low = cell & (LO - 1)
    zx = cell // LO
    return (zx & (CX // 2 - 1)) * Z + zx // (CX // 2), low


def passed_along(x, axis, by):
    length = lax.axis_size(axis)
    return lax.ppermute(x, axis, [(i, (i + by) % length) for i in range(length)])


def dot(a, b, dims=NN):
    return lax.dot_general(a, b, dims, preferred_element_type=F32)


def vmem():
    return pl.BlockSpec(memory_space=pltpu.VMEM)


def hbm():
    return pl.BlockSpec(memory_space=pltpu.HBM)


def in_hbm(x):
    return pltpu.with_memory_space_constraint(x, pltpu.HBM)


def call(kernel, name, ins, outs, scratch, flops, mib):
    return pl.pallas_call(
        kernel,
        name=name,
        out_shape=[jax.ShapeDtypeStruct(*shape) for shape, _ in outs],
        in_specs=ins,
        out_specs=[spec for _, spec in outs],
        scratch_shapes=scratch,
        cost_estimate=pl.CostEstimate(flops=flops, bytes_accessed=1 << 20, transcendentals=0),
        compiler_params=pltpu.CompilerParams(vmem_limit_bytes=mib << 20),
    )


def onehot(code, count):
    rows = lax.broadcasted_iota(jnp.int32, (count, code.shape[1]), 0).astype(F32).astype(BF)
    same = rows == jnp.broadcast_to(code, rows.shape)
    return jnp.where(same, jnp.ones_like(rows), jnp.zeros_like(rows))


def scatter_part(feats, high, low):
    spread = jnp.broadcast_to(high, feats.shape)
    zero = jnp.zeros_like(feats)
    parts = [jnp.where(spread == jnp.asarray(h, BF), feats, zero) for h in range(HI)]
    parts.append(onehot(high, HI))
    return dot(jnp.concatenate(parts, 0), onehot(low, LO), NT)


def pack_kernel(
    feat_in, slot_in, count_in, down_ref, up_ref, middle_ref, feat_ref, slot_ref, count_ref, sems
):
    pairs = ((count_in, count_ref), (slot_in, slot_ref), (feat_in, feat_ref))
    copies = [pltpu.make_async_copy(a, b, sems.at[k]) for k, (a, b) in enumerate(pairs)]
    for copy in copies:
        copy.start()
    for copy in copies:
        copy.wait()
    feat_dim, buckets, cap = feat_ref.shape
    turned = jnp.swapaxes(feat_ref[...].astype(F32), 0, 1)
    high, low = cell_codes(slot_ref[...])
    lane = lax.broadcasted_iota(jnp.int32, (1, cap), 1)
    high = high.astype(F32)
    low = low.astype(F32)
    blocks = cap // 128
    step = (feat_dim + 2) * blocks
    for out_ref, chosen in ((down_ref, (0, 3, 5)), (up_ref, (2, 4, 7)), (middle_ref, (1, 6))):
        for place, bucket in enumerate(chosen):
            code = jnp.where(
                lane < count_ref[bucket], high[bucket : bucket + 1], jnp.full((1, cap), DEAD, F32)
            )
            base = place * step
            pieces = []
            for value in (turned[bucket], code, low[bucket : bucket + 1]):
                pieces += [value[:, k * 128 : (k + 1) * 128] for k in range(blocks)]
            out_ref[base : base + step, :] = jnp.concatenate(pieces, 0).astype(BF)


def stay_kernel(feat_in, slot_in, sum_ref, feat_ref, slot_ref, sems):
    copies = [
        pltpu.make_async_copy(slot_in, slot_ref, sems.at[0]),
        pltpu.make_async_copy(feat_in, feat_ref, sems.at[1]),
    ]
    for copy in copies:
        copy.start()
    for copy in copies:
        copy.wait()
    chunk = CHUNK
    for step in range(feat_ref.shape[1] // chunk):
        at = aligned(step * chunk, chunk)
        high, low = cell_codes(slot_ref[:, at])
        part = scatter_part(
            feat_ref[:, at], high.astype(F32).astype(BF), low.astype(F32).astype(BF)
        )
        sum_ref[...] = sum_ref[...] + part if step else part


def tiled_rows(small, count):
    width = small.shape[1]
    pick = lax.broadcasted_iota(jnp.int32, (width, count * width), 0)
    column = lax.broadcasted_iota(jnp.int32, (width, count * width), 1) % width
    return dot(small, jnp.where(pick == column, 1.0, 0.0).astype(BF))


def build_spread(encoder):
    chans, feat_dim = encoder.shape
    tiled = tiled_rows(encoder, Z)
    group = lax.broadcasted_iota(jnp.int32, tiled.shape, 1) // feat_dim
    return jnp.concatenate([jnp.where(group == layer, tiled, 0.0) for layer in range(Z)], 0).astype(
        BF
    )


def build_band(weight_ref, layer, band_ref):
    _, chans, width = weight_ref.shape
    taps = 9
    per = 128 // chans
    lane = lax.broadcasted_iota(jnp.int32, (chans, 128), 1) // chans
    weight = weight_ref[layer].astype(F32)
    turned = []
    for start in range(0, width, 128):
        source = weight[:, start : start + 128]
        if source.shape[1] < 128:
            source = jnp.concatenate([source, jnp.zeros((chans, 128 - source.shape[1]), F32)], 1)
        turned.append(
            [(source if k == 0 else pltpu.roll(source, k * chans, 1)).astype(BF) for k in range(per)]
        )
    for out_z in range(Z):
        for tap in range(taps):
            for part in range(Z // per):
                tile = jnp.zeros((chans, 128), BF)
                for depth in range(3):
                    in_z = out_z + depth - 1
                    if in_z < 0 or in_z >= Z or in_z // per != part:
                        continue
                    index = depth * taps + tap
                    moved = turned[index // per][(in_z - index) % per]
                    tile = jnp.where(lane == in_z % per, moved, tile)
                lanes = tap * Z * chans + part * 128
                band_ref[layer, out_z * chans : (out_z + 1) * chans, lanes : lanes + 128] = tile


def unpacked(ref, which, feat_dim, blocks):
    step = (feat_dim + 2) * blocks
    block = ref[which * step : (which + 1) * step, :].astype(F32)
    feats = jnp.concatenate([block[k * feat_dim : (k + 1) * feat_dim] for k in range(blocks)], 1)
    codes = block[blocks * feat_dim :]
    pair = [
        jnp.concatenate([codes[j * blocks + k][None] for k in range(blocks)], 1) for j in range(2)
    ]
    return feats.astype(BF), jnp.concatenate(pair, 0).astype(BF)


def near_kernel(down_ref, up_ref, part_ref, sum_ref, held_ref):
    cap = held_ref.shape[1] // 2
    feat_dim = held_ref.shape[0] - 2
    for place, ref in enumerate((down_ref, up_ref)):
        feats, codes = unpacked(ref, 1, feat_dim, cap // 128)
        at = slice(place * cap, (place + 1) * cap)
        held_ref[:feat_dim, at] = feats
        held_ref[feat_dim:, at] = codes
    rows = held_ref[...]
    sum_ref[...] = part_ref[...] + scatter_part(
        rows[:feat_dim], rows[feat_dim : feat_dim + 1], rows[feat_dim + 1 : feat_dim + 2]
    )


def mean_kernel(
    near_ref, west_ref, east_ref, part_ref, mean_ref, first_ref, last_ref, held_ref, total
):
    cap = held_ref.shape[1] // 8
    feat_dim = held_ref.shape[0] - 2
    held_ref[:, 3 * cap : 5 * cap] = near_ref[...]
    order = [(west_ref, k, k) for k in range(3)] + [(east_ref, k, 5 + k) for k in range(3)]
    for ref, which, place in order:
        feats, codes = unpacked(ref, which, feat_dim, cap // 128)
        at = slice(place * cap, (place + 1) * cap)
        held_ref[:feat_dim, at] = feats
        held_ref[feat_dim:, at] = codes
    for k, (place, count) in enumerate(((0, 2), (2, 1), (5, 1), (6, 2))):
        rows = held_ref[:, place * cap : (place + count) * cap]
        part = scatter_part(
            rows[:feat_dim], rows[feat_dim : feat_dim + 1], rows[feat_dim + 1 : feat_dim + 2]
        )
        total[...] = (total[...] if k else part_ref[...]) + part

    inverse = 1.0 / jnp.maximum(total[HI * feat_dim :, :], 1.0)
    for pair in range(CX // 2):
        blocks = []
        for layer in range(Z):
            code = pair * Z + layer
            blocks.append(
                total[code * feat_dim : (code + 1) * feat_dim, :] * inverse[code : code + 1, :]
            )
        block = jnp.concatenate(blocks, 0)
        for odd in range(2):
            x = pair * 2 + odd
            turned = jnp.transpose(block[:, odd * CY : (odd + 1) * CY]).astype(BF)
            mean_ref[x * CY : (x + 1) * CY, :] = turned
            if x < HALO:
                first_ref[x * CY : (x + 1) * CY, :] = turned
            if x >= CX - HALO:
                at = x - (CX - HALO)
                last_ref[at * CY : (at + 1) * CY, :] = turned


def gelu(v):
    inner = 0.7978845608028654 * (v + 0.044715 * (v * v * v))
    return 0.5 * v * (1.0 + jnp.tanh(inner))


def store_shifted(target, start, block):
    rows = block.shape[0]
    for s, by in enumerate((1, 0, rows - 1)):
        moved = pltpu.roll(block, by, 0) if by else block
        target[s, start : start + rows, :] = moved.astype(BF)


def rows_of(source, pitch):
    return lambda s, x, count: source[s, x * pitch : (x + count) * pitch, :]


def conv(pick, band_ref, bias_ref, layer, x, count):
    pieces = [pick(s, x + q, count) for q in range(3) for s in range(3)]
    return dot(jnp.concatenate(pieces, 1), band_ref[layer], NT) + bias_ref[layer : layer + 1, :]


def hidden(pick, band_ref, bias_ref, layer, target, parts, pitch, base=0):
    for x, count in parts:
        value = gelu(conv(pick, band_ref, bias_ref, layer, x, count))
        store_shifted(target, (x - base) * pitch, value.astype(BF).astype(F32))


def build_decode(decoder):
    chans = decoder.shape[1]
    tiled = tiled_rows(decoder, Z)
    group = lax.broadcasted_iota(jnp.int32, (Z, Z * chans), 1) // chans
    level = lax.broadcasted_iota(jnp.int32, (Z, Z * chans), 0)
    return jnp.concatenate(
        [jnp.where(group == level, tiled[k : k + 1, :], 0.0) for k in range(3)], 0
    ).astype(BF)


def store_padded(target, x, value):
    side = jnp.zeros((SIDE, value.shape[1]), F32)
    for k in range(value.shape[0] // CY):
        block = jnp.concatenate([side, value[k * CY : (k + 1) * CY], side], 0)
        store_shifted(target, (x + k) * PITCH, block)


def core_kernel(
    mean_ref,
    weight_ref,
    encoder_ref,
    bias_ref,
    decoder_ref,
    middle_ref,
    own_ref,
    band_ref,
    spread_ref,
    decode_ref,
    input_one,
):
    spread = build_spread(encoder_ref[...])
    spread_ref[...] = spread
    decode_ref[...] = build_decode(decoder_ref[...])
    inside = dot(mean_ref[...], spread, NT).astype(BF)
    own_ref[...] = inside
    store_shifted(input_one, 0, inside.astype(F32))
    build_band(weight_ref, 0, band_ref)
    source = rows_of(input_one, CY)
    for x, count in CORE_PARTS:
        value = gelu(conv(source, band_ref, bias_ref, 0, x, count))
        store_padded(middle_ref, x, value.astype(BF).astype(F32))
    build_band(weight_ref, 1, band_ref)
    build_band(weight_ref, 2, band_ref)


def outer_kernel(
    own_ref, before_ref, after_ref, band_ref, spread_ref, bias_ref, outer_ref, input_one
):
    spread = spread_ref[...]
    near = (HALO - 1) * CY
    first = dot(before_ref[...], spread, NT).astype(BF).astype(F32)
    last = dot(after_ref[...], spread, NT).astype(BF).astype(F32)
    low = jnp.concatenate([first, own_ref[:near].astype(F32)], 0)
    high = jnp.concatenate([own_ref[CX * CY - near :].astype(F32), last], 0)
    store_shifted(input_one, 0, low)
    store_shifted(input_one, low.shape[0], high)
    source = rows_of(input_one, CY)
    for side in range(2):
        x = side * (2 * HALO - 1)
        value = gelu(conv(source, band_ref, bias_ref, 0, x, HALO))
        store_padded(outer_ref, side * HALO, value.astype(BF).astype(F32))


def pick_rows(table, feats, high, low, self_weight):
    count = feats.shape[1]
    both = dot(table, onehot(low, LO))
    half = both.shape[0] // 2
    values = both[:half] + both[half:]
    level = lax.broadcasted_iota(jnp.int32, (Z, count), 0).astype(F32)
    spread = jnp.broadcast_to(high, (Z, count))
    masks = [spread == (level + float(pair * Z)) for pair in range(CX // 2)]
    live = high < float(DEAD)
    wide = feats.astype(F32)
    rows = []
    for k in range(3):
        total = jnp.zeros((Z, count), F32)
        for pair in range(CX // 2):
            at = (pair * 3 + k) * Z
            total = total + jnp.where(masks[pair], values[at : at + Z], 0.0)
        for part in range(feats.shape[0] // Z):
            part_rows = slice(part * Z, (part + 1) * Z)
            total = total + wide[part_rows] * self_weight[part_rows, k : k + 1]
        rows.append(jnp.where(live, jnp.sum(total, 0, keepdims=True), 0.0))
    return rows


def pick_kernel(
    middle_ref,
    outer_ref,
    own_ref,
    below_ref,
    low_ref,
    high_ref,
    above_ref,
    band_ref,
    spread_ref,
    bias_ref,
    decode_ref,
    feat_in,
    slot_in,
    held_ref,
    self_ref,
    out_ref,
    strip_ref,
    ends_ref,
    input_three,
    table,
    feat_ref,
    slot_ref,
    sems,
):
    copies = [
        pltpu.make_async_copy(slot_in, slot_ref, sems.at[0]),
        pltpu.make_async_copy(feat_in, feat_ref, sems.at[1]),
    ]
    for copy in copies:
        copy.start()
    spread = spread_ref[...]
    sides = [
        dot(ref[...], spread, NT).astype(BF).astype(F32)
        for ref in (below_ref, low_ref, high_ref, above_ref)
    ]
    rows = CX + 2 * HALO
    strips = jnp.concatenate(
        [side[x * SIDE : (x + 1) * SIDE] for x in range(rows) for side in sides], 0
    )
    store_shifted(strip_ref, 0, strips)

    def end_rows(x, count):
        value = gelu(conv(rows_of(strip_ref, STRIP), band_ref, bias_ref, 0, x, count))
        store_shifted(ends_ref, x * STRIP, value.astype(BF).astype(F32))

    wide = own_ref.shape[1]
    half = STRIP // 2
    row = lax.broadcasted_iota(jnp.int32, (half, wide), 0)

    def mixed(s, x, count):
        blocks = []
        for at in range(x, x + count):
            if at < HALO:
                ref, base = outer_ref, at
            elif at < HALO + CX - 2:
                ref, base = middle_ref, at - HALO
            else:
                ref, base = outer_ref, at - (CX - 2)
            base = base * PITCH
            low = ends_ref[s, at * STRIP : at * STRIP + half, :]
            high = ends_ref[s, at * STRIP + half : (at + 1) * STRIP, :]
            blocks.append(jnp.where(row < half - KEPT, low, ref[s, base : base + half, :]))
            blocks.append(ref[s, base + half : base + PITCH - half, :])
            blocks.append(
                jnp.where(row >= KEPT, high, ref[s, base + PITCH - half : base + PITCH, :])
            )
        return jnp.concatenate(blocks, 0)

    def inner_rows(x, count):
        value = gelu(conv(mixed, band_ref, bias_ref, 1, x, count)).astype(BF).astype(F32)
        for k in range(count):
            block = value[k * PITCH : (k + 1) * PITCH]
            for s, by in enumerate((1, 0, PITCH - 1)):
                moved = pltpu.roll(block, by, 0) if by else block
                input_three[s, (x + k) * CY : (x + k + 1) * CY, :] = moved[
                    SIDE : SIDE + CY
                ].astype(BF)
    decode = decode_ref[...]
    source = rows_of(input_three, CY)
    size = decode.shape[0]

    def last_rows(x, count):
        own = own_ref[x * CY : (x + count) * CY, :].astype(F32)
        value = conv(source, band_ref, bias_ref, 2, x, count) + own
        flow = dot(decode, value.astype(BF), NT)
        top = flow.astype(BF)
        rest = (flow - top.astype(F32)).astype(BF)
        for k in range(count // 2):
            pair = x // 2 + k
            lanes = slice(k * LO, (k + 1) * LO)
            table[pair * size : (pair + 1) * size, :] = top[:, lanes]
            table[(CX // 2 + pair) * size : (CX // 2 + pair + 1) * size, :] = rest[:, lanes]

    steps = (end_rows, inner_rows, last_rows)
    for step, x, count in ORDER:
        steps[step](x, count)
    for copy in copies:
        copy.wait()
    chunk = CHUNK
    feat_dim, stay = feat_ref.shape
    eye = jnp.where(
        lax.broadcasted_iota(jnp.int32, (feat_dim, feat_dim), 0)
        == lax.broadcasted_iota(jnp.int32, (feat_dim, feat_dim), 1),
        1.0,
        0.0,
    ).astype(BF)
    weight = dot(eye, self_ref[...], NT)

    def staying(step):
        at = aligned(step * chunk, chunk)
        high, low = cell_codes(slot_ref[:, at])
        rows = pick_rows(
            table[...], feat_ref[:, at], high.astype(F32), low.astype(F32).astype(BF), weight
        )
        for k in range(3):
            out_ref[k, :, at] = rows[k]

    repeat(stay // chunk, staying)

    def arrived(step):
        at = aligned(step * chunk, chunk)
        block = held_ref[:, at]
        rows = pick_rows(
            table[...],
            block[:feat_dim],
            block[feat_dim : feat_dim + 1].astype(F32),
            block[feat_dim + 1 : feat_dim + 2],
            weight,
        )
        to = aligned(stay + step * chunk, chunk)
        for k in range(3):
            out_ref[k, :, to] = rows[k]

    repeat(held_ref.shape[1] // chunk, arrived)


def on_device(
    stay_feats,
    stay_slots,
    move_feats,
    move_slots,
    move_counts,
    encoder,
    conv_weights,
    conv_biases,
    decoder,
    self_weight,
):
    feat_dim = stay_feats.shape[0]
    stay = stay_feats.shape[3]
    cap = move_feats.shape[4]
    chans = encoder.shape[0]
    own_feats = stay_feats.reshape(feat_dim, stay)
    own_slots = stay_slots.reshape(1, stay)

    width = feat_dim + 2
    down, up, middle = call(
        pack_kernel,
        "pack",
        [hbm()] * 3,
        [
            (((3 * width * cap // 128, 128), BF), vmem()),
            (((3 * width * cap // 128, 128), BF), vmem()),
            (((2 * width * cap // 128, 128), BF), vmem()),
        ],
        [
            pltpu.VMEM((feat_dim, 8, cap), BF),
            pltpu.VMEM((8, cap), jnp.int32),
            pltpu.SMEM((8,), jnp.int32),
            pltpu.SemaphoreType.DMA((3,)),
        ],
        1 << 20,
        4,
    )(
        in_hbm(move_feats.reshape(feat_dim, 8, cap)),
        in_hbm(move_slots.reshape(8, cap)),
        in_hbm(move_counts.reshape(8)),
    )
    down = passed_along(down, "gy", -1)
    up = passed_along(up, "gy", 1)
    sums = (HI * (feat_dim + 1), LO)
    (part,) = call(
        stay_kernel,
        "stay",
        [hbm()] * 2,
        [((sums, F32), vmem())],
        [
            pltpu.VMEM((feat_dim, stay), BF),
            pltpu.VMEM((1, stay), jnp.int32),
            pltpu.SemaphoreType.DMA((2,)),
        ],
        5 << 30,
        8,
    )(in_hbm(own_feats), in_hbm(own_slots))
    down, up, part = lax.optimization_barrier((down, up, part))
    step = width * cap // 128

    def joined(place, inner):
        pieces = ((down, place), (middle, inner), (up, place))
        return jnp.concatenate([ref[k * step : (k + 1) * step] for ref, k in pieces], 0)

    west = passed_along(joined(0, 0), "gx", -1)
    east = passed_along(joined(2, 1), "gx", 1)
    wide = Z * chans
    lanes = Z * feat_dim
    part, near = call(
        near_kernel,
        "near",
        [vmem()] * 3,
        [((sums, F32), vmem()), (((width, 2 * cap), BF), vmem())],
        [],
        1 << 30,
        8,
    )(down, up, part)
    mean, first, last, held = call(
        mean_kernel,
        "mean",
        [vmem()] * 4,
        [
            (((CX * CY, lanes), BF), vmem()),
            (((HALO * CY, lanes), BF), vmem()),
            (((HALO * CY, lanes), BF), vmem()),
            (((width, 8 * cap), BF), vmem()),
        ],
        [pltpu.VMEM(sums, F32)],
        3 << 30,
        8,
    )(near, west, east, part)
    after = passed_along(first, "gx", -1)
    before = passed_along(last, "gx", 1)

    def edge(start):
        blocks = [
            value.reshape(-1, CY, lanes)[:, start : start + SIDE] for value in (before, mean, after)
        ]
        return jnp.concatenate(blocks, 0).reshape((CX + 2 * HALO) * SIDE, lanes)

    low, high = edge(0), edge(CY - SIDE)
    above = passed_along(low, "gy", -1)
    below = passed_along(high, "gy", 1)
    biases = jnp.tile(conv_biases, (1, Z))
    rows = CX + 2 * HALO
    taken, own, band, spread, decode = call(
        core_kernel,
        "core",
        [vmem()] * 5,
        [
            (((3, (CX - 2) * PITCH, wide), BF), vmem()),
            (((CX * CY, wide), BF), vmem()),
            (((3, wide, 9 * wide), BF), vmem()),
            (((wide, lanes), BF), vmem()),
            (((3 * Z, wide), BF), vmem()),
        ],
        [pltpu.VMEM((3, CX * CY, wide), BF)],
        2 << 30,
        GRANT,
    )(mean, conv_weights, encoder, biases, decoder)
    (outer,) = call(
        outer_kernel,
        "outer",
        [vmem()] * 6,
        [(((3, 2 * HALO * PITCH, wide), BF), vmem())],
        [pltpu.VMEM((3, (4 * HALO - 2) * CY, wide), BF)],
        2 << 30,
        GRANT,
    )(own, before, after, band, spread, biases)
    (out,) = call(
        pick_kernel,
        "pick",
        [vmem()] * 11 + [hbm()] * 2 + [vmem()] * 2,
        [(((3, 1, stay + 8 * cap), F32), vmem())],
        [
            pltpu.VMEM((3, rows * STRIP, wide), BF),
            pltpu.VMEM((3, (rows - 2) * STRIP, wide), BF),
            pltpu.VMEM((3, (rows - 4) * CY, wide), BF),
            pltpu.VMEM((2 * CX // 2 * 3 * Z, LO), BF),
            pltpu.VMEM((feat_dim, stay), BF),
            pltpu.VMEM((1, stay), jnp.int32),
            pltpu.SemaphoreType.DMA((2,)),
        ],
        8 << 30,
        GRANT,
    )(
        taken,
        outer,
        own,
        below,
        low,
        high,
        above,
        band,
        spread,
        biases,
        decode,
        in_hbm(own_feats),
        in_hbm(own_slots),
        held,
        self_weight,
    )
    return out.reshape(3, 1, 1, stay + 8 * cap)


def solution(mesh):
    placed = (
        P(None, "gx", "gy", "groups"),
        P("gx", "gy", "groups"),
        P(None, "gx", "gy", None, "groups"),
        P("gx", "gy", None, "groups"),
        P("gx", "gy", "groups"),
        P(),
        P(),
        P(),
        P(),
        P(),
    )
    return jax.shard_map(
        on_device,
        mesh=mesh,
        in_specs=placed,
        out_specs=P(None, "gx", "gy", "groups"),
        check_vma=False,
    )
```

```python
import functools

import jax
import jax.numpy as jnp
from jax import lax
from jax.experimental import pallas as pl
from jax.experimental.pallas import tpu as pltpu
from jax.sharding import PartitionSpec as P

Z = 8
CX = 8
CY = 128
CELLS = Z * CX * CY
LO = 2 * CY
HI = CELLS // LO
DEAD = 2 * HI
HALO = 3
SIDE = 8
PITCH = CY + 2 * SIDE
KEPT = SIDE // 2
STRIP = 4 * SIDE
BF = jnp.bfloat16
F32 = jnp.float32
NT = (((1,), (1,)), ((), ()))
NN = (((1,), (0,)), ((), ()))


CHUNK = 1024
GRANT = 24
CORE_PARTS = ((0, 3), (3, 3))
ORDER = (
    (0, 0, 4),
    (0, 4, 4),
    (1, 0, 3),
    (0, 8, 4),
    (1, 3, 3),
    (2, 0, 2),
    (1, 6, 2),
    (2, 2, 2),
    (1, 8, 2),
    (2, 4, 2),
    (2, 6, 2),
)


def repeat(count, body):
    for step in range(count):
        body(step)


def aligned(start, length):
    return slice(start, start + length)


def cell_codes(slots):
    cell = slots & (CELLS - 1)
    low = cell & (LO - 1)
    zx = cell // LO
    return (zx & (CX // 2 - 1)) * Z + zx // (CX // 2), low


def passed_along(x, axis, by):
    length = lax.axis_size(axis)
    return lax.ppermute(x, axis, [(i, (i + by) % length) for i in range(length)])


def exchanged(up, down, axis):
    length = lax.axis_size(axis)
    if length % 2:
        return passed_along(down, axis, -1), passed_along(up, axis, 1)
    even = lax.axis_index(axis) % 2 == 0
    within = [(i, i + 1 - 2 * (i % 2)) for i in range(length)]
    between = [(i, (i - 1 + 2 * (i % 2)) % length) for i in range(length)]
    inner = lax.ppermute(jnp.where(even, up, down), axis, within)
    outer = lax.ppermute(jnp.where(even, down, up), axis, between)
    return jnp.where(even, inner, outer), jnp.where(even, outer, inner)


def dot(a, b, dims=NN):
    return lax.dot_general(a, b, dims, preferred_element_type=F32)


def vmem():
    return pl.BlockSpec(memory_space=pltpu.VMEM)


def hbm():
    return pl.BlockSpec(memory_space=pltpu.HBM)


def in_hbm(x):
    return pltpu.with_memory_space_constraint(x, pltpu.HBM)


def call(kernel, name, ins, outs, scratch, flops, mib):
    return pl.pallas_call(
        kernel,
        name=name,
        out_shape=[jax.ShapeDtypeStruct(*shape) for shape, _ in outs],
        in_specs=ins,
        out_specs=[spec for _, spec in outs],
        scratch_shapes=scratch,
        cost_estimate=pl.CostEstimate(flops=flops, bytes_accessed=1 << 20, transcendentals=0),
        compiler_params=pltpu.CompilerParams(vmem_limit_bytes=mib << 20),
    )


def onehot(code, count):
    rows = lax.broadcasted_iota(jnp.int32, (count, code.shape[1]), 0).astype(F32).astype(BF)
    same = rows == jnp.broadcast_to(code, rows.shape)
    return jnp.where(same, jnp.ones_like(rows), jnp.zeros_like(rows))


def scatter_part(feats, high, low):
    spread = jnp.broadcast_to(high, feats.shape)
    zero = jnp.zeros_like(feats)
    parts = [jnp.where(spread == jnp.asarray(h, BF), feats, zero) for h in range(HI)]
    parts.append(onehot(high, HI))
    return dot(jnp.concatenate(parts, 0), onehot(low, LO), NT)


def pack_kernel(
    feat_in, slot_in, count_in, down_ref, up_ref, middle_ref, feat_ref, slot_ref, count_ref, sems
):
    pairs = ((count_in, count_ref), (slot_in, slot_ref), (feat_in, feat_ref))
    copies = [pltpu.make_async_copy(a, b, sems.at[k]) for k, (a, b) in enumerate(pairs)]
    for copy in copies:
        copy.start()
    for copy in copies:
        copy.wait()
    feat_dim, buckets, cap = feat_ref.shape
    turned = jnp.swapaxes(feat_ref[...].astype(F32), 0, 1)
    high, low = cell_codes(slot_ref[...])
    lane = lax.broadcasted_iota(jnp.int32, (1, cap), 1)
    high = high.astype(F32)
    low = low.astype(F32)
    blocks = cap // 128
    step = (feat_dim + 2) * blocks
    for out_ref, chosen in ((down_ref, (0, 3, 5)), (up_ref, (2, 4, 7)), (middle_ref, (1, 6))):
        for place, bucket in enumerate(chosen):
            code = jnp.where(
                lane < count_ref[bucket], high[bucket : bucket + 1], jnp.full((1, cap), DEAD, F32)
            )
            base = place * step
            pieces = []
            for value in (turned[bucket], code, low[bucket : bucket + 1]):
                pieces += [value[:, k * 128 : (k + 1) * 128] for k in range(blocks)]
            out_ref[base : base + step, :] = jnp.concatenate(pieces, 0).astype(BF)


def stay_kernel(feat_in, slot_in, sum_ref, feat_ref, slot_ref, sems):
    copies = [
        pltpu.make_async_copy(slot_in, slot_ref, sems.at[0]),
        pltpu.make_async_copy(feat_in, feat_ref, sems.at[1]),
    ]
    for copy in copies:
        copy.start()
    for copy in copies:
        copy.wait()
    chunk = CHUNK
    for step in range(feat_ref.shape[1] // chunk):
        at = aligned(step * chunk, chunk)
        high, low = cell_codes(slot_ref[:, at])
        part = scatter_part(
            feat_ref[:, at], high.astype(F32).astype(BF), low.astype(F32).astype(BF)
        )
        sum_ref[...] = sum_ref[...] + part if step else part


def tiled_rows(small, count):
    width = small.shape[1]
    pick = lax.broadcasted_iota(jnp.int32, (width, count * width), 0)
    column = lax.broadcasted_iota(jnp.int32, (width, count * width), 1) % width
    return dot(small, jnp.where(pick == column, 1.0, 0.0).astype(BF))


def build_spread(encoder):
    chans, feat_dim = encoder.shape
    tiled = tiled_rows(encoder, Z)
    group = lax.broadcasted_iota(jnp.int32, tiled.shape, 1) // feat_dim
    return jnp.concatenate([jnp.where(group == layer, tiled, 0.0) for layer in range(Z)], 0).astype(
        BF
    )


def build_band(weight_ref, layer, band_ref):
    _, chans, width = weight_ref.shape
    taps = 9
    per = 128 // chans
    lane = lax.broadcasted_iota(jnp.int32, (chans, 128), 1) // chans
    weight = weight_ref[layer].astype(F32)
    turned = []
    for start in range(0, width, 128):
        source = weight[:, start : start + 128]
        if source.shape[1] < 128:
            source = jnp.concatenate([source, jnp.zeros((chans, 128 - source.shape[1]), F32)], 1)
        turned.append(
            [(source if k == 0 else pltpu.roll(source, k * chans, 1)).astype(BF) for k in range(per)]
        )
    for out_z in range(Z):
        for tap in range(taps):
            for part in range(Z // per):
                tile = jnp.zeros((chans, 128), BF)
                for depth in range(3):
                    in_z = out_z + depth - 1
                    if in_z < 0 or in_z >= Z or in_z // per != part:
                        continue
                    index = depth * taps + tap
                    moved = turned[index // per][(in_z - index) % per]
                    tile = jnp.where(lane == in_z % per, moved, tile)
                lanes = tap * Z * chans + part * 128
                band_ref[layer, out_z * chans : (out_z + 1) * chans, lanes : lanes + 128] = tile


def unpacked(ref, which, feat_dim, blocks):
    step = (feat_dim + 2) * blocks
    block = ref[which * step : (which + 1) * step, :].astype(F32)
    feats = jnp.concatenate([block[k * feat_dim : (k + 1) * feat_dim] for k in range(blocks)], 1)
    codes = block[blocks * feat_dim :]
    pair = [
        jnp.concatenate([codes[j * blocks + k][None] for k in range(blocks)], 1) for j in range(2)
    ]
    return feats.astype(BF), jnp.concatenate(pair, 0).astype(BF)


def near_kernel(down_ref, up_ref, part_ref, sum_ref, held_ref):
    cap = held_ref.shape[1] // 2
    feat_dim = held_ref.shape[0] - 2
    for place, ref in enumerate((down_ref, up_ref)):
        feats, codes = unpacked(ref, 1, feat_dim, cap // 128)
        at = slice(place * cap, (place + 1) * cap)
        held_ref[:feat_dim, at] = feats
        held_ref[feat_dim:, at] = codes
    rows = held_ref[...]
    sum_ref[...] = part_ref[...] + scatter_part(
        rows[:feat_dim], rows[feat_dim : feat_dim + 1], rows[feat_dim + 1 : feat_dim + 2]
    )


def mean_kernel(
    near_ref, west_ref, east_ref, part_ref, mean_ref, first_ref, last_ref, held_ref, total
):
    cap = held_ref.shape[1] // 8
    feat_dim = held_ref.shape[0] - 2
    held_ref[:, 3 * cap : 5 * cap] = near_ref[...]
    order = [(west_ref, k, k) for k in range(3)] + [(east_ref, k, 5 + k) for k in range(3)]
    for ref, which, place in order:
        feats, codes = unpacked(ref, which, feat_dim, cap // 128)
        at = slice(place * cap, (place + 1) * cap)
        held_ref[:feat_dim, at] = feats
        held_ref[feat_dim:, at] = codes
    for k, (place, count) in enumerate(((0, 2), (2, 1), (5, 1), (6, 2))):
        rows = held_ref[:, place * cap : (place + count) * cap]
        part = scatter_part(
            rows[:feat_dim], rows[feat_dim : feat_dim + 1], rows[feat_dim + 1 : feat_dim + 2]
        )
        total[...] = (total[...] if k else part_ref[...]) + part

    inverse = 1.0 / jnp.maximum(total[HI * feat_dim :, :], 1.0)
    for pair in range(CX // 2):
        blocks = []
        for layer in range(Z):
            code = pair * Z + layer
            blocks.append(
                total[code * feat_dim : (code + 1) * feat_dim, :] * inverse[code : code + 1, :]
            )
        block = jnp.concatenate(blocks, 0)
        for odd in range(2):
            x = pair * 2 + odd
            turned = jnp.transpose(block[:, odd * CY : (odd + 1) * CY]).astype(BF)
            mean_ref[x * CY : (x + 1) * CY, :] = turned
            if x < HALO:
                first_ref[x * CY : (x + 1) * CY, :] = turned
            if x >= CX - HALO:
                at = x - (CX - HALO)
                last_ref[at * CY : (at + 1) * CY, :] = turned


def gelu(v):
    inner = 0.7978845608028654 * (v + 0.044715 * (v * v * v))
    return 0.5 * v * (1.0 + jnp.tanh(inner))


def store_shifted(target, start, block):
    rows = block.shape[0]
    for s, by in enumerate((1, 0, rows - 1)):
        moved = pltpu.roll(block, by, 0) if by else block
        target[s, start : start + rows, :] = moved.astype(BF)


def rows_of(source, pitch):
    return lambda s, x, count: source[s, x * pitch : (x + count) * pitch, :]


def conv(pick, band_ref, bias_ref, layer, x, count):
    pieces = [pick(s, x + q, count) for q in range(3) for s in range(3)]
    return dot(jnp.concatenate(pieces, 1), band_ref[layer], NT) + bias_ref[layer : layer + 1, :]


def hidden(pick, band_ref, bias_ref, layer, target, parts, pitch, base=0):
    for x, count in parts:
        value = gelu(conv(pick, band_ref, bias_ref, layer, x, count))
        store_shifted(target, (x - base) * pitch, value.astype(BF).astype(F32))


def build_decode(decoder):
    chans = decoder.shape[1]
    tiled = tiled_rows(decoder, Z)
    group = lax.broadcasted_iota(jnp.int32, (Z, Z * chans), 1) // chans
    level = lax.broadcasted_iota(jnp.int32, (Z, Z * chans), 0)
    return jnp.concatenate(
        [jnp.where(group == level, tiled[k : k + 1, :], 0.0) for k in range(3)], 0
    ).astype(BF)


def store_padded(target, x, value):
    side = jnp.zeros((SIDE, value.shape[1]), F32)
    for k in range(value.shape[0] // CY):
        block = jnp.concatenate([side, value[k * CY : (k + 1) * CY], side], 0)
        store_shifted(target, (x + k) * PITCH, block)


def core_kernel(
    mean_ref,
    weight_ref,
    encoder_ref,
    bias_ref,
    decoder_ref,
    middle_ref,
    own_ref,
    band_ref,
    spread_ref,
    decode_ref,
    input_one,
):
    spread = build_spread(encoder_ref[...])
    spread_ref[...] = spread
    decode_ref[...] = build_decode(decoder_ref[...])
    inside = dot(mean_ref[...], spread, NT).astype(BF)
    own_ref[...] = inside
    store_shifted(input_one, 0, inside.astype(F32))
    build_band(weight_ref, 0, band_ref)
    source = rows_of(input_one, CY)
    for x, count in CORE_PARTS:
        value = gelu(conv(source, band_ref, bias_ref, 0, x, count))
        store_padded(middle_ref, x, value.astype(BF).astype(F32))
    build_band(weight_ref, 1, band_ref)
    build_band(weight_ref, 2, band_ref)


def outer_kernel(
    own_ref, before_ref, after_ref, band_ref, spread_ref, bias_ref, outer_ref, input_one
):
    spread = spread_ref[...]
    near = (HALO - 1) * CY
    first = dot(before_ref[...], spread, NT).astype(BF).astype(F32)
    last = dot(after_ref[...], spread, NT).astype(BF).astype(F32)
    low = jnp.concatenate([first, own_ref[:near].astype(F32)], 0)
    high = jnp.concatenate([own_ref[CX * CY - near :].astype(F32), last], 0)
    store_shifted(input_one, 0, low)
    store_shifted(input_one, low.shape[0], high)
    source = rows_of(input_one, CY)
    for side in range(2):
        x = side * (2 * HALO - 1)
        value = gelu(conv(source, band_ref, bias_ref, 0, x, HALO))
        store_padded(outer_ref, side * HALO, value.astype(BF).astype(F32))


def pick_rows(table, feats, high, low, self_weight):
    count = feats.shape[1]
    both = dot(table, onehot(low, LO))
    half = both.shape[0] // 2
    values = both[:half] + both[half:]
    level = lax.broadcasted_iota(jnp.int32, (Z, count), 0).astype(F32)
    spread = jnp.broadcast_to(high, (Z, count))
    masks = [spread == (level + float(pair * Z)) for pair in range(CX // 2)]
    live = high < float(DEAD)
    wide = feats.astype(F32)
    rows = []
    for k in range(3):
        total = jnp.zeros((Z, count), F32)
        for pair in range(CX // 2):
            at = (pair * 3 + k) * Z
            total = total + jnp.where(masks[pair], values[at : at + Z], 0.0)
        for part in range(feats.shape[0] // Z):
            part_rows = slice(part * Z, (part + 1) * Z)
            total = total + wide[part_rows] * self_weight[part_rows, k : k + 1]
        rows.append(jnp.where(live, jnp.sum(total, 0, keepdims=True), 0.0))
    return rows


def pick_kernel(
    middle_ref,
    outer_ref,
    own_ref,
    below_ref,
    low_ref,
    high_ref,
    above_ref,
    band_ref,
    spread_ref,
    bias_ref,
    decode_ref,
    feat_in,
    slot_in,
    held_ref,
    self_ref,
    out_ref,
    strip_ref,
    ends_ref,
    input_three,
    table,
    feat_ref,
    slot_ref,
    sems,
):
    copies = [
        pltpu.make_async_copy(slot_in, slot_ref, sems.at[0]),
        pltpu.make_async_copy(feat_in, feat_ref, sems.at[1]),
    ]
    for copy in copies:
        copy.start()
    spread = spread_ref[...]
    sides = [
        dot(ref[...], spread, NT).astype(BF).astype(F32)
        for ref in (below_ref, low_ref, high_ref, above_ref)
    ]
    rows = CX + 2 * HALO
    strips = jnp.concatenate(
        [side[x * SIDE : (x + 1) * SIDE] for x in range(rows) for side in sides], 0
    )
    store_shifted(strip_ref, 0, strips)

    def end_rows(x, count):
        value = gelu(conv(rows_of(strip_ref, STRIP), band_ref, bias_ref, 0, x, count))
        store_shifted(ends_ref, x * STRIP, value.astype(BF).astype(F32))

    wide = own_ref.shape[1]
    half = STRIP // 2
    row = lax.broadcasted_iota(jnp.int32, (half, wide), 0)

    def mixed(s, x, count):
        blocks = []
        for at in range(x, x + count):
            if at < HALO:
                ref, base = outer_ref, at
            elif at < HALO + CX - 2:
                ref, base = middle_ref, at - HALO
            else:
                ref, base = outer_ref, at - (CX - 2)
            base = base * PITCH
            low = ends_ref[s, at * STRIP : at * STRIP + half, :]
            high = ends_ref[s, at * STRIP + half : (at + 1) * STRIP, :]
            blocks.append(jnp.where(row < half - KEPT, low, ref[s, base : base + half, :]))
            blocks.append(ref[s, base + half : base + PITCH - half, :])
            blocks.append(
                jnp.where(row >= KEPT, high, ref[s, base + PITCH - half : base + PITCH, :])
            )
        return jnp.concatenate(blocks, 0)

    def inner_rows(x, count):
        value = gelu(conv(mixed, band_ref, bias_ref, 1, x, count)).astype(BF).astype(F32)
        for k in range(count):
            block = value[k * PITCH : (k + 1) * PITCH]
            for s, by in enumerate((1, 0, PITCH - 1)):
                moved = pltpu.roll(block, by, 0) if by else block
                input_three[s, (x + k) * CY : (x + k + 1) * CY, :] = moved[
                    SIDE : SIDE + CY
                ].astype(BF)
    decode = decode_ref[...]
    source = rows_of(input_three, CY)
    size = decode.shape[0]

    def last_rows(x, count):
        own = own_ref[x * CY : (x + count) * CY, :].astype(F32)
        value = conv(source, band_ref, bias_ref, 2, x, count) + own
        flow = dot(decode, value.astype(BF), NT)
        top = flow.astype(BF)
        rest = (flow - top.astype(F32)).astype(BF)
        for k in range(count // 2):
            pair = x // 2 + k
            lanes = slice(k * LO, (k + 1) * LO)
            table[pair * size : (pair + 1) * size, :] = top[:, lanes]
            table[(CX // 2 + pair) * size : (CX // 2 + pair + 1) * size, :] = rest[:, lanes]

    steps = (end_rows, inner_rows, last_rows)
    for step, x, count in ORDER:
        steps[step](x, count)
    for copy in copies:
        copy.wait()
    chunk = CHUNK
    feat_dim, stay = feat_ref.shape
    eye = jnp.where(
        lax.broadcasted_iota(jnp.int32, (feat_dim, feat_dim), 0)
        == lax.broadcasted_iota(jnp.int32, (feat_dim, feat_dim), 1),
        1.0,
        0.0,
    ).astype(BF)
    weight = dot(eye, self_ref[...], NT)

    def staying(step):
        at = aligned(step * chunk, chunk)
        high, low = cell_codes(slot_ref[:, at])
        rows = pick_rows(
            table[...], feat_ref[:, at], high.astype(F32), low.astype(F32).astype(BF), weight
        )
        for k in range(3):
            out_ref[k, :, at] = rows[k]

    repeat(stay // chunk, staying)

    def arrived(step):
        at = aligned(step * chunk, chunk)
        block = held_ref[:, at]
        rows = pick_rows(
            table[...],
            block[:feat_dim],
            block[feat_dim : feat_dim + 1].astype(F32),
            block[feat_dim + 1 : feat_dim + 2],
            weight,
        )
        to = aligned(stay + step * chunk, chunk)
        for k in range(3):
            out_ref[k, :, to] = rows[k]

    repeat(held_ref.shape[1] // chunk, arrived)


def on_device(
    stay_feats,
    stay_slots,
    move_feats,
    move_slots,
    move_counts,
    encoder,
    conv_weights,
    conv_biases,
    decoder,
    self_weight,
):
    feat_dim = stay_feats.shape[0]
    stay = stay_feats.shape[3]
    cap = move_feats.shape[4]
    chans = encoder.shape[0]
    own_feats = stay_feats.reshape(feat_dim, stay)
    own_slots = stay_slots.reshape(1, stay)

    width = feat_dim + 2
    down, up, middle = call(
        pack_kernel,
        "pack",
        [hbm()] * 3,
        [
            (((3 * width * cap // 128, 128), BF), vmem()),
            (((3 * width * cap // 128, 128), BF), vmem()),
            (((2 * width * cap // 128, 128), BF), vmem()),
        ],
        [
            pltpu.VMEM((feat_dim, 8, cap), BF),
            pltpu.VMEM((8, cap), jnp.int32),
            pltpu.SMEM((8,), jnp.int32),
            pltpu.SemaphoreType.DMA((3,)),
        ],
        1 << 20,
        4,
    )(
        in_hbm(move_feats.reshape(feat_dim, 8, cap)),
        in_hbm(move_slots.reshape(8, cap)),
        in_hbm(move_counts.reshape(8)),
    )
    down = passed_along(down, "gy", -1)
    up = passed_along(up, "gy", 1)
    sums = (HI * (feat_dim + 1), LO)
    (part,) = call(
        stay_kernel,
        "stay",
        [hbm()] * 2,
        [((sums, F32), vmem())],
        [
            pltpu.VMEM((feat_dim, stay), BF),
            pltpu.VMEM((1, stay), jnp.int32),
            pltpu.SemaphoreType.DMA((2,)),
        ],
        5 << 30,
        8,
    )(in_hbm(own_feats), in_hbm(own_slots))
    down, up, part = lax.optimization_barrier((down, up, part))
    step = width * cap // 128

    def joined(place, inner):
        pieces = ((down, place), (middle, inner), (up, place))
        return jnp.concatenate([ref[k * step : (k + 1) * step] for ref, k in pieces], 0)

    west, east = exchanged(joined(2, 1), joined(0, 0), "gx")
    wide = Z * chans
    lanes = Z * feat_dim
    part, near = call(
        near_kernel,
        "near",
        [vmem()] * 3,
        [((sums, F32), vmem()), (((width, 2 * cap), BF), vmem())],
        [],
        1 << 30,
        8,
    )(down, up, part)
    mean, first, last, held = call(
        mean_kernel,
        "mean",
        [vmem()] * 4,
        [
            (((CX * CY, lanes), BF), vmem()),
            (((HALO * CY, lanes), BF), vmem()),
            (((HALO * CY, lanes), BF), vmem()),
            (((width, 8 * cap), BF), vmem()),
        ],
        [pltpu.VMEM(sums, F32)],
        3 << 30,
        8,
    )(near, west, east, part)
    after = passed_along(first, "gx", -1)
    before = passed_along(last, "gx", 1)

    def edge(start):
        blocks = [
            value.reshape(-1, CY, lanes)[:, start : start + SIDE] for value in (before, mean, after)
        ]
        return jnp.concatenate(blocks, 0).reshape((CX + 2 * HALO) * SIDE, lanes)

    low, high = edge(0), edge(CY - SIDE)
    above = passed_along(low, "gy", -1)
    below = passed_along(high, "gy", 1)
    biases = jnp.tile(conv_biases, (1, Z))
    rows = CX + 2 * HALO
    taken, own, band, spread, decode = call(
        core_kernel,
        "core",
        [vmem()] * 5,
        [
            (((3, (CX - 2) * PITCH, wide), BF), vmem()),
            (((CX * CY, wide), BF), vmem()),
            (((3, wide, 9 * wide), BF), vmem()),
            (((wide, lanes), BF), vmem()),
            (((3 * Z, wide), BF), vmem()),
        ],
        [pltpu.VMEM((3, CX * CY, wide), BF)],
        2 << 30,
        GRANT,
    )(mean, conv_weights, encoder, biases, decoder)
    (outer,) = call(
        outer_kernel,
        "outer",
        [vmem()] * 6,
        [(((3, 2 * HALO * PITCH, wide), BF), vmem())],
        [pltpu.VMEM((3, (4 * HALO - 2) * CY, wide), BF)],
        2 << 30,
        GRANT,
    )(own, before, after, band, spread, biases)
    (out,) = call(
        pick_kernel,
        "pick",
        [vmem()] * 11 + [hbm()] * 2 + [vmem()] * 2,
        [(((3, 1, stay + 8 * cap), F32), vmem())],
        [
            pltpu.VMEM((3, rows * STRIP, wide), BF),
            pltpu.VMEM((3, (rows - 2) * STRIP, wide), BF),
            pltpu.VMEM((3, (rows - 4) * CY, wide), BF),
            pltpu.VMEM((2 * CX // 2 * 3 * Z, LO), BF),
            pltpu.VMEM((feat_dim, stay), BF),
            pltpu.VMEM((1, stay), jnp.int32),
            pltpu.SemaphoreType.DMA((2,)),
        ],
        8 << 30,
        GRANT,
    )(
        taken,
        outer,
        own,
        below,
        low,
        high,
        above,
        band,
        spread,
        biases,
        decode,
        in_hbm(own_feats),
        in_hbm(own_slots),
        held,
        self_weight,
    )
    return out.reshape(3, 1, 1, stay + 8 * cap)


def solution(mesh):
    placed = (
        P(None, "gx", "gy", "groups"),
        P("gx", "gy", "groups"),
        P(None, "gx", "gy", None, "groups"),
        P("gx", "gy", None, "groups"),
        P("gx", "gy", "groups"),
        P(),
        P(),
        P(),
        P(),
        P(),
    )
    return jax.shard_map(
        on_device,
        mesh=mesh,
        in_specs=placed,
        out_specs=P(None, "gx", "gy", "groups"),
        check_vma=False,
    )
```

```python
import functools

import jax
import jax.numpy as jnp
from jax import lax
from jax.experimental import pallas as pl
from jax.experimental.pallas import tpu as pltpu
from jax.sharding import PartitionSpec as P

Z = 8
CX = 8
CY = 128
CELLS = Z * CX * CY
LO = 2 * CY
HI = CELLS // LO
DEAD = 2 * HI
HALO = 3
SIDE = 8
PITCH = CY + 2 * SIDE
KEPT = SIDE // 2
STRIP = 4 * SIDE
BF = jnp.bfloat16
F32 = jnp.float32
NT = (((1,), (1,)), ((), ()))
NN = (((1,), (0,)), ((), ()))


CHUNK = 1024
GRANT = 24
CORE_PARTS = ((0, 3), (3, 3))
ORDER = (
    (0, 0, 4),
    (0, 4, 4),
    (1, 0, 3),
    (0, 8, 4),
    (1, 3, 3),
    (2, 0, 2),
    (1, 6, 2),
    (2, 2, 2),
    (1, 8, 2),
    (2, 4, 2),
    (2, 6, 2),
)


def repeat(count, body):
    for step in range(count):
        body(step)


def aligned(start, length):
    return slice(start, start + length)


def cell_codes(slots):
    cell = slots & (CELLS - 1)
    low = cell & (LO - 1)
    zx = cell // LO
    return (zx & (CX // 2 - 1)) * Z + zx // (CX // 2), low


def passed_along(x, axis, by):
    length = lax.axis_size(axis)
    return lax.ppermute(x, axis, [(i, (i + by) % length) for i in range(length)])


def exchanged(up, down, axis):
    length = lax.axis_size(axis)
    if length % 2:
        return passed_along(down, axis, -1), passed_along(up, axis, 1)
    even = lax.axis_index(axis) % 2 == 0
    within = [(i, i + 1 - 2 * (i % 2)) for i in range(length)]
    between = [(i, (i - 1 + 2 * (i % 2)) % length) for i in range(length)]
    inner = lax.ppermute(jnp.where(even, up, down), axis, within)
    outer = lax.ppermute(jnp.where(even, down, up), axis, between)
    return jnp.where(even, inner, outer), jnp.where(even, outer, inner)


def dot(a, b, dims=NN):
    return lax.dot_general(a, b, dims, preferred_element_type=F32)


def vmem():
    return pl.BlockSpec(memory_space=pltpu.VMEM)


def hbm():
    return pl.BlockSpec(memory_space=pltpu.HBM)


def in_hbm(x):
    return pltpu.with_memory_space_constraint(x, pltpu.HBM)


def call(kernel, name, ins, outs, scratch, flops, mib):
    return pl.pallas_call(
        kernel,
        name=name,
        out_shape=[jax.ShapeDtypeStruct(*shape) for shape, _ in outs],
        in_specs=ins,
        out_specs=[spec for _, spec in outs],
        scratch_shapes=scratch,
        cost_estimate=pl.CostEstimate(flops=flops, bytes_accessed=1 << 20, transcendentals=0),
        compiler_params=pltpu.CompilerParams(vmem_limit_bytes=mib << 20),
    )


def onehot(code, count):
    rows = lax.broadcasted_iota(jnp.int32, (count, code.shape[1]), 0).astype(F32).astype(BF)
    same = rows == jnp.broadcast_to(code, rows.shape)
    return jnp.where(same, jnp.ones_like(rows), jnp.zeros_like(rows))


def scatter_part(feats, high, low):
    spread = jnp.broadcast_to(high, feats.shape)
    zero = jnp.zeros_like(feats)
    parts = [jnp.where(spread == jnp.asarray(h, BF), feats, zero) for h in range(HI)]
    parts.append(onehot(high, HI))
    return dot(jnp.concatenate(parts, 0), onehot(low, LO), NT)


def pack_kernel(
    feat_in, slot_in, count_in, down_ref, up_ref, middle_ref, feat_ref, slot_ref, count_ref, sems
):
    pairs = ((count_in, count_ref), (slot_in, slot_ref), (feat_in, feat_ref))
    copies = [pltpu.make_async_copy(a, b, sems.at[k]) for k, (a, b) in enumerate(pairs)]
    for copy in copies:
        copy.start()
    for copy in copies[:2]:
        copy.wait()
    feat_dim, buckets, cap = feat_ref.shape
    high, low = cell_codes(slot_ref[...])
    lane = lax.broadcasted_iota(jnp.int32, (1, cap), 1)
    high = high.astype(F32)
    low = low.astype(F32)
    blocks = cap // 128
    step = (feat_dim + 2) * blocks
    copies[2].wait()
    turned = jnp.swapaxes(feat_ref[...].astype(F32), 0, 1)
    for out_ref, chosen in ((down_ref, (0, 3, 5)), (up_ref, (2, 4, 7)), (middle_ref, (1, 6))):
        for place, bucket in enumerate(chosen):
            code = jnp.where(
                lane < count_ref[bucket], high[bucket : bucket + 1], jnp.full((1, cap), DEAD, F32)
            )
            base = place * step
            pieces = []
            for value in (turned[bucket], code, low[bucket : bucket + 1]):
                pieces += [value[:, k * 128 : (k + 1) * 128] for k in range(blocks)]
            out_ref[base : base + step, :] = jnp.concatenate(pieces, 0).astype(BF)


def stay_kernel(feat_in, slot_in, sum_ref, feat_ref, slot_ref, sems):
    copies = [
        pltpu.make_async_copy(slot_in, slot_ref, sems.at[0]),
        pltpu.make_async_copy(feat_in, feat_ref, sems.at[1]),
    ]
    for copy in copies:
        copy.start()
    for copy in copies:
        copy.wait()
    chunk = CHUNK
    for step in range(feat_ref.shape[1] // chunk):
        at = aligned(step * chunk, chunk)
        high, low = cell_codes(slot_ref[:, at])
        part = scatter_part(
            feat_ref[:, at], high.astype(F32).astype(BF), low.astype(F32).astype(BF)
        )
        sum_ref[...] = sum_ref[...] + part if step else part


def tiled_rows(small, count):
    width = small.shape[1]
    pick = lax.broadcasted_iota(jnp.int32, (width, count * width), 0)
    column = lax.broadcasted_iota(jnp.int32, (width, count * width), 1) % width
    return dot(small, jnp.where(pick == column, 1.0, 0.0).astype(BF))


def build_spread(encoder):
    chans, feat_dim = encoder.shape
    tiled = tiled_rows(encoder, Z)
    group = lax.broadcasted_iota(jnp.int32, tiled.shape, 1) // feat_dim
    return jnp.concatenate([jnp.where(group == layer, tiled, 0.0) for layer in range(Z)], 0).astype(
        BF
    )


def build_band(weight_ref, layer, band_ref):
    _, chans, width = weight_ref.shape
    taps = 9
    per = 128 // chans
    lane = lax.broadcasted_iota(jnp.int32, (chans, 128), 1) // chans
    weight = weight_ref[layer].astype(F32)
    turned = []
    for start in range(0, width, 128):
        source = weight[:, start : start + 128]
        if source.shape[1] < 128:
            source = jnp.concatenate([source, jnp.zeros((chans, 128 - source.shape[1]), F32)], 1)
        turned.append(
            [(source if k == 0 else pltpu.roll(source, k * chans, 1)).astype(BF) for k in range(per)]
        )
    for out_z in range(Z):
        for tap in range(taps):
            for part in range(Z // per):
                tile = jnp.zeros((chans, 128), BF)
                for depth in range(3):
                    in_z = out_z + depth - 1
                    if in_z < 0 or in_z >= Z or in_z // per != part:
                        continue
                    index = depth * taps + tap
                    moved = turned[index // per][(in_z - index) % per]
                    tile = jnp.where(lane == in_z % per, moved, tile)
                lanes = tap * Z * chans + part * 128
                band_ref[layer, out_z * chans : (out_z + 1) * chans, lanes : lanes + 128] = tile


def unpacked(ref, which, feat_dim, blocks):
    step = (feat_dim + 2) * blocks
    block = ref[which * step : (which + 1) * step, :].astype(F32)
    feats = jnp.concatenate([block[k * feat_dim : (k + 1) * feat_dim] for k in range(blocks)], 1)
    codes = block[blocks * feat_dim :]
    pair = [
        jnp.concatenate([codes[j * blocks + k][None] for k in range(blocks)], 1) for j in range(2)
    ]
    return feats.astype(BF), jnp.concatenate(pair, 0).astype(BF)


def near_kernel(down_ref, up_ref, part_ref, sum_ref, held_ref):
    cap = held_ref.shape[1] // 2
    feat_dim = held_ref.shape[0] - 2
    for place, ref in enumerate((down_ref, up_ref)):
        feats, codes = unpacked(ref, 1, feat_dim, cap // 128)
        at = slice(place * cap, (place + 1) * cap)
        held_ref[:feat_dim, at] = feats
        held_ref[feat_dim:, at] = codes
    rows = held_ref[...]
    sum_ref[...] = part_ref[...] + scatter_part(
        rows[:feat_dim], rows[feat_dim : feat_dim + 1], rows[feat_dim + 1 : feat_dim + 2]
    )


def mean_kernel(
    near_ref, west_ref, east_ref, part_ref, mean_ref, first_ref, last_ref, held_ref, total
):
    cap = held_ref.shape[1] // 8
    feat_dim = held_ref.shape[0] - 2
    held_ref[:, 3 * cap : 5 * cap] = near_ref[...]
    order = [(west_ref, k, k) for k in range(3)] + [(east_ref, k, 5 + k) for k in range(3)]
    for ref, which, place in order:
        feats, codes = unpacked(ref, which, feat_dim, cap // 128)
        at = slice(place * cap, (place + 1) * cap)
        held_ref[:feat_dim, at] = feats
        held_ref[feat_dim:, at] = codes
    for k, (place, count) in enumerate(((0, 2), (2, 1), (5, 1), (6, 2))):
        rows = held_ref[:, place * cap : (place + count) * cap]
        part = scatter_part(
            rows[:feat_dim], rows[feat_dim : feat_dim + 1], rows[feat_dim + 1 : feat_dim + 2]
        )
        total[...] = (total[...] if k else part_ref[...]) + part

    inverse = 1.0 / jnp.maximum(total[HI * feat_dim :, :], 1.0)
    for pair in range(CX // 2):
        blocks = []
        for layer in range(Z):
            code = pair * Z + layer
            blocks.append(
                total[code * feat_dim : (code + 1) * feat_dim, :] * inverse[code : code + 1, :]
            )
        block = jnp.concatenate(blocks, 0)
        for odd in range(2):
            x = pair * 2 + odd
            turned = jnp.transpose(block[:, odd * CY : (odd + 1) * CY]).astype(BF)
            mean_ref[x * CY : (x + 1) * CY, :] = turned
            if x < HALO:
                first_ref[x * CY : (x + 1) * CY, :] = turned
            if x >= CX - HALO:
                at = x - (CX - HALO)
                last_ref[at * CY : (at + 1) * CY, :] = turned


def gelu(v):
    inner = 0.7978845608028654 * (v + 0.044715 * (v * v * v))
    return 0.5 * v * (1.0 + jnp.tanh(inner))


def store_shifted(target, start, block):
    rows = block.shape[0]
    for s, by in enumerate((1, 0, rows - 1)):
        moved = pltpu.roll(block, by, 0) if by else block
        target[s, start : start + rows, :] = moved.astype(BF)


def rows_of(source, pitch):
    return lambda s, x, count: source[s, x * pitch : (x + count) * pitch, :]


def conv(pick, band_ref, bias_ref, layer, x, count):
    pieces = [pick(s, x + q, count) for q in range(3) for s in range(3)]
    return dot(jnp.concatenate(pieces, 1), band_ref[layer], NT) + bias_ref[layer : layer + 1, :]


def hidden(pick, band_ref, bias_ref, layer, target, parts, pitch, base=0):
    for x, count in parts:
        value = gelu(conv(pick, band_ref, bias_ref, layer, x, count))
        store_shifted(target, (x - base) * pitch, value.astype(BF).astype(F32))


def build_decode(decoder):
    chans = decoder.shape[1]
    tiled = tiled_rows(decoder, Z)
    group = lax.broadcasted_iota(jnp.int32, (Z, Z * chans), 1) // chans
    level = lax.broadcasted_iota(jnp.int32, (Z, Z * chans), 0)
    return jnp.concatenate(
        [jnp.where(group == level, tiled[k : k + 1, :], 0.0) for k in range(3)], 0
    ).astype(BF)


def store_padded(target, x, value):
    side = jnp.zeros((SIDE, value.shape[1]), F32)
    for k in range(value.shape[0] // CY):
        block = jnp.concatenate([side, value[k * CY : (k + 1) * CY], side], 0)
        store_shifted(target, (x + k) * PITCH, block)


def core_kernel(
    mean_ref,
    weight_ref,
    encoder_ref,
    bias_ref,
    decoder_ref,
    middle_ref,
    own_ref,
    band_ref,
    spread_ref,
    decode_ref,
    input_one,
):
    spread = build_spread(encoder_ref[...])
    spread_ref[...] = spread
    decode_ref[...] = build_decode(decoder_ref[...])
    inside = dot(mean_ref[...], spread, NT).astype(BF)
    own_ref[...] = inside
    store_shifted(input_one, 0, inside.astype(F32))
    build_band(weight_ref, 0, band_ref)
    source = rows_of(input_one, CY)
    for x, count in CORE_PARTS:
        value = gelu(conv(source, band_ref, bias_ref, 0, x, count))
        store_padded(middle_ref, x, value.astype(BF).astype(F32))
    build_band(weight_ref, 1, band_ref)
    build_band(weight_ref, 2, band_ref)


def outer_kernel(
    own_ref, before_ref, after_ref, band_ref, spread_ref, bias_ref, outer_ref, input_one
):
    spread = spread_ref[...]
    near = (HALO - 1) * CY
    first = dot(before_ref[...], spread, NT).astype(BF).astype(F32)
    last = dot(after_ref[...], spread, NT).astype(BF).astype(F32)
    low = jnp.concatenate([first, own_ref[:near].astype(F32)], 0)
    high = jnp.concatenate([own_ref[CX * CY - near :].astype(F32), last], 0)
    store_shifted(input_one, 0, low)
    store_shifted(input_one, low.shape[0], high)
    source = rows_of(input_one, CY)
    for side in range(2):
        x = side * (2 * HALO - 1)
        value = gelu(conv(source, band_ref, bias_ref, 0, x, HALO))
        store_padded(outer_ref, side * HALO, value.astype(BF).astype(F32))


def pick_rows(table, feats, high, low, self_weight):
    count = feats.shape[1]
    both = dot(table, onehot(low, LO))
    half = both.shape[0] // 2
    values = both[:half] + both[half:]
    level = lax.broadcasted_iota(jnp.int32, (Z, count), 0).astype(F32)
    spread = jnp.broadcast_to(high, (Z, count))
    masks = [spread == (level + float(pair * Z)) for pair in range(CX // 2)]
    live = high < float(DEAD)
    wide = feats.astype(F32)
    rows = []
    for k in range(3):
        total = jnp.zeros((Z, count), F32)
        for pair in range(CX // 2):
            at = (pair * 3 + k) * Z
            total = total + jnp.where(masks[pair], values[at : at + Z], 0.0)
        for part in range(feats.shape[0] // Z):
            part_rows = slice(part * Z, (part + 1) * Z)
            total = total + wide[part_rows] * self_weight[part_rows, k : k + 1]
        rows.append(jnp.where(live, jnp.sum(total, 0, keepdims=True), 0.0))
    return rows


def pick_kernel(
    middle_ref,
    outer_ref,
    own_ref,
    below_ref,
    low_ref,
    high_ref,
    above_ref,
    band_ref,
    spread_ref,
    bias_ref,
    decode_ref,
    feat_in,
    slot_in,
    held_ref,
    self_ref,
    out_ref,
    strip_ref,
    ends_ref,
    input_three,
    table,
    feat_ref,
    slot_ref,
    sems,
):
    copies = [
        pltpu.make_async_copy(slot_in, slot_ref, sems.at[0]),
        pltpu.make_async_copy(feat_in, feat_ref, sems.at[1]),
    ]
    for copy in copies:
        copy.start()
    spread = spread_ref[...]
    sides = [
        dot(ref[...], spread, NT).astype(BF).astype(F32)
        for ref in (below_ref, low_ref, high_ref, above_ref)
    ]
    rows = CX + 2 * HALO
    strips = jnp.concatenate(
        [side[x * SIDE : (x + 1) * SIDE] for x in range(rows) for side in sides], 0
    )
    store_shifted(strip_ref, 0, strips)

    def end_rows(x, count):
        value = gelu(conv(rows_of(strip_ref, STRIP), band_ref, bias_ref, 0, x, count))
        store_shifted(ends_ref, x * STRIP, value.astype(BF).astype(F32))

    wide = own_ref.shape[1]
    half = STRIP // 2
    row = lax.broadcasted_iota(jnp.int32, (half, wide), 0)

    def mixed(s, x, count):
        blocks = []
        for at in range(x, x + count):
            if at < HALO:
                ref, base = outer_ref, at
            elif at < HALO + CX - 2:
                ref, base = middle_ref, at - HALO
            else:
                ref, base = outer_ref, at - (CX - 2)
            base = base * PITCH
            low = ends_ref[s, at * STRIP : at * STRIP + half, :]
            high = ends_ref[s, at * STRIP + half : (at + 1) * STRIP, :]
            blocks.append(jnp.where(row < half - KEPT, low, ref[s, base : base + half, :]))
            blocks.append(ref[s, base + half : base + PITCH - half, :])
            blocks.append(
                jnp.where(row >= KEPT, high, ref[s, base + PITCH - half : base + PITCH, :])
            )
        return jnp.concatenate(blocks, 0)

    def inner_rows(x, count):
        value = gelu(conv(mixed, band_ref, bias_ref, 1, x, count)).astype(BF).astype(F32)
        for k in range(count):
            block = value[k * PITCH : (k + 1) * PITCH]
            for s, by in enumerate((1, 0, PITCH - 1)):
                moved = pltpu.roll(block, by, 0) if by else block
                input_three[s, (x + k) * CY : (x + k + 1) * CY, :] = moved[
                    SIDE : SIDE + CY
                ].astype(BF)
    decode = decode_ref[...]
    source = rows_of(input_three, CY)
    size = decode.shape[0]

    def last_rows(x, count):
        own = own_ref[x * CY : (x + count) * CY, :].astype(F32)
        value = conv(source, band_ref, bias_ref, 2, x, count) + own
        flow = dot(decode, value.astype(BF), NT)
        top = flow.astype(BF)
        rest = (flow - top.astype(F32)).astype(BF)
        for k in range(count // 2):
            pair = x // 2 + k
            lanes = slice(k * LO, (k + 1) * LO)
            table[pair * size : (pair + 1) * size, :] = top[:, lanes]
            table[(CX // 2 + pair) * size : (CX // 2 + pair + 1) * size, :] = rest[:, lanes]

    steps = (end_rows, inner_rows, last_rows)
    for step, x, count in ORDER:
        steps[step](x, count)
    for copy in copies:
        copy.wait()
    chunk = CHUNK
    feat_dim, stay = feat_ref.shape
    eye = jnp.where(
        lax.broadcasted_iota(jnp.int32, (feat_dim, feat_dim), 0)
        == lax.broadcasted_iota(jnp.int32, (feat_dim, feat_dim), 1),
        1.0,
        0.0,
    ).astype(BF)
    weight = dot(eye, self_ref[...], NT)

    def staying(step):
        at = aligned(step * chunk, chunk)
        high, low = cell_codes(slot_ref[:, at])
        rows = pick_rows(
            table[...], feat_ref[:, at], high.astype(F32), low.astype(F32).astype(BF), weight
        )
        for k in range(3):
            out_ref[k, :, at] = rows[k]

    repeat(stay // chunk, staying)

    def arrived(step):
        at = aligned(step * chunk, chunk)
        block = held_ref[:, at]
        rows = pick_rows(
            table[...],
            block[:feat_dim],
            block[feat_dim : feat_dim + 1].astype(F32),
            block[feat_dim + 1 : feat_dim + 2],
            weight,
        )
        to = aligned(stay + step * chunk, chunk)
        for k in range(3):
            out_ref[k, :, to] = rows[k]

    repeat(held_ref.shape[1] // chunk, arrived)


def on_device(
    stay_feats,
    stay_slots,
    move_feats,
    move_slots,
    move_counts,
    encoder,
    conv_weights,
    conv_biases,
    decoder,
    self_weight,
):
    feat_dim = stay_feats.shape[0]
    stay = stay_feats.shape[3]
    cap = move_feats.shape[4]
    chans = encoder.shape[0]
    own_feats = stay_feats.reshape(feat_dim, stay)
    own_slots = stay_slots.reshape(1, stay)

    width = feat_dim + 2
    down, up, middle = call(
        pack_kernel,
        "pack",
        [hbm()] * 3,
        [
            (((3 * width * cap // 128, 128), BF), vmem()),
            (((3 * width * cap // 128, 128), BF), vmem()),
            (((2 * width * cap // 128, 128), BF), vmem()),
        ],
        [
            pltpu.VMEM((feat_dim, 8, cap), BF),
            pltpu.VMEM((8, cap), jnp.int32),
            pltpu.SMEM((8,), jnp.int32),
            pltpu.SemaphoreType.DMA((3,)),
        ],
        1 << 20,
        4,
    )(
        in_hbm(move_feats.reshape(feat_dim, 8, cap)),
        in_hbm(move_slots.reshape(8, cap)),
        in_hbm(move_counts.reshape(8)),
    )
    down = passed_along(down, "gy", -1)
    up = passed_along(up, "gy", 1)
    sums = (HI * (feat_dim + 1), LO)
    (part,) = call(
        stay_kernel,
        "stay",
        [hbm()] * 2,
        [((sums, F32), vmem())],
        [
            pltpu.VMEM((feat_dim, stay), BF),
            pltpu.VMEM((1, stay), jnp.int32),
            pltpu.SemaphoreType.DMA((2,)),
        ],
        5 << 30,
        8,
    )(in_hbm(own_feats), in_hbm(own_slots))
    down, up, part = lax.optimization_barrier((down, up, part))
    step = width * cap // 128

    def joined(place, inner):
        pieces = ((down, place), (middle, inner), (up, place))
        return jnp.concatenate([ref[k * step : (k + 1) * step] for ref, k in pieces], 0)

    west, east = exchanged(joined(2, 1), joined(0, 0), "gx")
    wide = Z * chans
    lanes = Z * feat_dim
    part, near = call(
        near_kernel,
        "near",
        [vmem()] * 3,
        [((sums, F32), vmem()), (((width, 2 * cap), BF), vmem())],
        [],
        1 << 30,
        8,
    )(down, up, part)
    mean, first, last, held = call(
        mean_kernel,
        "mean",
        [vmem()] * 4,
        [
            (((CX * CY, lanes), BF), vmem()),
            (((HALO * CY, lanes), BF), vmem()),
            (((HALO * CY, lanes), BF), vmem()),
            (((width, 8 * cap), BF), vmem()),
        ],
        [pltpu.VMEM(sums, F32)],
        3 << 30,
        8,
    )(near, west, east, part)
    after = passed_along(first, "gx", -1)
    before = passed_along(last, "gx", 1)

    def edge(start):
        blocks = [
            value.reshape(-1, CY, lanes)[:, start : start + SIDE] for value in (before, mean, after)
        ]
        return jnp.concatenate(blocks, 0).reshape((CX + 2 * HALO) * SIDE, lanes)

    low, high = edge(0), edge(CY - SIDE)
    above = passed_along(low, "gy", -1)
    below = passed_along(high, "gy", 1)
    biases = jnp.tile(conv_biases, (1, Z))
    rows = CX + 2 * HALO
    taken, own, band, spread, decode = call(
        core_kernel,
        "core",
        [vmem()] * 5,
        [
            (((3, (CX - 2) * PITCH, wide), BF), vmem()),
            (((CX * CY, wide), BF), vmem()),
            (((3, wide, 9 * wide), BF), vmem()),
            (((wide, lanes), BF), vmem()),
            (((3 * Z, wide), BF), vmem()),
        ],
        [pltpu.VMEM((3, CX * CY, wide), BF)],
        2 << 30,
        GRANT,
    )(mean, conv_weights, encoder, biases, decoder)
    (outer,) = call(
        outer_kernel,
        "outer",
        [vmem()] * 6,
        [(((3, 2 * HALO * PITCH, wide), BF), vmem())],
        [pltpu.VMEM((3, (4 * HALO - 2) * CY, wide), BF)],
        2 << 30,
        GRANT,
    )(own, before, after, band, spread, biases)
    (out,) = call(
        pick_kernel,
        "pick",
        [vmem()] * 11 + [hbm()] * 2 + [vmem()] * 2,
        [(((3, 1, stay + 8 * cap), F32), vmem())],
        [
            pltpu.VMEM((3, rows * STRIP, wide), BF),
            pltpu.VMEM((3, (rows - 2) * STRIP, wide), BF),
            pltpu.VMEM((3, (rows - 4) * CY, wide), BF),
            pltpu.VMEM((2 * CX // 2 * 3 * Z, LO), BF),
            pltpu.VMEM((feat_dim, stay), BF),
            pltpu.VMEM((1, stay), jnp.int32),
            pltpu.SemaphoreType.DMA((2,)),
        ],
        8 << 30,
        GRANT,
    )(
        taken,
        outer,
        own,
        below,
        low,
        high,
        above,
        band,
        spread,
        biases,
        decode,
        in_hbm(own_feats),
        in_hbm(own_slots),
        held,
        self_weight,
    )
    return out.reshape(3, 1, 1, stay + 8 * cap)


def solution(mesh):
    placed = (
        P(None, "gx", "gy", "groups"),
        P("gx", "gy", "groups"),
        P(None, "gx", "gy", None, "groups"),
        P("gx", "gy", None, "groups"),
        P("gx", "gy", "groups"),
        P(),
        P(),
        P(),
        P(),
        P(),
    )
    return jax.shard_map(
        on_device,
        mesh=mesh,
        in_specs=placed,
        out_specs=P(None, "gx", "gy", "groups"),
        check_vma=False,
    )
```

```python
import functools

import jax
import jax.numpy as jnp
from jax import lax
from jax.experimental import pallas as pl
from jax.experimental.pallas import tpu as pltpu
from jax.sharding import PartitionSpec as P

Z = 8
CX = 8
CY = 128
CELLS = Z * CX * CY
LO = 2 * CY
HI = CELLS // LO
DEAD = 2 * HI
HALO = 3
SIDE = 8
PITCH = CY + 2 * SIDE
KEPT = SIDE // 2
STRIP = 4 * SIDE
BF = jnp.bfloat16
F32 = jnp.float32
NT = (((1,), (1,)), ((), ()))
NN = (((1,), (0,)), ((), ()))


CHUNK = 1024
GRANT = 24
CORE_PARTS = ((0, 2), (2, 2), (4, 2))
ORDER = (
    (0, 0, 4),
    (0, 4, 4),
    (1, 0, 3),
    (0, 8, 4),
    (1, 3, 3),
    (2, 0, 2),
    (1, 6, 2),
    (2, 2, 2),
    (1, 8, 2),
    (2, 4, 2),
    (2, 6, 2),
)


def repeat(count, body):
    for step in range(count):
        body(step)


def aligned(start, length):
    return slice(start, start + length)


def cell_codes(slots):
    cell = slots & (CELLS - 1)
    low = cell & (LO - 1)
    zx = cell // LO
    return (zx & (CX // 2 - 1)) * Z + zx // (CX // 2), low


def passed_along(x, axis, by):
    length = lax.axis_size(axis)
    return lax.ppermute(x, axis, [(i, (i + by) % length) for i in range(length)])


def exchanged(up, down, axis):
    length = lax.axis_size(axis)
    if length % 2:
        return passed_along(down, axis, -1), passed_along(up, axis, 1)
    even = lax.axis_index(axis) % 2 == 0
    within = [(i, i + 1 - 2 * (i % 2)) for i in range(length)]
    between = [(i, (i - 1 + 2 * (i % 2)) % length) for i in range(length)]
    inner = lax.ppermute(jnp.where(even, up, down), axis, within)
    outer = lax.ppermute(jnp.where(even, down, up), axis, between)
    return jnp.where(even, inner, outer), jnp.where(even, outer, inner)


def dot(a, b, dims=NN):
    return lax.dot_general(a, b, dims, preferred_element_type=F32)


def vmem():
    return pl.BlockSpec(memory_space=pltpu.VMEM)


def hbm():
    return pl.BlockSpec(memory_space=pltpu.HBM)


def in_hbm(x):
    return pltpu.with_memory_space_constraint(x, pltpu.HBM)


def call(kernel, name, ins, outs, scratch, flops, mib):
    return pl.pallas_call(
        kernel,
        name=name,
        out_shape=[jax.ShapeDtypeStruct(*shape) for shape, _ in outs],
        in_specs=ins,
        out_specs=[spec for _, spec in outs],
        scratch_shapes=scratch,
        cost_estimate=pl.CostEstimate(flops=flops, bytes_accessed=1 << 20, transcendentals=0),
        compiler_params=pltpu.CompilerParams(vmem_limit_bytes=mib << 20),
    )


def onehot(code, count):
    rows = lax.broadcasted_iota(jnp.int32, (count, code.shape[1]), 0).astype(F32).astype(BF)
    same = rows == jnp.broadcast_to(code, rows.shape)
    return jnp.where(same, jnp.ones_like(rows), jnp.zeros_like(rows))


def scatter_part(feats, high, low):
    spread = jnp.broadcast_to(high, feats.shape)
    zero = jnp.zeros_like(feats)
    parts = [jnp.where(spread == jnp.asarray(h, BF), feats, zero) for h in range(HI)]
    parts.append(onehot(high, HI))
    return dot(jnp.concatenate(parts, 0), onehot(low, LO), NT)


def pack_kernel(
    feat_in, slot_in, count_in, down_ref, up_ref, middle_ref, feat_ref, slot_ref, count_ref, sems
):
    pairs = ((count_in, count_ref), (slot_in, slot_ref), (feat_in, feat_ref))
    copies = [pltpu.make_async_copy(a, b, sems.at[k]) for k, (a, b) in enumerate(pairs)]
    for copy in copies:
        copy.start()
    for copy in copies:
        copy.wait()
    feat_dim, buckets, cap = feat_ref.shape
    turned = jnp.swapaxes(feat_ref[...].astype(F32), 0, 1)
    high, low = cell_codes(slot_ref[...])
    lane = lax.broadcasted_iota(jnp.int32, (1, cap), 1)
    high = high.astype(F32)
    low = low.astype(F32)
    blocks = cap // 128
    step = (feat_dim + 2) * blocks
    for out_ref, chosen in ((down_ref, (0, 3, 5)), (up_ref, (2, 4, 7)), (middle_ref, (1, 6))):
        for place, bucket in enumerate(chosen):
            code = jnp.where(
                lane < count_ref[bucket], high[bucket : bucket + 1], jnp.full((1, cap), DEAD, F32)
            )
            base = place * step
            pieces = []
            for value in (turned[bucket], code, low[bucket : bucket + 1]):
                pieces += [value[:, k * 128 : (k + 1) * 128] for k in range(blocks)]
            out_ref[base : base + step, :] = jnp.concatenate(pieces, 0).astype(BF)


def stay_kernel(feat_in, slot_in, sum_ref, feat_ref, slot_ref, sems):
    copies = [
        pltpu.make_async_copy(slot_in, slot_ref, sems.at[0]),
        pltpu.make_async_copy(feat_in, feat_ref, sems.at[1]),
    ]
    for copy in copies:
        copy.start()
    for copy in copies:
        copy.wait()
    chunk = CHUNK
    for step in range(feat_ref.shape[1] // chunk):
        at = aligned(step * chunk, chunk)
        high, low = cell_codes(slot_ref[:, at])
        part = scatter_part(
            feat_ref[:, at], high.astype(F32).astype(BF), low.astype(F32).astype(BF)
        )
        sum_ref[...] = sum_ref[...] + part if step else part


def tiled_rows(small, count):
    width = small.shape[1]
    pick = lax.broadcasted_iota(jnp.int32, (width, count * width), 0)
    column = lax.broadcasted_iota(jnp.int32, (width, count * width), 1) % width
    return dot(small, jnp.where(pick == column, 1.0, 0.0).astype(BF))


def build_spread(encoder):
    chans, feat_dim = encoder.shape
    tiled = tiled_rows(encoder, Z)
    group = lax.broadcasted_iota(jnp.int32, tiled.shape, 1) // feat_dim
    return jnp.concatenate([jnp.where(group == layer, tiled, 0.0) for layer in range(Z)], 0).astype(
        BF
    )


def build_band(weight_ref, layer, band_ref):
    _, chans, width = weight_ref.shape
    taps = 9
    per = 128 // chans
    lane = lax.broadcasted_iota(jnp.int32, (chans, 128), 1) // chans
    weight = weight_ref[layer].astype(F32)
    turned = []
    for start in range(0, width, 128):
        source = weight[:, start : start + 128]
        if source.shape[1] < 128:
            source = jnp.concatenate([source, jnp.zeros((chans, 128 - source.shape[1]), F32)], 1)
        turned.append(
            [(source if k == 0 else pltpu.roll(source, k * chans, 1)).astype(BF) for k in range(per)]
        )
    for out_z in range(Z):
        for tap in range(taps):
            for part in range(Z // per):
                tile = jnp.zeros((chans, 128), BF)
                for depth in range(3):
                    in_z = out_z + depth - 1
                    if in_z < 0 or in_z >= Z or in_z // per != part:
                        continue
                    index = depth * taps + tap
                    moved = turned[index // per][(in_z - index) % per]
                    tile = jnp.where(lane == in_z % per, moved, tile)
                lanes = tap * Z * chans + part * 128
                band_ref[layer, out_z * chans : (out_z + 1) * chans, lanes : lanes + 128] = tile


def unpacked(ref, which, feat_dim, blocks):
    step = (feat_dim + 2) * blocks
    block = ref[which * step : (which + 1) * step, :].astype(F32)
    feats = jnp.concatenate([block[k * feat_dim : (k + 1) * feat_dim] for k in range(blocks)], 1)
    codes = block[blocks * feat_dim :]
    pair = [
        jnp.concatenate([codes[j * blocks + k][None] for k in range(blocks)], 1) for j in range(2)
    ]
    return feats.astype(BF), jnp.concatenate(pair, 0).astype(BF)


def near_kernel(down_ref, up_ref, part_ref, sum_ref, held_ref):
    cap = held_ref.shape[1] // 2
    feat_dim = held_ref.shape[0] - 2
    for place, ref in enumerate((down_ref, up_ref)):
        feats, codes = unpacked(ref, 1, feat_dim, cap // 128)
        at = slice(place * cap, (place + 1) * cap)
        held_ref[:feat_dim, at] = feats
        held_ref[feat_dim:, at] = codes
    rows = held_ref[...]
    sum_ref[...] = part_ref[...] + scatter_part(
        rows[:feat_dim], rows[feat_dim : feat_dim + 1], rows[feat_dim + 1 : feat_dim + 2]
    )


def mean_kernel(
    near_ref, west_ref, east_ref, part_ref, mean_ref, first_ref, last_ref, held_ref, total
):
    cap = held_ref.shape[1] // 8
    feat_dim = held_ref.shape[0] - 2
    held_ref[:, 3 * cap : 5 * cap] = near_ref[...]
    order = [(west_ref, k, k) for k in range(3)] + [(east_ref, k, 5 + k) for k in range(3)]
    for ref, which, place in order:
        feats, codes = unpacked(ref, which, feat_dim, cap // 128)
        at = slice(place * cap, (place + 1) * cap)
        held_ref[:feat_dim, at] = feats
        held_ref[feat_dim:, at] = codes
    for k, (place, count) in enumerate(((0, 2), (2, 1), (5, 1), (6, 2))):
        rows = held_ref[:, place * cap : (place + count) * cap]
        part = scatter_part(
            rows[:feat_dim], rows[feat_dim : feat_dim + 1], rows[feat_dim + 1 : feat_dim + 2]
        )
        total[...] = (total[...] if k else part_ref[...]) + part

    inverse = 1.0 / jnp.maximum(total[HI * feat_dim :, :], 1.0)
    for pair in range(CX // 2):
        blocks = []
        for layer in range(Z):
            code = pair * Z + layer
            blocks.append(
                total[code * feat_dim : (code + 1) * feat_dim, :] * inverse[code : code + 1, :]
            )
        block = jnp.concatenate(blocks, 0)
        for odd in range(2):
            x = pair * 2 + odd
            turned = jnp.transpose(block[:, odd * CY : (odd + 1) * CY]).astype(BF)
            mean_ref[x * CY : (x + 1) * CY, :] = turned
            if x < HALO:
                first_ref[x * CY : (x + 1) * CY, :] = turned
            if x >= CX - HALO:
                at = x - (CX - HALO)
                last_ref[at * CY : (at + 1) * CY, :] = turned


def gelu(v):
    inner = 0.7978845608028654 * (v + 0.044715 * (v * v * v))
    return 0.5 * v * (1.0 + jnp.tanh(inner))


def store_shifted(target, start, block):
    rows = block.shape[0]
    for s, by in enumerate((1, 0, rows - 1)):
        moved = pltpu.roll(block, by, 0) if by else block
        target[s, start : start + rows, :] = moved.astype(BF)


def rows_of(source, pitch):
    return lambda s, x, count: source[s, x * pitch : (x + count) * pitch, :]


def conv(pick, band_ref, bias_ref, layer, x, count):
    pieces = [pick(s, x + q, count) for q in range(3) for s in range(3)]
    return dot(jnp.concatenate(pieces, 1), band_ref[layer], NT) + bias_ref[layer : layer + 1, :]


def hidden(pick, band_ref, bias_ref, layer, target, parts, pitch, base=0):
    for x, count in parts:
        value = gelu(conv(pick, band_ref, bias_ref, layer, x, count))
        store_shifted(target, (x - base) * pitch, value.astype(BF).astype(F32))


def build_decode(decoder):
    chans = decoder.shape[1]
    tiled = tiled_rows(decoder, Z)
    group = lax.broadcasted_iota(jnp.int32, (Z, Z * chans), 1) // chans
    level = lax.broadcasted_iota(jnp.int32, (Z, Z * chans), 0)
    return jnp.concatenate(
        [jnp.where(group == level, tiled[k : k + 1, :], 0.0) for k in range(3)], 0
    ).astype(BF)


def store_padded(target, x, value):
    side = jnp.zeros((SIDE, value.shape[1]), F32)
    for k in range(value.shape[0] // CY):
        block = jnp.concatenate([side, value[k * CY : (k + 1) * CY], side], 0)
        store_shifted(target, (x + k) * PITCH, block)


def core_kernel(
    mean_ref,
    weight_ref,
    encoder_ref,
    bias_ref,
    decoder_ref,
    middle_ref,
    own_ref,
    band_ref,
    spread_ref,
    decode_ref,
    input_one,
):
    spread = build_spread(encoder_ref[...])
    spread_ref[...] = spread
    decode_ref[...] = build_decode(decoder_ref[...])
    inside = dot(mean_ref[...], spread, NT).astype(BF)
    own_ref[...] = inside
    store_shifted(input_one, 0, inside.astype(F32))
    build_band(weight_ref, 0, band_ref)
    source = rows_of(input_one, CY)
    for x, count in CORE_PARTS:
        value = gelu(conv(source, band_ref, bias_ref, 0, x, count))
        store_padded(middle_ref, x, value.astype(BF).astype(F32))
    build_band(weight_ref, 1, band_ref)
    build_band(weight_ref, 2, band_ref)


def outer_kernel(
    own_ref, before_ref, after_ref, band_ref, spread_ref, bias_ref, outer_ref, input_one
):
    spread = spread_ref[...]
    near = (HALO - 1) * CY
    first = dot(before_ref[...], spread, NT).astype(BF).astype(F32)
    last = dot(after_ref[...], spread, NT).astype(BF).astype(F32)
    low = jnp.concatenate([first, own_ref[:near].astype(F32)], 0)
    high = jnp.concatenate([own_ref[CX * CY - near :].astype(F32), last], 0)
    store_shifted(input_one, 0, low)
    store_shifted(input_one, low.shape[0], high)
    source = rows_of(input_one, CY)
    for side in range(2):
        x = side * (2 * HALO - 1)
        value = gelu(conv(source, band_ref, bias_ref, 0, x, HALO))
        store_padded(outer_ref, side * HALO, value.astype(BF).astype(F32))


def pick_rows(table, feats, high, low, self_weight):
    count = feats.shape[1]
    both = dot(table, onehot(low, LO))
    half = both.shape[0] // 2
    values = both[:half] + both[half:]
    level = lax.broadcasted_iota(jnp.int32, (Z, count), 0).astype(F32)
    spread = jnp.broadcast_to(high, (Z, count))
    masks = [spread == (level + float(pair * Z)) for pair in range(CX // 2)]
    live = high < float(DEAD)
    wide = feats.astype(F32)
    rows = []
    for k in range(3):
        total = jnp.zeros((Z, count), F32)
        for pair in range(CX // 2):
            at = (pair * 3 + k) * Z
            total = total + jnp.where(masks[pair], values[at : at + Z], 0.0)
        for part in range(feats.shape[0] // Z):
            part_rows = slice(part * Z, (part + 1) * Z)
            total = total + wide[part_rows] * self_weight[part_rows, k : k + 1]
        rows.append(jnp.where(live, jnp.sum(total, 0, keepdims=True), 0.0))
    return rows


def pick_kernel(
    middle_ref,
    outer_ref,
    own_ref,
    below_ref,
    low_ref,
    high_ref,
    above_ref,
    band_ref,
    spread_ref,
    bias_ref,
    decode_ref,
    feat_in,
    slot_in,
    held_ref,
    self_ref,
    out_ref,
    strip_ref,
    ends_ref,
    input_three,
    table,
    feat_ref,
    slot_ref,
    sems,
):
    copies = [
        pltpu.make_async_copy(slot_in, slot_ref, sems.at[0]),
        pltpu.make_async_copy(feat_in, feat_ref, sems.at[1]),
    ]
    for copy in copies:
        copy.start()
    spread = spread_ref[...]
    sides = [
        dot(ref[...], spread, NT).astype(BF).astype(F32)
        for ref in (below_ref, low_ref, high_ref, above_ref)
    ]
    rows = CX + 2 * HALO
    strips = jnp.concatenate(
        [side[x * SIDE : (x + 1) * SIDE] for x in range(rows) for side in sides], 0
    )
    store_shifted(strip_ref, 0, strips)

    def end_rows(x, count):
        value = gelu(conv(rows_of(strip_ref, STRIP), band_ref, bias_ref, 0, x, count))
        store_shifted(ends_ref, x * STRIP, value.astype(BF).astype(F32))

    wide = own_ref.shape[1]
    half = STRIP // 2
    row = lax.broadcasted_iota(jnp.int32, (half, wide), 0)

    def mixed(s, x, count):
        blocks = []
        for at in range(x, x + count):
            if at < HALO:
                ref, base = outer_ref, at
            elif at < HALO + CX - 2:
                ref, base = middle_ref, at - HALO
            else:
                ref, base = outer_ref, at - (CX - 2)
            base = base * PITCH
            low = ends_ref[s, at * STRIP : at * STRIP + half, :]
            high = ends_ref[s, at * STRIP + half : (at + 1) * STRIP, :]
            blocks.append(jnp.where(row < half - KEPT, low, ref[s, base : base + half, :]))
            blocks.append(ref[s, base + half : base + PITCH - half, :])
            blocks.append(
                jnp.where(row >= KEPT, high, ref[s, base + PITCH - half : base + PITCH, :])
            )
        return jnp.concatenate(blocks, 0)

    def inner_rows(x, count):
        value = gelu(conv(mixed, band_ref, bias_ref, 1, x, count)).astype(BF).astype(F32)
        for k in range(count):
            block = value[k * PITCH : (k + 1) * PITCH]
            for s, by in enumerate((1, 0, PITCH - 1)):
                moved = pltpu.roll(block, by, 0) if by else block
                input_three[s, (x + k) * CY : (x + k + 1) * CY, :] = moved[
                    SIDE : SIDE + CY
                ].astype(BF)
    decode = decode_ref[...]
    source = rows_of(input_three, CY)
    size = decode.shape[0]

    def last_rows(x, count):
        own = own_ref[x * CY : (x + count) * CY, :].astype(F32)
        value = conv(source, band_ref, bias_ref, 2, x, count) + own
        flow = dot(decode, value.astype(BF), NT)
        top = flow.astype(BF)
        rest = (flow - top.astype(F32)).astype(BF)
        for k in range(count // 2):
            pair = x // 2 + k
            lanes = slice(k * LO, (k + 1) * LO)
            table[pair * size : (pair + 1) * size, :] = top[:, lanes]
            table[(CX // 2 + pair) * size : (CX // 2 + pair + 1) * size, :] = rest[:, lanes]

    steps = (end_rows, inner_rows, last_rows)
    for step, x, count in ORDER:
        steps[step](x, count)
    for copy in copies:
        copy.wait()
    chunk = CHUNK
    feat_dim, stay = feat_ref.shape
    eye = jnp.where(
        lax.broadcasted_iota(jnp.int32, (feat_dim, feat_dim), 0)
        == lax.broadcasted_iota(jnp.int32, (feat_dim, feat_dim), 1),
        1.0,
        0.0,
    ).astype(BF)
    weight = dot(eye, self_ref[...], NT)

    def staying(step):
        at = aligned(step * chunk, chunk)
        high, low = cell_codes(slot_ref[:, at])
        rows = pick_rows(
            table[...], feat_ref[:, at], high.astype(F32), low.astype(F32).astype(BF), weight
        )
        for k in range(3):
            out_ref[k, :, at] = rows[k]

    repeat(stay // chunk, staying)

    def arrived(step):
        at = aligned(step * chunk, chunk)
        block = held_ref[:, at]
        rows = pick_rows(
            table[...],
            block[:feat_dim],
            block[feat_dim : feat_dim + 1].astype(F32),
            block[feat_dim + 1 : feat_dim + 2],
            weight,
        )
        to = aligned(stay + step * chunk, chunk)
        for k in range(3):
            out_ref[k, :, to] = rows[k]

    repeat(held_ref.shape[1] // chunk, arrived)


def on_device(
    stay_feats,
    stay_slots,
    move_feats,
    move_slots,
    move_counts,
    encoder,
    conv_weights,
    conv_biases,
    decoder,
    self_weight,
):
    feat_dim = stay_feats.shape[0]
    stay = stay_feats.shape[3]
    cap = move_feats.shape[4]
    chans = encoder.shape[0]
    own_feats = stay_feats.reshape(feat_dim, stay)
    own_slots = stay_slots.reshape(1, stay)

    width = feat_dim + 2
    down, up, middle = call(
        pack_kernel,
        "pack",
        [hbm()] * 3,
        [
            (((3 * width * cap // 128, 128), BF), vmem()),
            (((3 * width * cap // 128, 128), BF), vmem()),
            (((2 * width * cap // 128, 128), BF), vmem()),
        ],
        [
            pltpu.VMEM((feat_dim, 8, cap), BF),
            pltpu.VMEM((8, cap), jnp.int32),
            pltpu.SMEM((8,), jnp.int32),
            pltpu.SemaphoreType.DMA((3,)),
        ],
        1 << 20,
        4,
    )(
        in_hbm(move_feats.reshape(feat_dim, 8, cap)),
        in_hbm(move_slots.reshape(8, cap)),
        in_hbm(move_counts.reshape(8)),
    )
    down = passed_along(down, "gy", -1)
    up = passed_along(up, "gy", 1)
    sums = (HI * (feat_dim + 1), LO)
    (part,) = call(
        stay_kernel,
        "stay",
        [hbm()] * 2,
        [((sums, F32), vmem())],
        [
            pltpu.VMEM((feat_dim, stay), BF),
            pltpu.VMEM((1, stay), jnp.int32),
            pltpu.SemaphoreType.DMA((2,)),
        ],
        5 << 30,
        8,
    )(in_hbm(own_feats), in_hbm(own_slots))
    down, up, part = lax.optimization_barrier((down, up, part))
    step = width * cap // 128

    def joined(place, inner):
        pieces = ((down, place), (middle, inner), (up, place))
        return jnp.concatenate([ref[k * step : (k + 1) * step] for ref, k in pieces], 0)

    west, east = exchanged(joined(2, 1), joined(0, 0), "gx")
    wide = Z * chans
    lanes = Z * feat_dim
    part, near = call(
        near_kernel,
        "near",
        [vmem()] * 3,
        [((sums, F32), vmem()), (((width, 2 * cap), BF), vmem())],
        [],
        1 << 30,
        8,
    )(down, up, part)
    mean, first, last, held = call(
        mean_kernel,
        "mean",
        [vmem()] * 4,
        [
            (((CX * CY, lanes), BF), vmem()),
            (((HALO * CY, lanes), BF), vmem()),
            (((HALO * CY, lanes), BF), vmem()),
            (((width, 8 * cap), BF), vmem()),
        ],
        [pltpu.VMEM(sums, F32)],
        3 << 30,
        8,
    )(near, west, east, part)
    after = passed_along(first, "gx", -1)
    before = passed_along(last, "gx", 1)

    def edge(start):
        blocks = [
            value.reshape(-1, CY, lanes)[:, start : start + SIDE] for value in (before, mean, after)
        ]
        return jnp.concatenate(blocks, 0).reshape((CX + 2 * HALO) * SIDE, lanes)

    low, high = edge(0), edge(CY - SIDE)
    above = passed_along(low, "gy", -1)
    below = passed_along(high, "gy", 1)
    biases = jnp.tile(conv_biases, (1, Z))
    rows = CX + 2 * HALO
    taken, own, band, spread, decode = call(
        core_kernel,
        "core",
        [vmem()] * 5,
        [
            (((3, (CX - 2) * PITCH, wide), BF), vmem()),
            (((CX * CY, wide), BF), vmem()),
            (((3, wide, 9 * wide), BF), vmem()),
            (((wide, lanes), BF), vmem()),
            (((3 * Z, wide), BF), vmem()),
        ],
        [pltpu.VMEM((3, CX * CY, wide), BF)],
        2 << 30,
        GRANT,
    )(mean, conv_weights, encoder, biases, decoder)
    (outer,) = call(
        outer_kernel,
        "outer",
        [vmem()] * 6,
        [(((3, 2 * HALO * PITCH, wide), BF), vmem())],
        [pltpu.VMEM((3, (4 * HALO - 2) * CY, wide), BF)],
        2 << 30,
        GRANT,
    )(own, before, after, band, spread, biases)
    (out,) = call(
        pick_kernel,
        "pick",
        [vmem()] * 11 + [hbm()] * 2 + [vmem()] * 2,
        [(((3, 1, stay + 8 * cap), F32), vmem())],
        [
            pltpu.VMEM((3, rows * STRIP, wide), BF),
            pltpu.VMEM((3, (rows - 2) * STRIP, wide), BF),
            pltpu.VMEM((3, (rows - 4) * CY, wide), BF),
            pltpu.VMEM((2 * CX // 2 * 3 * Z, LO), BF),
            pltpu.VMEM((feat_dim, stay), BF),
            pltpu.VMEM((1, stay), jnp.int32),
            pltpu.SemaphoreType.DMA((2,)),
        ],
        8 << 30,
        GRANT,
    )(
        taken,
        outer,
        own,
        below,
        low,
        high,
        above,
        band,
        spread,
        biases,
        decode,
        in_hbm(own_feats),
        in_hbm(own_slots),
        held,
        self_weight,
    )
    return out.reshape(3, 1, 1, stay + 8 * cap)


def solution(mesh):
    placed = (
        P(None, "gx", "gy", "groups"),
        P("gx", "gy", "groups"),
        P(None, "gx", "gy", None, "groups"),
        P("gx", "gy", None, "groups"),
        P("gx", "gy", "groups"),
        P(),
        P(),
        P(),
        P(),
        P(),
    )
    return jax.shard_map(
        on_device,
        mesh=mesh,
        in_specs=placed,
        out_specs=P(None, "gx", "gy", "groups"),
        check_vma=False,
    )
```
